32 devices in a mesh: member: 2 (over y), lon: 8 (over z, x), lat: 2 (over core).
Axes of the slice: x: 2, y: 2, z: 4, core: 2. Of those that a mesh axis runs over, the one named last changes fastest.
Arguments:
- fields: bfloat16 [1280, 32, 128], P('member', 'lat', 'lon'), parts along dimension 0, may hold values from -6 to 6
- support_rows: int32 [7, 32, 16], replicated, may hold values from -1 to 1
- support_lons: int32 [7, 32, 16], replicated, may hold values from -64 to 64, as said below
- support_weights: float32 [7, 32, 16], replicated, may hold values from -1.5 to 1.5
- mix_weight: bfloat16 [7, 640, 640], replicated, may hold values from -0.09375 to 0.09375
- norm_gain: float32 [640], replicated, may hold values from 0.1 to 1.9
- up_weight: bfloat16 [640, 1280], replicated, may hold values from -0.25 to 0.25
- down_weight: bfloat16 [1280, 640], replicated, may hold values from -0.15625 to 0.15625
Outputs:
- output: bfloat16 [1280, 32, 128], P('member', 'lat', 'lon'), parts along dimension 0
The draws below stay inside these ranges and needn't reach their ends.
There are 2 independent parts, one for each index of `member`. The reference program is written for one: setup_inputs(seed, part) draws one part's arguments, and reference() takes and returns one part's arrays. A program takes and returns all parts, laid end to end along the dimension named above; an argument that names none is the same for every part. Nothing has to cross between parts.
Inputs may be any that keep to these rules, and one draw needn't show every extreme that they name: `support_lons`: at output row i every offset lies within plus or minus min(64, 4 * 32 // min(i + 1, 32 - i)); in every basis filter the first pole row has an entry at -(64) and the last pole row one at 64.
All inputs are finite; a program needn't handle non-finite values.
Results may differ from the reference program's by a relative error of at most 0.0095.
Values may be sent and summed in bfloat16 or wider, within the bound.
A program may use at most 128 MiB of HBM per device.

```python
import math
import jax
import jax.numpy as jnp
from jax import lax

C = 640
HID = 1280
K = 7
S = 16
NLAT = 32
NLON = 128


def draw_support_rows(key, part):
    return jax.random.randint(key, (K, NLAT, S), -1, 2, dtype=jnp.int32)


def draw_support_lons(key, part):
    row_index = lax.broadcasted_iota(jnp.int32, (K, NLAT, S), 1)
    slot_index = lax.broadcasted_iota(jnp.int32, (K, NLAT, S), 2)
    nearest = jnp.minimum(row_index + 1, NLAT - row_index)
    half_reach = jnp.minimum(NLON // 2, 4 * NLAT // nearest)
    random_bits = jax.random.randint(key, (K, NLAT, S), 0, 2 ** 30, dtype=jnp.int32)
    offset = jnp.mod(random_bits, 2 * half_reach + 1) - half_reach
    offset = jnp.where((row_index == 0) & (slot_index == 0), -(NLON // 2), offset)
    offset = jnp.where((row_index == NLAT - 1) & (slot_index == 0), NLON // 2, offset)
    return offset.astype(jnp.int32)


def block_levels(rng, extent, shards, smallest, largest):
    loudness, own = 1.0, jax.random.fold_in(rng, 6)
    for dim, shards_of in shards:
        heights = jnp.exp(jax.random.uniform(jax.random.fold_in(own, dim), (shards_of,), jnp.float32, smallest / len(shards), largest / len(shards)))
        loudness = loudness * jnp.repeat(heights, extent[dim] // shards_of).reshape([-1 if axis == dim else 1 for axis in range(len(extent))])
    return loudness


def bell_draw(key, shape, width, reach, split=(), kind=jnp.bfloat16):
    drawn = jax.random.normal(key, shape, jnp.float32) * width
    if len(split) > 0:
        drawn = block_levels(key, shape, split, -0.22, 0.18) * drawn
    return jnp.clip(drawn, min=-reach, max=reach).astype(kind)


def setup_inputs(seed: int = 0, part: int = 0) -> dict:
    seeds = jax.random.split(jax.random.key(seed), 9)
    part_keys = jax.random.split(jax.random.fold_in(seeds[8], part), 9)
    return {
        "fields": bell_draw(part_keys[0], (C, NLAT, NLON), 1.0, 6.0, ((1, 2), (2, 8))),
        "support_rows": draw_support_rows(jax.random.fold_in(seeds[8], 71), part),
        "support_lons": draw_support_lons(jax.random.fold_in(seeds[8], 71), part),
        "support_weights": bell_draw(seeds[3], (K, NLAT, S), 0.25, 1.5, (), jnp.float32),
        "mix_weight": bell_draw(seeds[4], (K, C, C), (K * C) ** -0.5, 0.09375),
        "norm_gain": jnp.clip(1.0 + 0.18 * jax.random.normal(seeds[5], (C,), jnp.float32), 0.1, 1.9),
        "up_weight": bell_draw(seeds[6], (C, HID), C ** -0.5, 0.25),
        "down_weight": bell_draw(seeds[7], (HID, C), HID ** -0.5, 0.15625),
    }


full_turn = 2.0 * math.pi
norm_eps = 1e-05

def round_half(values):
    return lax.optimization_barrier(values.astype(jnp.bfloat16)).astype(jnp.float32)

def reference(fields, support_rows, support_lons, support_weights, mix_weight, norm_gain, up_weight, down_weight):
    lon_total = NLON
    lon_half = lon_total // 2
    frequency = jnp.arange(lon_half + 1, dtype=jnp.int32)
    spectrum = jnp.fft.rfft(fields.astype(jnp.float32), axis=2)
    cos_part = jnp.pad(round_half(jnp.real(spectrum).astype(jnp.float32)), ((0, 0), (1, 1), (0, 0)))
    sin_part = jnp.pad(round_half((-jnp.imag(spectrum)).astype(jnp.float32)), ((0, 0), (1, 1), (0, 0)))

    def basis_term(running, basis_index):
        row_offsets = support_rows[basis_index]
        lon_offsets = support_lons[basis_index]
        weights = support_weights[basis_index]
        turns = jnp.mod(lon_offsets[:, :, None] * frequency[None, None, :], lon_total).astype(jnp.int32)
        phase_angle = turns.astype(jnp.float32) * (full_turn / lon_total)
        cos_table = jnp.cos(phase_angle)
        sin_table = jnp.sin(phase_angle)
        spec_cos = jnp.zeros((C, NLAT, lon_half + 1), jnp.float32)
        spec_sin = jnp.zeros((C, NLAT, lon_half + 1), jnp.float32)
        for offset in (-1, 0, 1):
            picked = jnp.where(row_offsets == offset, weights, jnp.zeros_like(weights))
            filter_cos = jnp.einsum('is,isf->if', picked, cos_table, precision=lax.Precision.HIGHEST)
            filter_sin = jnp.einsum('is,isf->if', picked, sin_table, precision=lax.Precision.HIGHEST)
            field_cos = cos_part[:, 1 + offset:1 + offset + NLAT]
            field_sin = sin_part[:, 1 + offset:1 + offset + NLAT]
            spec_cos = spec_cos + field_cos * filter_cos + field_sin * filter_sin
            spec_sin = spec_sin + field_sin * filter_cos - field_cos * filter_sin
        weight_k = mix_weight[basis_index]
        run_cos = running[0] + lax.dot_general(weight_k, spec_cos.astype(jnp.bfloat16).reshape(C, -1), (((0,), (0,)), ((), ())), preferred_element_type=jnp.float32)
        run_sin = running[1] + lax.dot_general(weight_k, spec_sin.astype(jnp.bfloat16).reshape(C, -1), (((0,), (0,)), ((), ())), preferred_element_type=jnp.float32)
        return ((run_cos, run_sin), None)
    start = jnp.zeros((C, NLAT * (lon_half + 1)), jnp.float32)
    mixed_parts, _ = lax.scan(basis_term, (start, start), jnp.arange(K, dtype=jnp.int32))
    mixed_cos = mixed_parts[0].reshape(C, NLAT, lon_half + 1)
    mixed_sin = mixed_parts[1].reshape(C, NLAT, lon_half + 1)
    mixed = jnp.fft.irfft(lax.complex(mixed_cos, -mixed_sin), n=lon_total, axis=2).astype(jnp.float32)
    latent = fields.reshape(C, NLAT * NLON).astype(jnp.float32) + mixed.reshape(C, NLAT * NLON)
    row_mean = lax.optimization_barrier(jnp.mean(latent, axis=0))
    variance = lax.optimization_barrier(jnp.mean(jnp.square(latent - row_mean), axis=0))
    normed = ((latent - row_mean) * lax.rsqrt(variance + norm_eps) * norm_gain[:, None]).astype(jnp.bfloat16)
    hidden = jax.nn.gelu(lax.dot_general(up_weight, normed, (((0,), (0,)), ((), ())), preferred_element_type=jnp.float32), approximate=False).astype(jnp.bfloat16)
    output = latent + lax.dot_general(down_weight, hidden, (((0,), (0,)), ((), ())), preferred_element_type=jnp.float32)
    return output.astype(jnp.bfloat16).reshape(C, NLAT, NLON)
```

```python
import functools
import math

import jax
import jax.numpy as jnp
from jax import lax
from jax.experimental import pallas as pl
from jax.experimental.pallas import tpu as pltpu
from jax.sharding import PartitionSpec as P

norm_eps = 1e-05
MESH = pl.DeviceIdType.MESH


def plan_copies(lon_count, lat_count, rows, cols):
    lon_total, row_total = lon_count * cols, lat_count * rows

    def reach(row):
        nearest = min(row + 1, row_total - row)
        return min(lon_total // 2, 4 * row_total // nearest)

    def distance(row):
        return min(-(-reach(row) // cols), lon_count // 2)

    def in_half(span, delta):
        if delta == 0 or abs(delta) == lon_count // 2:
            return False
        return span - cols * (abs(delta) - 1) <= cols // 2

    need = [distance(max(p - 1, 0)) for p in range(rows)]
    deltas = [d for d in range(1 - lon_count // 2, lon_count // 2 + 1) if d != 0]
    counts = {delta: sum(1 for d in need if d >= abs(delta)) for delta in deltas}
    spans = [reach(max(p - 1, 0)) for p in range(rows)]
    fulls = {d: sum(1 for p in range(counts[d]) if not in_half(spans[p], d)) for d in deltas}
    edge, edge_span = 0, 0
    for boundary in range(1, lat_count):
        edge = max(edge, distance(boundary * rows - 1), distance(boundary * rows))
        edge_span = max(edge_span, reach(boundary * rows - 1), reach(boundary * rows))
    halo = [d for d in range(1 - lon_count // 2, lon_count // 2 + 1) if abs(d) <= edge]
    groups = [(rows // 2, rows), (rows // 4, rows // 2), (0, rows // 4)]
    stages = []
    upper = rows
    for low, _ in groups:
        lower = max(low - 1, 0)
        stage = []
        for delta in sorted(deltas, key=lambda d: -abs(d)):
            full, top = min(fulls[delta], upper), min(counts[delta], upper)
            if full > lower:
                stage.append(("block", delta, lower, full, False))
            if top > max(full, lower):
                stage.append(("block", delta, max(full, lower), top, True))
        stages.append(stage)
        upper = lower
    if lat_count > 1:
        stages[0] = [
            (side, d, 0, 1, in_half(edge_span, d)) for d in halo for side in ("down", "up")
        ] + stages[0]
    halves = [d for d in halo if in_half(edge_span, d)]
    return groups, stages, counts, fulls, halo, halves


def block_kernel(
    lon_count,
    lat_count,
    plan,
    x_hbm,
    rows_ref,
    lons_ref,
    weights_ref,
    gain_ref,
    mix_hbm,
    up_hbm,
    down_hbm,
    out_hbm,
    x_ref,
    out_ref,
    window,
    filters,
    product,
    mix_ref,
    up_ref,
    down_ref,
    send_sem,
    recv_sem,
    load_sem,
    out_sem,
):
    rows, cols, channels = x_ref.shape
    bases, entries = rows_ref.shape[:2]
    lon_total = lon_count * cols
    middle = lon_count // 2
    groups, stages, counts, fulls, halo, halves = plan
    me, lat = lax.axis_index("lon"), lax.axis_index("lat")
    north = 2 * lat < lat_count
    has_low, has_high = lat > 0, lat < lat_count - 1

    loads = [
        pltpu.make_async_copy(mix_hbm, mix_ref, load_sem.at[0]),
        pltpu.make_async_copy(up_hbm, up_ref, load_sem.at[1]),
        pltpu.make_async_copy(down_hbm, down_ref, load_sem.at[2]),
    ]
    fetch = pltpu.make_async_copy(x_hbm, x_ref, load_sem.at[3])
    fetch.start()

    barrier = pltpu.get_barrier_semaphore()
    halo_deltas = halo if lat_count > 1 else []
    for delta in range(1, lon_count):
        pl.semaphore_signal(
            barrier, inc=1, device_id={"lon": lax.rem(me + delta, lon_count)}, device_id_type=MESH
        )
    for present, other in ((has_low, lat - 1), (has_high, lat + 1)):

        @pl.when(present)
        def _():
            for delta in halo_deltas:
                target = lax.rem(me + lon_count - delta, lon_count)
                pl.semaphore_signal(
                    barrier, inc=1, device_id={"lon": target, "lat": other}, device_id_type=MESH
                )

    sides = jnp.where(has_low, 1, 0) + jnp.where(has_high, 1, 0)
    pl.semaphore_wait(barrier, lon_count - 1 + sides * len(halo_deltas))
    fetch.wait()

    def copy_of(index, item):
        kind, delta, first, last, halved = item
        width = cols // 2 if halved else cols
        offset = cols // 2 if halved and delta < 0 else 0
        target = lax.rem(me + lon_count - delta, lon_count)
        slot = (delta + middle) % lon_count
        here, there = pl.ds(offset, width), pl.ds(slot * cols + offset, width)
        if kind == "block":
            start = jnp.where(north, first, rows - last)
            source = x_ref.at[pl.ds(start, last - first), here]
            landing = window.at[pl.ds(start + 1, last - first), there]
            device = {"lon": target}
        elif kind == "down":
            source = x_ref.at[pl.ds(rows - 1, 1), here]
            landing = window.at[pl.ds(0, 1), there]
            device = {"lon": target, "lat": jnp.minimum(lat + 1, lat_count - 1)}
        else:
            source = x_ref.at[pl.ds(0, 1), here]
            landing = window.at[pl.ds(rows + 1, 1), there]
            device = {"lon": target, "lat": jnp.maximum(lat - 1, 0)}
        return pltpu.make_async_remote_copy(
            src_ref=source,
            dst_ref=landing,
            send_sem=send_sem.at[index],
            recv_sem=recv_sem.at[index],
            device_id=device,
            device_id_type=MESH,
        )

    copies = []
    for stage in stages:
        copies.append(list(enumerate(stage, sum(len(done) for done in copies))))

    def each(items, sending, action):
        for index, item in items:
            if item[0] == "block":
                action(copy_of(index, item))
            else:
                present = has_high if (item[0] == "down") == sending else has_low

                @pl.when(present)
                def _():
                    action(copy_of(index, item))

    for stage in copies:
        each(stage, True, lambda copy: copy.start())
    for load in loads:
        load.start()

    window[1 : rows + 1, middle * cols : (middle + 1) * cols, :] = x_ref[...]
    for delta, count in counts.items():
        slot = (delta + middle) % lon_count
        if count < rows:
            gap = (rows - count, cols, channels)
            window[pl.ds(jnp.where(north, count, 0) + 1, rows - count),
                   slot * cols : (slot + 1) * cols] = jnp.zeros(gap, jnp.bfloat16)
        partial = count - fulls[delta]
        if partial > 0:
            far = slot * cols + (0 if delta < 0 else cols // 2)
            window[pl.ds(jnp.where(north, fulls[delta], rows - count) + 1, partial),
                   far : far + cols // 2] = jnp.zeros(
                (partial, cols // 2, channels), jnp.bfloat16
            )
    for delta in halves:
        far = (delta + middle) % lon_count * cols + (0 if delta < 0 else cols // 2)
        for line in (0, rows + 1):
            window[line, far : far + cols // 2] = jnp.zeros((cols // 2, channels), jnp.bfloat16)
    for present, line in ((has_low, 0), (has_high, rows + 1)):
        for delta in range(1 - middle, middle + 1):
            slot = (delta + middle) % lon_count

            def clear():
                window[line, slot * cols : (slot + 1) * cols] = jnp.zeros(
                    (cols, channels), jnp.bfloat16
                )

            if delta in halo and lat_count > 1:
                pl.when(jnp.logical_not(present))(clear)
            else:
                clear()

    lanes = lax.broadcasted_iota(jnp.int32, (rows, lon_total), 1)
    wide = (rows, rows_ref.shape[2])
    own_rows = (
        lax.broadcasted_iota(jnp.int32, wide, 0) + lat * rows
        == lax.broadcasted_iota(jnp.int32, wide, 1)
    ).astype(jnp.float32)

    def own(ref, k):
        return lax.dot_general(
            own_rows,
            ref[k].astype(jnp.float32),
            (((1,), (1,)), ((), ())),
            precision=lax.Precision.HIGHEST,
            preferred_element_type=jnp.float32,
        )

    def build(k, carry):
        spot = own(lons_ref, k).astype(jnp.int32) + middle * cols
        spot = jnp.where(spot >= lon_total, spot - lon_total, spot)
        row_offset = own(rows_ref, k)
        weight = own(weights_ref, k)
        picked = [jnp.where(row_offset == r, weight, 0.0) for r in (-1.0, 0.0, 1.0)]
        sums = [jnp.zeros((rows, lon_total), jnp.float32) for _ in range(3)]
        for s in range(entries):
            hit = spot[:, s : s + 1] == lanes
            for r in range(3):
                sums[r] = sums[r] + jnp.where(hit, picked[r][:, s : s + 1], 0.0)
        for r in range(3):
            for i in range(rows):
                line = jnp.broadcast_to(sums[r][i : i + 1, :], (cols, lon_total))
                turned = pltpu.roll(line, 0, 1, stride=1, stride_axis=0)
                filters[i, pl.ds(pl.multiple_of(k * cols, cols), cols),
                        r * lon_total : (r + 1) * lon_total] = turned.astype(jnp.bfloat16)
        return carry

    lax.fori_loop(0, bases, build, 0)

    def group(low, high):
        start = jnp.where(north, low, rows - high)
        half = high - low
        lines = half * cols
        def filter_row(t, carry):
            i = start + t
            source = window[pl.ds(i, 3)].reshape(3 * lon_total, channels)
            filtered = jnp.dot(filters[i], source, preferred_element_type=jnp.float32)
            filtered = filtered.astype(jnp.bfloat16)
            at = pl.multiple_of(t * cols, cols)
            for k in range(bases):
                product[pl.ds(at, cols), k * channels : (k + 1) * channels] = filtered[
                    k * cols : (k + 1) * cols
                ]
            return carry

        lax.fori_loop(0, half, filter_row, 0)
        mixed = jnp.dot(product[:lines], mix_ref[...], preferred_element_type=jnp.float32)
        here = x_ref[pl.ds(start, half)].reshape(lines, channels)
        latent = here.astype(jnp.float32) + mixed
        mean = jnp.mean(latent, axis=1, keepdims=True)
        centred = latent - mean
        variance = jnp.mean(centred * centred, axis=1, keepdims=True)
        normed = (centred * lax.rsqrt(variance + norm_eps) * gain_ref[...][None, :]).astype(jnp.bfloat16)
        raised = jnp.dot(normed, up_ref[...], preferred_element_type=jnp.float32)
        hidden = 0.5 * raised * (1.0 + lax.erf(raised * math.sqrt(0.5)))
        lowered = jnp.dot(
            hidden.astype(jnp.bfloat16), down_ref[...], preferred_element_type=jnp.float32
        )
        result = (latent + lowered).astype(jnp.bfloat16)
        out_ref[pl.ds(start, half)] = result.reshape(half, cols, channels)

    puts = []
    for stage, (low, high) in zip(copies, groups):
        each(stage, False, lambda copy: copy.wait_recv())
        if stage is copies[0]:
            for load in loads:
                load.wait()
        group(low, high)
        part = pl.ds(jnp.where(north, low, rows - high), high - low)
        put = pltpu.make_async_copy(out_ref.at[part], out_hbm.at[part], out_sem.at[len(puts)])
        put.start()
        puts.append(put)
    for stage in copies:
        each(stage, True, lambda copy: copy.wait_send())
    for put in puts:
        put.wait()


def source_reach(lon_total, row_total, p):
    row = max(p - 1, 0)
    return min(lon_total // 2, 4 * row_total // min(row + 1, row_total - row))


def relay_fits(lon_count, lat_count, rows, cols):
    lon_total, row_total = lon_count * cols, lat_count * rows
    if lon_count != 8 or lat_count != 2 or rows % 8 != 0 or cols % 16 != 0:
        return False
    return source_reach(lon_total, row_total, rows // 2 + 1) <= cols and lon_total == 128


def relay_kernel(
    lon_count,
    lat_count,
    x_hbm,
    rows_ref,
    lons_ref,
    weights_ref,
    gain_ref,
    mix_hbm,
    up_hbm,
    down_hbm,
    out_ref,
    window,
    wide_filters,
    near_filters,
    product,
    mix_ref,
    up_ref,
    down_ref,
    send_sem,
    recv_sem,
    load_sem,
):
    rows, cols, channels = x_hbm.shape
    bases, entries = rows_ref.shape[:2]
    lon_total, row_total = lon_count * cols, lat_count * rows
    middle, part, half = lon_count // 2, cols // 2, rows // 2
    home = middle * cols
    reaches = [source_reach(lon_total, row_total, p) for p in range(rows)]
    full = sum(1 for r in reaches if r > 2 * cols)
    wide = sum(1 for r in reaches if r > cols + part)
    near = sum(1 for r in reaches if r > cols)
    me, lat = lax.axis_index("lon"), lax.axis_index("lat")
    north = lat == 0
    turn = 1 - 2 * lax.rem(me, 2)
    edge = jnp.where(north, rows - 1, 0)

    def device(delta):
        return lax.rem(me + delta + lon_count, lon_count)

    def at(delta):
        return pl.multiple_of(lax.rem(delta + middle + lon_count, lon_count) * cols, cols)

    def lines(first, last):
        return pl.ds(jnp.where(north, first, rows - last) + 1, last - first)

    fetch = pltpu.make_async_copy(
        x_hbm, window.at[pl.ds(1, rows), pl.ds(home, cols)], load_sem.at[3]
    )
    fetch.start()
    loads = [
        pltpu.make_async_copy(mix_hbm, mix_ref, load_sem.at[0]),
        pltpu.make_async_copy(up_hbm, up_ref, load_sem.at[1]),
        pltpu.make_async_copy(down_hbm, down_ref, load_sem.at[2]),
    ]
    barrier = pltpu.get_barrier_semaphore()
    others = [{"lon": me + turn}] + [{"lon": device(2 * e)} for e in (1, -1, 2)]
    others.append({"lat": 1 - lat})
    for other in others:
        pl.semaphore_signal(barrier, inc=1, device_id=other, device_id_type=MESH)
    for load in loads:
        load.start()

    def clear(where, low, high):
        size = where.size if isinstance(where, pl.Slice) else 1
        window[where, low:high] = jnp.zeros((size, high - low, channels), jnp.bfloat16)

    outer, halo = jnp.where(north, 0, rows + 1), jnp.where(north, rows + 1, 0)
    clear(pl.ds(outer, 1), 0, lon_total)
    clear(lines(full, wide), 0, home - 2 * cols)
    clear(lines(full, wide), home + 3 * cols, lon_total)
    clear(lines(wide, near), 0, home - cols - part)
    clear(lines(wide, near), home + 2 * cols + part, lon_total)
    clear(lines(near, half + 1), 0, home - cols)
    clear(lines(near, half + 1), home + 2 * cols, lon_total)
    clear(lines(half + 1, rows), home + 2 * cols, home + 3 * cols)
    clear(pl.ds(halo, 1), home - cols, home - part)
    clear(pl.ds(halo, 1), home + cols + part, home + 3 * cols)

    count = [0]

    def message(where, here, there, width, target, landing=None):
        index = count[0]
        count[0] += 1
        landing = where if landing is None else landing
        return pltpu.make_async_remote_copy(
            src_ref=window.at[where, pl.ds(here, width)],
            dst_ref=window.at[landing, pl.ds(there, width)],
            send_sem=send_sem.at[index],
            recv_sem=recv_sem.at[index],
            device_id=target,
            device_id_type=MESH,
        )

    partner, beside = {"lon": me + turn}, {"lon": device(2 * turn)}
    core, core_line = {"lat": 1 - lat}, pl.ds(edge + 1, 1)
    core_landing = pl.ds(jnp.where(north, 0, rows + 1), 1)

    def own_across(first, last):
        return message(lines(first, last), home, at(-turn), cols, partner)

    def own_along(first, last, e):
        return message(lines(first, last), home, at(-2 * e), cols, {"lon": device(2 * e)})

    def half_along(first, last, e):
        offset = part if e > 0 else 0
        return message(
            lines(first, last), home + offset, at(-2 * e) + offset, part, {"lon": device(2 * e)}
        )

    def pass_along(first, last):
        return message(lines(first, last), at(turn), at(-turn), cols, beside)

    def pass_across(first, last, e):
        return message(lines(first, last), at(2 * e), at(2 * e - turn), cols, partner)

    def to_core(col, width):
        return message(core_line, col, col, width, core, core_landing)

    after = pl.multiple_of(home + jnp.where(turn > 0, cols, -part), part)
    before = pl.multiple_of(home + jnp.where(turn > 0, -part, cols), part)
    near_cut = half + (rows - half) // 2
    steps = (1, -1, 2)
    halo_own = to_core(home, cols)
    halo_across, halo_along = to_core(after, part), to_core(before, part)
    across = [own_across(near_cut, rows), own_across(half, near_cut), own_across(wide, half)]
    across_wide = own_across(0, wide)
    along = [pass_along(near_cut, rows), pass_along(half, near_cut), pass_along(wide, half)]
    halves = [half_along(wide, near, e) for e in (1, -1)]
    wide_along = {e: own_along(full, wide, e) for e in (1, -1)}
    wide_across = message(lines(full, wide), at(2 * turn), at(turn), cols, partner)
    bands = [(full - 1, full), (1, full - 1), (0, 1)]
    full_along = [[own_along(a, b, e) for e in steps] for a, b in bands]
    full_across = [[pass_across(a, b, e) for e in steps] for a, b in bands]

    def start(*copies):
        for copy in copies:
            copy.start()

    def arrived(*copies):
        for copy in copies:
            copy.wait_recv()

    wide_rows = (half, rows_ref.shape[2])

    def table(ref, k, first):
        order = lax.broadcasted_iota(jnp.int32, wide_rows, 0) + first
        local = jnp.where(north, order, rows - 2 - order + 2 * lax.rem(order, 2))
        mine = (local + lat * rows == lax.broadcasted_iota(jnp.int32, wide_rows, 1)).astype(
            jnp.float32
        )
        return lax.dot_general(
            mine,
            ref[k].astype(jnp.float32),
            (((1,), (1,)), ((), ())),
            precision=lax.Precision.HIGHEST,
            preferred_element_type=jnp.float32,
        )

    lanes = lax.broadcasted_iota(jnp.int32, (half, lon_total), 1)
    second = lax.rem(lax.broadcasted_iota(jnp.int32, (half, entries), 0), 2)

    def turned(line):
        spread = jnp.broadcast_to(line, (cols, lon_total))
        return pltpu.roll(spread, 0, 1, stride=1, stride_axis=0).astype(jnp.bfloat16)

    def build_near(k, carry):
        offset = table(lons_ref, k, half).astype(jnp.int32)
        row_offset = table(rows_ref, k, half).astype(jnp.int32)
        weight = table(weights_ref, k, half)
        spot = (row_offset + 1 + second) * (4 * cols) + offset + cols
        sums = [jnp.zeros((half, lon_total), jnp.float32) for _ in range(2)]
        for s in range(entries):
            for v in range(2):
                hit = spot[:, s : s + 1] == lanes + v * lon_total
                sums[v] = sums[v] + jnp.where(hit, weight[:, s : s + 1], 0.0)
        for n in range(half):
            for v in range(2):
                spot_at = pl.multiple_of(k * 2 * cols + (n % 2) * cols, cols)
                near_filters[n // 2, pl.ds(spot_at, cols), v * lon_total : (v + 1) * lon_total] = (
                    turned(sums[v][n : n + 1, :])
                )
        return carry

    def build_wide(k, carry):
        spot = table(lons_ref, k, 0).astype(jnp.int32) + home
        spot = jnp.where(spot >= lon_total, spot - lon_total, spot)
        row_offset = table(rows_ref, k, 0)
        weight = table(weights_ref, k, 0)
        picked = [jnp.where(row_offset == r, weight, 0.0) for r in (-1.0, 0.0, 1.0)]
        sums = [jnp.zeros((half, lon_total), jnp.float32) for _ in range(3)]
        for s in range(entries):
            hit = spot[:, s : s + 1] == lanes
            for r in range(3):
                sums[r] = sums[r] + jnp.where(hit, picked[r][:, s : s + 1], 0.0)
        for n in range(half):
            late = n % 2
            spot_at = pl.ds(pl.multiple_of(k * 2 * cols + late * cols, cols), cols)
            for r in range(3):
                low = (r + late) * lon_total
                wide_filters[n // 2, spot_at, low : low + lon_total] = turned(sums[r][n : n + 1, :])
            low = (3 - 3 * late) * lon_total
            wide_filters[n // 2, spot_at, low : low + lon_total] = jnp.zeros(
                (cols, lon_total), jnp.bfloat16
            )
        return carry

    def filter_pairs(first, last):
        pairs = last - first
        base = jnp.where(north, 2 * first, rows - 2 * last)
        for t in range(pairs):
            q = jnp.where(north, first + t, last - 1 - t)
            taken = pl.ds(base + 2 * t, 4)
            if 2 * first >= half:
                low = home - cols
                source = window[taken, low : low + 4 * cols].reshape(16 * cols, channels)
                matrix = near_filters[q - half // 2]
            else:
                source = window[taken].reshape(4 * lon_total, channels)
                matrix = wide_filters[q]
            filtered = jnp.dot(matrix, source, preferred_element_type=jnp.float32)
            filtered = filtered.astype(jnp.bfloat16)
            for k in range(bases):
                product[2 * t * cols : 2 * (t + 1) * cols, k * channels : (k + 1) * channels] = (
                    filtered[2 * k * cols : 2 * (k + 1) * cols]
                )

    def finish_pairs(first, last, between=()):
        base = jnp.where(north, 2 * first, rows - 2 * last)
        depth = 2 * (last - first)
        cells = depth * cols
        mixed = jnp.dot(product[:cells], mix_ref[...], preferred_element_type=jnp.float32)
        here = window[pl.ds(base + 1, depth), home : home + cols].reshape(cells, channels)
        latent = here.astype(jnp.float32) + mixed
        mean = jnp.mean(latent, axis=1, keepdims=True)
        centred = latent - mean
        variance = jnp.mean(centred * centred, axis=1, keepdims=True)
        normed = (centred * lax.rsqrt(variance + norm_eps) * gain_ref[...][None, :]).astype(
            jnp.bfloat16
        )
        raised = jnp.dot(normed, up_ref[...], preferred_element_type=jnp.float32)
        hidden = 0.5 * raised * (1.0 + lax.erf(raised * math.sqrt(0.5)))
        lowered = jnp.dot(
            hidden.astype(jnp.bfloat16), down_ref[...], preferred_element_type=jnp.float32
        )
        result = (latent + lowered).astype(jnp.bfloat16)
        out_ref[pl.ds(base, depth)] = result.reshape(depth, cols, channels)

    pl.semaphore_wait(barrier, len(others))
    fetch.wait()
    start(halo_own, *across, across_wide)
    start(*wide_along.values(), *full_along[0])
    lax.fori_loop(0, bases, build_near, 0)
    arrived(across[0])
    start(along[0], halo_across)
    start(*full_along[1])
    lax.fori_loop(0, bases, build_wide, 0)
    arrived(across[1])
    start(along[1])
    arrived(*wide_along.values())
    start(wide_across)
    arrived(*full_along[0])
    start(*full_across[0])
    start(*full_along[2])
    arrived(across[2])
    start(along[2], *halves)
    arrived(along[0])
    start(halo_along)
    for load in loads:
        load.wait()
    quarter = half // 4
    arrived(halo_own, halo_across, halo_along)
    arrived(*full_along[1])
    start(*full_across[1])
    arrived(along[1])
    filter_pairs(3 * quarter, 4 * quarter)
    finish_pairs(3 * quarter, 4 * quarter)
    arrived(*full_along[2])
    start(*full_across[2])
    arrived(along[2], *halves)
    filter_pairs(2 * quarter, 3 * quarter)
    finish_pairs(2 * quarter, 3 * quarter)
    arrived(across_wide, wide_across, *full_across[0])
    filter_pairs(quarter, 2 * quarter)
    finish_pairs(quarter, 2 * quarter)
    arrived(*full_across[1], *full_across[2])
    filter_pairs(0, quarter)
    finish_pairs(0, quarter)
    sent = [halo_own, halo_across, halo_along, across_wide, wide_across]
    sent += across + along + halves + list(wide_along.values())
    for group in full_along + full_across:
        sent += group
    for copy in sent:
        copy.wait_send()


def relay_call(
    lon_count,
    lat_count,
    fields,
    support_rows,
    support_lons,
    support_weights,
    mix_weight,
    norm_gain,
    up_weight,
    down_weight,
):
    channels, rows, cols = fields.shape
    bases, hidden = mix_weight.shape[0], up_weight.shape[1]
    lon_total = lon_count * cols
    half, copies = rows // 2, 36
    in_vmem = pl.BlockSpec(memory_space=pltpu.VMEM)
    anywhere = pl.BlockSpec(memory_space=pl.ANY)
    result = pl.pallas_call(
        functools.partial(relay_kernel, lon_count, lat_count),
        out_shape=pltpu.VMEM((rows, cols, channels), jnp.bfloat16),
        in_specs=[anywhere] + [in_vmem] * 4 + [anywhere] * 3,
        out_specs=in_vmem,
        scratch_shapes=[
            pltpu.VMEM((rows + 2, lon_total, channels), jnp.bfloat16),
            pltpu.VMEM((half // 2, 2 * bases * cols, 4 * lon_total), jnp.bfloat16),
            pltpu.VMEM((half // 2, 2 * bases * cols, 16 * cols), jnp.bfloat16),
            pltpu.VMEM((half * cols, bases * channels), jnp.bfloat16),
            pltpu.VMEM((bases * channels, channels), jnp.bfloat16),
            pltpu.VMEM((channels, hidden), jnp.bfloat16),
            pltpu.VMEM((hidden, channels), jnp.bfloat16),
            pltpu.SemaphoreType.DMA((copies,)),
            pltpu.SemaphoreType.DMA((copies,)),
            pltpu.SemaphoreType.DMA((4,)),
        ],
        compiler_params=pltpu.CompilerParams(
            collective_id=0, has_side_effects=True, vmem_limit_bytes=56 * 1024 * 1024
        ),
    )(
        jnp.transpose(fields, (1, 2, 0)),
        jnp.transpose(support_rows, (0, 2, 1)),
        jnp.transpose(support_lons, (0, 2, 1)),
        jnp.transpose(support_weights, (0, 2, 1)),
        norm_gain,
        mix_weight.reshape(bases * channels, channels),
        up_weight,
        down_weight,
    )
    return jnp.transpose(result, (2, 0, 1))


def direct_call(
    lon_count,
    lat_count,
    fields,
    support_rows,
    support_lons,
    support_weights,
    mix_weight,
    norm_gain,
    up_weight,
    down_weight,
):
    channels, rows, cols = fields.shape
    bases, hidden = mix_weight.shape[0], up_weight.shape[1]
    lon_total = lon_count * cols
    plan = plan_copies(lon_count, lat_count, rows, cols)
    count = sum(len(stage) for stage in plan[1])
    in_vmem = pl.BlockSpec(memory_space=pltpu.VMEM)
    anywhere = pl.BlockSpec(memory_space=pl.ANY)
    result = pl.pallas_call(
        functools.partial(block_kernel, lon_count, lat_count, plan),
        out_shape=jax.ShapeDtypeStruct((rows, cols, channels), jnp.bfloat16),
        in_specs=[anywhere] + [in_vmem] * 4 + [anywhere] * 3,
        out_specs=anywhere,
        scratch_shapes=[
            pltpu.VMEM((rows, cols, channels), jnp.bfloat16),
            pltpu.VMEM((rows, cols, channels), jnp.bfloat16),
            pltpu.VMEM((rows + 2, lon_total, channels), jnp.bfloat16),
            pltpu.VMEM((rows, bases * cols, 3 * lon_total), jnp.bfloat16),
            pltpu.VMEM((rows // 2 * cols, bases * channels), jnp.bfloat16),
            pltpu.VMEM((bases * channels, channels), jnp.bfloat16),
            pltpu.VMEM((channels, hidden), jnp.bfloat16),
            pltpu.VMEM((hidden, channels), jnp.bfloat16),
            pltpu.SemaphoreType.DMA((count,)),
            pltpu.SemaphoreType.DMA((count,)),
            pltpu.SemaphoreType.DMA((4,)),
            pltpu.SemaphoreType.DMA((len(plan[0]),)),
        ],
        compiler_params=pltpu.CompilerParams(
            collective_id=0, has_side_effects=True, vmem_limit_bytes=56 * 1024 * 1024
        ),
    )(
        jnp.transpose(fields, (1, 2, 0)),
        jnp.transpose(support_rows, (0, 2, 1)),
        jnp.transpose(support_lons, (0, 2, 1)),
        jnp.transpose(support_weights, (0, 2, 1)),
        norm_gain,
        mix_weight.reshape(bases * channels, channels),
        up_weight,
        down_weight,
    )
    return jnp.transpose(result, (2, 0, 1))


def on_device(lon_count, lat_count, *arrays):
    channels, rows, cols = arrays[0].shape
    if relay_fits(lon_count, lat_count, rows, cols):
        return relay_call(lon_count, lat_count, *arrays)
    return direct_call(lon_count, lat_count, *arrays)


def solution(mesh):
    in_specs = (P("member", "lat", "lon"), P(), P(), P(), P(), P(), P(), P())
    out_specs = P("member", "lat", "lon")
    return jax.shard_map(
        functools.partial(on_device, mesh.shape["lon"], mesh.shape["lat"]),
        mesh=mesh,
        in_specs=in_specs,
        out_specs=out_specs,
        check_vma=False,
    )
```

```python
import functools
import math

import jax
import jax.numpy as jnp
from jax import lax
from jax.experimental import pallas as pl
from jax.experimental.pallas import tpu as pltpu
from jax.sharding import PartitionSpec as P

norm_eps = 1e-05
MESH = pl.DeviceIdType.MESH


def plan_copies(lon_count, lat_count, rows, cols):
    lon_total, row_total = lon_count * cols, lat_count * rows

    def reach(row):
        nearest = min(row + 1, row_total - row)
        return min(lon_total // 2, 4 * row_total // nearest)

    def distance(row):
        return min(-(-reach(row) // cols), lon_count // 2)

    def in_half(span, delta):
        if delta == 0 or abs(delta) == lon_count // 2:
            return False
        return span - cols * (abs(delta) - 1) <= cols // 2

    need = [distance(max(p - 1, 0)) for p in range(rows)]
    deltas = [d for d in range(1 - lon_count // 2, lon_count // 2 + 1) if d != 0]
    counts = {delta: sum(1 for d in need if d >= abs(delta)) for delta in deltas}
    spans = [reach(max(p - 1, 0)) for p in range(rows)]
    fulls = {d: sum(1 for p in range(counts[d]) if not in_half(spans[p], d)) for d in deltas}
    edge, edge_span = 0, 0
    for boundary in range(1, lat_count):
        edge = max(edge, distance(boundary * rows - 1), distance(boundary * rows))
        edge_span = max(edge_span, reach(boundary * rows - 1), reach(boundary * rows))
    halo = [d for d in range(1 - lon_count // 2, lon_count // 2 + 1) if abs(d) <= edge]
    groups = [(rows // 2, rows), (rows // 4, rows // 2), (0, rows // 4)]
    stages = []
    upper = rows
    for low, _ in groups:
        lower = max(low - 1, 0)
        stage = []
        for delta in sorted(deltas, key=lambda d: -abs(d)):
            full, top = min(fulls[delta], upper), min(counts[delta], upper)
            if full > lower:
                stage.append(("block", delta, lower, full, False))
            if top > max(full, lower):
                stage.append(("block", delta, max(full, lower), top, True))
        stages.append(stage)
        upper = lower
    if lat_count > 1:
        stages[0] = [
            (side, d, 0, 1, in_half(edge_span, d)) for d in halo for side in ("down", "up")
        ] + stages[0]
    halves = [d for d in halo if in_half(edge_span, d)]
    return groups, stages, counts, fulls, halo, halves


def block_kernel(
    lon_count,
    lat_count,
    plan,
    x_hbm,
    rows_ref,
    lons_ref,
    weights_ref,
    gain_ref,
    mix_hbm,
    up_hbm,
    down_hbm,
    out_hbm,
    x_ref,
    out_ref,
    window,
    filters,
    product,
    mix_ref,
    up_ref,
    down_ref,
    send_sem,
    recv_sem,
    load_sem,
    out_sem,
):
    rows, cols, channels = x_ref.shape
    bases, entries = rows_ref.shape[:2]
    lon_total = lon_count * cols
    middle = lon_count // 2
    groups, stages, counts, fulls, halo, halves = plan
    me, lat = lax.axis_index("lon"), lax.axis_index("lat")
    north = 2 * lat < lat_count
    has_low, has_high = lat > 0, lat < lat_count - 1

    loads = [
        pltpu.make_async_copy(mix_hbm, mix_ref, load_sem.at[0]),
        pltpu.make_async_copy(up_hbm, up_ref, load_sem.at[1]),
        pltpu.make_async_copy(down_hbm, down_ref, load_sem.at[2]),
    ]
    fetch = pltpu.make_async_copy(x_hbm, x_ref, load_sem.at[3])
    fetch.start()

    barrier = pltpu.get_barrier_semaphore()
    halo_deltas = halo if lat_count > 1 else []
    for delta in range(1, lon_count):
        pl.semaphore_signal(
            barrier, inc=1, device_id={"lon": lax.rem(me + delta, lon_count)}, device_id_type=MESH
        )
    for present, other in ((has_low, lat - 1), (has_high, lat + 1)):

        @pl.when(present)
        def _():
            for delta in halo_deltas:
                target = lax.rem(me + lon_count - delta, lon_count)
                pl.semaphore_signal(
                    barrier, inc=1, device_id={"lon": target, "lat": other}, device_id_type=MESH
                )

    sides = jnp.where(has_low, 1, 0) + jnp.where(has_high, 1, 0)
    pl.semaphore_wait(barrier, lon_count - 1 + sides * len(halo_deltas))
    fetch.wait()

    def copy_of(index, item):
        kind, delta, first, last, halved = item
        width = cols // 2 if halved else cols
        offset = cols // 2 if halved and delta < 0 else 0
        target = lax.rem(me + lon_count - delta, lon_count)
        slot = (delta + middle) % lon_count
        here, there = pl.ds(offset, width), pl.ds(slot * cols + offset, width)
        if kind == "block":
            start = jnp.where(north, first, rows - last)
            source = x_ref.at[pl.ds(start, last - first), here]
            landing = window.at[pl.ds(start + 1, last - first), there]
            device = {"lon": target}
        elif kind == "down":
            source = x_ref.at[pl.ds(rows - 1, 1), here]
            landing = window.at[pl.ds(0, 1), there]
            device = {"lon": target, "lat": jnp.minimum(lat + 1, lat_count - 1)}
        else:
            source = x_ref.at[pl.ds(0, 1), here]
            landing = window.at[pl.ds(rows + 1, 1), there]
            device = {"lon": target, "lat": jnp.maximum(lat - 1, 0)}
        return pltpu.make_async_remote_copy(
            src_ref=source,
            dst_ref=landing,
            send_sem=send_sem.at[index],
            recv_sem=recv_sem.at[index],
            device_id=device,
            device_id_type=MESH,
        )

    copies = []
    for stage in stages:
        copies.append(list(enumerate(stage, sum(len(done) for done in copies))))

    def each(items, sending, action):
        for index, item in items:
            if item[0] == "block":
                action(copy_of(index, item))
            else:
                present = has_high if (item[0] == "down") == sending else has_low

                @pl.when(present)
                def _():
                    action(copy_of(index, item))

    for stage in copies:
        each(stage, True, lambda copy: copy.start())
    for load in loads:
        load.start()

    window[1 : rows + 1, middle * cols : (middle + 1) * cols, :] = x_ref[...]
    for delta, count in counts.items():
        slot = (delta + middle) % lon_count
        if count < rows:
            gap = (rows - count, cols, channels)
            window[pl.ds(jnp.where(north, count, 0) + 1, rows - count),
                   slot * cols : (slot + 1) * cols] = jnp.zeros(gap, jnp.bfloat16)
        partial = count - fulls[delta]
        if partial > 0:
            far = slot * cols + (0 if delta < 0 else cols // 2)
            window[pl.ds(jnp.where(north, fulls[delta], rows - count) + 1, partial),
                   far : far + cols // 2] = jnp.zeros(
                (partial, cols // 2, channels), jnp.bfloat16
            )
    for delta in halves:
        far = (delta + middle) % lon_count * cols + (0 if delta < 0 else cols // 2)
        for line in (0, rows + 1):
            window[line, far : far + cols // 2] = jnp.zeros((cols // 2, channels), jnp.bfloat16)
    for present, line in ((has_low, 0), (has_high, rows + 1)):
        for delta in range(1 - middle, middle + 1):
            slot = (delta + middle) % lon_count

            def clear():
                window[line, slot * cols : (slot + 1) * cols] = jnp.zeros(
                    (cols, channels), jnp.bfloat16
                )

            if delta in halo and lat_count > 1:
                pl.when(jnp.logical_not(present))(clear)
            else:
                clear()

    lanes = lax.broadcasted_iota(jnp.int32, (rows, lon_total), 1)
    wide = (rows, rows_ref.shape[2])
    own_rows = (
        lax.broadcasted_iota(jnp.int32, wide, 0) + lat * rows
        == lax.broadcasted_iota(jnp.int32, wide, 1)
    ).astype(jnp.float32)

    def own(ref, k):
        return lax.dot_general(
            own_rows,
            ref[k].astype(jnp.float32),
            (((1,), (1,)), ((), ())),
            precision=lax.Precision.HIGHEST,
            preferred_element_type=jnp.float32,
        )

    def build(k, carry):
        spot = own(lons_ref, k).astype(jnp.int32) + middle * cols
        spot = jnp.where(spot >= lon_total, spot - lon_total, spot)
        row_offset = own(rows_ref, k)
        weight = own(weights_ref, k)
        picked = [jnp.where(row_offset == r, weight, 0.0) for r in (-1.0, 0.0, 1.0)]
        sums = [jnp.zeros((rows, lon_total), jnp.float32) for _ in range(3)]
        for s in range(entries):
            hit = spot[:, s : s + 1] == lanes
            for r in range(3):
                sums[r] = sums[r] + jnp.where(hit, picked[r][:, s : s + 1], 0.0)
        for r in range(3):
            for i in range(rows):
                line = jnp.broadcast_to(sums[r][i : i + 1, :], (cols, lon_total))
                turned = pltpu.roll(line, 0, 1, stride=1, stride_axis=0)
                filters[i, pl.ds(pl.multiple_of(k * cols, cols), cols),
                        r * lon_total : (r + 1) * lon_total] = turned.astype(jnp.bfloat16)
        return carry

    lax.fori_loop(0, bases, build, 0)

    def group(low, high):
        start = jnp.where(north, low, rows - high)
        half = high - low
        lines = half * cols
        def filter_row(t, carry):
            i = start + t
            source = window[pl.ds(i, 3)].reshape(3 * lon_total, channels)
            filtered = jnp.dot(filters[i], source, preferred_element_type=jnp.float32)
            filtered = filtered.astype(jnp.bfloat16)
            at = pl.multiple_of(t * cols, cols)
            for k in range(bases):
                product[pl.ds(at, cols), k * channels : (k + 1) * channels] = filtered[
                    k * cols : (k + 1) * cols
                ]
            return carry

        lax.fori_loop(0, half, filter_row, 0)
        mixed = jnp.dot(product[:lines], mix_ref[...], preferred_element_type=jnp.float32)
        here = x_ref[pl.ds(start, half)].reshape(lines, channels)
        latent = here.astype(jnp.float32) + mixed
        mean = jnp.mean(latent, axis=1, keepdims=True)
        centred = latent - mean
        variance = jnp.mean(centred * centred, axis=1, keepdims=True)
        normed = (centred * lax.rsqrt(variance + norm_eps) * gain_ref[...][None, :]).astype(jnp.bfloat16)
        raised = jnp.dot(normed, up_ref[...], preferred_element_type=jnp.float32)
        hidden = 0.5 * raised * (1.0 + lax.erf(raised * math.sqrt(0.5)))
        lowered = jnp.dot(
            hidden.astype(jnp.bfloat16), down_ref[...], preferred_element_type=jnp.float32
        )
        result = (latent + lowered).astype(jnp.bfloat16)
        out_ref[pl.ds(start, half)] = result.reshape(half, cols, channels)

    puts = []
    for stage, (low, high) in zip(copies, groups):
        each(stage, False, lambda copy: copy.wait_recv())
        if stage is copies[0]:
            for load in loads:
                load.wait()
        group(low, high)
        part = pl.ds(jnp.where(north, low, rows - high), high - low)
        put = pltpu.make_async_copy(out_ref.at[part], out_hbm.at[part], out_sem.at[len(puts)])
        put.start()
        puts.append(put)
    for stage in copies:
        each(stage, True, lambda copy: copy.wait_send())
    for put in puts:
        put.wait()


def source_reach(lon_total, row_total, p):
    row = max(p - 1, 0)
    return min(lon_total // 2, 4 * row_total // min(row + 1, row_total - row))


def fold_rows(lon_count, lat_count, rows, cols):
    lon_total, row_total = lon_count * cols, lat_count * rows
    fold = 2
    while source_reach(lon_total, row_total, fold + 1) > 2 * cols:
        fold += 2
    return fold


def relay_fits(lon_count, lat_count, rows, cols):
    lon_total, row_total = lon_count * cols, lat_count * rows
    if lon_count != 8 or lat_count != 2 or rows % 4 != 0 or cols != 16:
        return False
    near = source_reach(lon_total, row_total, rows // 2 + 1) <= cols
    return near and fold_rows(lon_count, lat_count, rows, cols) <= rows // 4


def relay_kernel(
    lon_count,
    lat_count,
    x_hbm,
    rows_ref,
    lons_ref,
    weights_ref,
    gain_ref,
    mix_hbm,
    up_hbm,
    down_hbm,
    out_ref,
    window,
    fold_filters,
    wide_filters,
    near_filters,
    product,
    mixed_ref,
    fold_out,
    fold_in,
    mix_ref,
    up_ref,
    down_ref,
    send_sem,
    recv_sem,
    load_sem,
):
    rows, cols, channels = x_hbm.shape
    bases, entries = rows_ref.shape[:2]
    lon_total, row_total = lon_count * cols, lat_count * rows
    middle, part, half = lon_count // 2, cols // 2, rows // 2
    home = middle * cols
    fold = fold_rows(lon_count, lat_count, rows, cols)
    reaches = [source_reach(lon_total, row_total, max(p, fold + 1)) for p in range(rows)]
    wide = sum(1 for r in reaches if r > cols + part)
    near = sum(1 for r in reaches if r > cols)
    me, lat = lax.axis_index("lon"), lax.axis_index("lat")
    north = lat == 0
    turn = 1 - 2 * lax.rem(me, 2)
    place = lax.rem(me, middle)
    inward = jnp.where(place < 2, 1, -1)
    edge = jnp.where(north, rows - 1, 0)

    def device(delta):
        return lax.rem(me + delta + lon_count, lon_count)

    def at(delta):
        return pl.multiple_of(lax.rem(delta + middle + lon_count, lon_count) * cols, cols)

    def lines(first, last):
        return pl.ds(jnp.where(north, first, rows - last) + 1, last - first)

    fetch = pltpu.make_async_copy(
        x_hbm, window.at[pl.ds(1, rows), pl.ds(home, cols)], load_sem.at[3]
    )
    fetch.start()
    loads = [
        pltpu.make_async_copy(mix_hbm, mix_ref, load_sem.at[0]),
        pltpu.make_async_copy(up_hbm, up_ref, load_sem.at[1]),
        pltpu.make_async_copy(down_hbm, down_ref, load_sem.at[2]),
    ]
    barrier = pltpu.get_barrier_semaphore()
    others = [{"lon": me + turn}] + [{"lon": device(2 * e)} for e in (1, -1, 2)]
    others.append({"lat": 1 - lat})
    for other in others:
        pl.semaphore_signal(barrier, inc=1, device_id=other, device_id_type=MESH)
    for load in loads:
        load.start()

    def clear(where, low, high):
        size = where.size if isinstance(where, pl.Slice) else 1
        window[where, low:high] = jnp.zeros((size, high - low, channels), jnp.bfloat16)

    outer, halo = jnp.where(north, 0, rows + 1), jnp.where(north, rows + 1, 0)
    clear(pl.ds(outer, 1), 0, lon_total)
    clear(lines(fold + 1, wide), 0, home - 2 * cols)
    clear(lines(fold + 1, wide), home + 3 * cols, lon_total)
    clear(lines(fold - 1, fold + 1), 0, cols)

    @pl.when(place != middle - 1)
    def _():
        clear(lines(fold - 1, fold + 1), cols, 2 * cols)

    @pl.when(place != 0)
    def _():
        clear(lines(fold - 1, fold + 1), home + 3 * cols, lon_total)

    clear(lines(wide, near), 0, home - cols - part)
    clear(lines(wide, near), home + 2 * cols + part, lon_total)
    clear(lines(near, half + 1), 0, home - cols)
    clear(lines(near, half + 1), home + 2 * cols, lon_total)
    clear(lines(half + 1, rows), home + 2 * cols, home + 3 * cols)
    clear(pl.ds(halo, 1), home - cols, home - part)
    clear(pl.ds(halo, 1), home + cols + part, home + 3 * cols)

    count = [0]

    def message(where, here, there, width, target, landing=None):
        index = count[0]
        count[0] += 1
        landing = where if landing is None else landing
        return pltpu.make_async_remote_copy(
            src_ref=window.at[where, pl.ds(here, width)],
            dst_ref=window.at[landing, pl.ds(there, width)],
            send_sem=send_sem.at[index],
            recv_sem=recv_sem.at[index],
            device_id=target,
            device_id_type=MESH,
        )

    partner, beside = {"lon": me + turn}, {"lon": device(2 * turn)}
    core, core_line = {"lat": 1 - lat}, pl.ds(edge + 1, 1)
    core_landing = pl.ds(jnp.where(north, 0, rows + 1), 1)

    def own_across(first, last):
        return message(lines(first, last), home, at(-turn), cols, partner)

    def own_along(first, last, e):
        return message(lines(first, last), home, at(-2 * e), cols, {"lon": device(2 * e)})

    def half_along(first, last, e):
        offset = part if e > 0 else 0
        return message(
            lines(first, last), home + offset, at(-2 * e) + offset, part, {"lon": device(2 * e)}
        )

    def pass_along(first, last):
        return message(lines(first, last), at(turn), at(-turn), cols, beside)

    def pass_across(first, last, e):
        return message(lines(first, last), at(2 * e), at(2 * e - turn), cols, partner)

    def to_core(col, width):
        return message(core_line, col, col, width, core, core_landing)

    after = pl.multiple_of(home + jnp.where(turn > 0, cols, -part), part)
    before = pl.multiple_of(home + jnp.where(turn > 0, -part, cols), part)
    near_cut = half + (rows - half) // 2
    halo_own = to_core(home, cols)
    halo_across, halo_along = to_core(after, part), to_core(before, part)
    cuts = [(near_cut, rows), (half - 1, near_cut), (wide - 1, half - 1)]
    across = [own_across(*cut) for cut in cuts]
    along = [pass_along(*cut) for cut in cuts[:2]] + [pass_along(wide, half - 1)]
    halves = [half_along(wide, near, e) for e in (1, -1)]
    fold_own = own_across(0, fold + 1)
    along_in, along_out = own_along(0, wide, inward), own_along(fold - 1, wide, -inward)
    fold_across = pass_across(0, fold + 1, inward)
    same = turn == inward
    late_across = pass_across(fold + 1, wide, turn), pass_across(fold - 1, wide, turn)
    index = count[0]
    fold_swap = pltpu.make_async_remote_copy(
        src_ref=fold_out,
        dst_ref=fold_in,
        send_sem=send_sem.at[index],
        recv_sem=recv_sem.at[index],
        device_id={"lon": device(middle)},
        device_id_type=MESH,
    )

    def start(*copies):
        for copy in copies:
            copy.start()

    def arrived(*copies):
        for copy in copies:
            copy.wait_recv()

    wide_rows = (half, rows_ref.shape[2])

    def table(ref, k, first):
        order = lax.broadcasted_iota(jnp.int32, wide_rows, 0) + first
        local = jnp.where(north, order, rows - 2 - order + 2 * lax.rem(order, 2))
        mine = (local + lat * rows == lax.broadcasted_iota(jnp.int32, wide_rows, 1)).astype(
            jnp.float32
        )
        return lax.dot_general(
            mine,
            ref[k].astype(jnp.float32),
            (((1,), (1,)), ((), ())),
            precision=lax.Precision.HIGHEST,
            preferred_element_type=jnp.float32,
        )

    lanes = lax.broadcasted_iota(jnp.int32, (half, lon_total), 1)
    second = lax.rem(lax.broadcasted_iota(jnp.int32, (half, entries), 0), 2)

    def turned(line, shift):
        spread = jnp.broadcast_to(line, (cols, lon_total))
        return pltpu.roll(spread, shift, 1, stride=1, stride_axis=0)

    def build_near(k, carry):
        offset = table(lons_ref, k, half).astype(jnp.int32)
        row_offset = table(rows_ref, k, half).astype(jnp.int32)
        weight = table(weights_ref, k, half)
        spot = (row_offset + 1 + second) * (4 * cols) + offset + cols
        sums = [jnp.zeros((half, lon_total), jnp.float32) for _ in range(2)]
        for s in range(entries):
            for v in range(2):
                hit = spot[:, s : s + 1] == lanes + v * lon_total
                sums[v] = sums[v] + jnp.where(hit, weight[:, s : s + 1], 0.0)
        for n in range(half):
            for v in range(2):
                spot_at = pl.multiple_of(k * 2 * cols + (n % 2) * cols, cols)
                near_filters[n // 2, pl.ds(spot_at, cols), v * lon_total : (v + 1) * lon_total] = (
                    turned(sums[v][n : n + 1, :], 0).astype(jnp.bfloat16)
                )
        return carry

    polar = lax.broadcasted_iota(jnp.int32, (half, entries), 0) < fold
    start_col = jnp.where(polar, place * cols, home)
    lower = lax.broadcasted_iota(jnp.int32, (cols, lon_total), 1) < home

    def build_polar(k, carry):
        spot = table(lons_ref, k, 0).astype(jnp.int32) + start_col
        spot = jnp.where(spot >= lon_total, spot - lon_total, spot)
        spot = jnp.where(spot < 0, spot + lon_total, spot)
        row_offset = table(rows_ref, k, 0)
        weight = table(weights_ref, k, 0)
        picked = [jnp.where(row_offset == r, weight, 0.0) for r in (-1.0, 0.0, 1.0)]
        sums = [jnp.zeros((half, lon_total), jnp.float32) for _ in range(3)]
        for s in range(entries):
            hit = spot[:, s : s + 1] == lanes
            for r in range(3):
                sums[r] = sums[r] + jnp.where(hit, picked[r][:, s : s + 1], 0.0)
        none = jnp.zeros((cols, lon_total), jnp.float32)
        for n in range(fold):
            late = n % 2
            kept = [none] * 4
            moved = [none] * 4
            for r in range(3):
                kept[r + late] = turned(sums[r][n : n + 1, :], 0)
                moved[r + late] = turned(sums[r][n : n + 1, :], home)
            for v in range(2):
                here = jnp.where(lower, kept[2 * v], moved[2 * v + 1])
                there = jnp.where(lower, moved[2 * v], kept[2 * v + 1])
                for who, value in enumerate((here, there)):
                    spot_at = pl.multiple_of(k * 4 * cols + (2 * who + late) * cols, cols)
                    fold_filters[
                        n // 2, pl.ds(spot_at, cols), v * lon_total : (v + 1) * lon_total
                    ] = value.astype(jnp.bfloat16)
        for n in range(fold, half):
            late = n % 2
            spot_at = pl.ds(pl.multiple_of(k * 2 * cols + late * cols, cols), cols)
            for r in range(3):
                low = (r + late) * lon_total
                wide_filters[(n - fold) // 2, spot_at, low : low + lon_total] = turned(
                    sums[r][n : n + 1, :], 0
                ).astype(jnp.bfloat16)
            low = (3 - 3 * late) * lon_total
            wide_filters[(n - fold) // 2, spot_at, low : low + lon_total] = none.astype(jnp.bfloat16)
        return carry

    def filter_pairs(first, last):
        pairs = last - first
        base = jnp.where(north, 2 * first, rows - 2 * last)
        for t in range(pairs):
            q = jnp.where(north, first + t, last - 1 - t)
            taken = pl.ds(base + 2 * t, 4)
            if 2 * first >= half:
                low = home - cols
                source = window[taken, low : low + 4 * cols].reshape(16 * cols, channels)
                matrix = near_filters[q - half // 2]
            else:
                source = window[taken].reshape(4 * lon_total, channels)
                matrix = wide_filters[q - fold // 2]
            filtered = jnp.dot(matrix, source, preferred_element_type=jnp.float32)
            filtered = filtered.astype(jnp.bfloat16)
            for k in range(bases):
                product[2 * t * cols : 2 * (t + 1) * cols, k * channels : (k + 1) * channels] = (
                    filtered[2 * k * cols : 2 * (k + 1) * cols]
                )

    def fold_pairs():
        pairs = fold // 2
        cells = fold * cols
        base = jnp.where(north, 0, rows - fold)
        for t in range(pairs):
            q = jnp.where(north, t, pairs - 1 - t)
            source = window[pl.ds(base + 2 * t, 4), pl.ds(at(-place), 4 * cols)]
            source = source.reshape(16 * cols, channels)
            filtered = jnp.dot(fold_filters[q], source, preferred_element_type=jnp.float32)
            filtered = filtered.astype(jnp.bfloat16)
            for k in range(bases):
                for who in range(2):
                    low, from_row = who * cells + 2 * t * cols, (4 * k + 2 * who) * cols
                    product[low : low + 2 * cols, k * channels : (k + 1) * channels] = filtered[
                        from_row : from_row + 2 * cols
                    ]
        mixed = jnp.dot(product[: 2 * cells], mix_ref[...], preferred_element_type=jnp.float32)
        fold_out[...] = mixed[cells:].astype(jnp.bfloat16)
        mixed_ref[pl.ds(jnp.where(north, 0, half * cols - cells), cells)] = mixed[:cells]

    def mix_pairs(pairs):
        cells = 2 * pairs * cols
        return jnp.dot(product[:cells], mix_ref[...], preferred_element_type=jnp.float32)

    def finish(mixed, base, depth):
        cells = depth * cols
        here = window[pl.ds(base + 1, depth), home : home + cols].reshape(cells, channels)
        latent = here.astype(jnp.float32) + mixed
        mean = jnp.mean(latent, axis=1, keepdims=True)
        centred = latent - mean
        variance = jnp.mean(centred * centred, axis=1, keepdims=True)
        normed = (centred * lax.rsqrt(variance + norm_eps) * gain_ref[...][None, :]).astype(
            jnp.bfloat16
        )
        raised = jnp.dot(normed, up_ref[...], preferred_element_type=jnp.float32)
        hidden = 0.5 * raised * (1.0 + lax.erf(raised * math.sqrt(0.5)))
        lowered = jnp.dot(
            hidden.astype(jnp.bfloat16), down_ref[...], preferred_element_type=jnp.float32
        )
        result = (latent + lowered).astype(jnp.bfloat16)
        out_ref[pl.ds(base, depth)] = result.reshape(depth, cols, channels)

    fold_pair, half_pair, all_pairs = fold // 2, half // 2, rows // 2
    pl.semaphore_wait(barrier, len(others))
    fetch.wait()
    start(halo_own, fold_own, along_in, along_out, across[0], across[1], *halves)
    lax.fori_loop(0, bases, build_near, 0)
    lax.fori_loop(0, bases, build_polar, 0)
    arrived(across[0])
    start(along[0], halo_across)
    arrived(along_in)
    start(fold_across, across[2])
    arrived(across[1])
    start(along[1])
    arrived(along_out)

    @pl.when(same)
    def _():
        start(late_across[0])

    @pl.when(jnp.logical_not(same))
    def _():
        start(late_across[1])

    for load in loads:
        load.wait()
    arrived(fold_own, fold_across)
    fold_pairs()
    arrived(across[2])
    start(along[2])
    start(fold_swap)
    arrived(along[0])
    start(halo_along)
    arrived(halo_own, halo_across, halo_along, along[1], *halves)
    filter_pairs(half_pair, all_pairs)
    finish(mix_pairs(all_pairs - half_pair), jnp.where(north, half, 0), rows - half)
    arrived(along[2])

    @pl.when(same)
    def _():
        arrived(late_across[1])

    @pl.when(jnp.logical_not(same))
    def _():
        arrived(late_across[0])

    filter_pairs(fold_pair, half_pair)
    cells = (half - fold) * cols
    mixed_ref[pl.ds(jnp.where(north, fold * cols, 0), cells)] = mix_pairs(half_pair - fold_pair)
    arrived(fold_swap)
    own_part = pl.ds(jnp.where(north, 0, half * cols - fold * cols), fold * cols)
    mixed_ref[own_part] = mixed_ref[own_part] + fold_in[...].astype(jnp.float32)
    finish(mixed_ref[...], jnp.where(north, 0, half), half)

    @pl.when(same)
    def _():
        late_across[0].wait_send()

    @pl.when(jnp.logical_not(same))
    def _():
        late_across[1].wait_send()

    sent = [halo_own, halo_across, halo_along, fold_own, fold_across, along_in, along_out]
    for copy in sent + across + along + halves + [fold_swap]:
        copy.wait_send()


def relay_call(
    lon_count,
    lat_count,
    fields,
    support_rows,
    support_lons,
    support_weights,
    mix_weight,
    norm_gain,
    up_weight,
    down_weight,
):
    channels, rows, cols = fields.shape
    bases, hidden = mix_weight.shape[0], up_weight.shape[1]
    lon_total = lon_count * cols
    half, copies = rows // 2, 20
    fold = fold_rows(lon_count, lat_count, rows, cols)
    in_vmem = pl.BlockSpec(memory_space=pltpu.VMEM)
    anywhere = pl.BlockSpec(memory_space=pl.ANY)
    result = pl.pallas_call(
        functools.partial(relay_kernel, lon_count, lat_count),
        out_shape=pltpu.VMEM((rows, cols, channels), jnp.bfloat16),
        in_specs=[anywhere] + [in_vmem] * 4 + [anywhere] * 3,
        out_specs=in_vmem,
        scratch_shapes=[
            pltpu.VMEM((rows + 2, lon_total, channels), jnp.bfloat16),
            pltpu.VMEM((fold // 2, 4 * bases * cols, 16 * cols), jnp.bfloat16),
            pltpu.VMEM(((half - fold) // 2, 2 * bases * cols, 4 * lon_total), jnp.bfloat16),
            pltpu.VMEM((half // 2, 2 * bases * cols, 16 * cols), jnp.bfloat16),
            pltpu.VMEM((half * cols, bases * channels), jnp.bfloat16),
            pltpu.VMEM((half * cols, channels), jnp.float32),
            pltpu.VMEM((fold * cols, channels), jnp.bfloat16),
            pltpu.VMEM((fold * cols, channels), jnp.bfloat16),
            pltpu.VMEM((bases * channels, channels), jnp.bfloat16),
            pltpu.VMEM((channels, hidden), jnp.bfloat16),
            pltpu.VMEM((hidden, channels), jnp.bfloat16),
            pltpu.SemaphoreType.DMA((copies,)),
            pltpu.SemaphoreType.DMA((copies,)),
            pltpu.SemaphoreType.DMA((4,)),
        ],
        compiler_params=pltpu.CompilerParams(
            collective_id=0, has_side_effects=True, vmem_limit_bytes=56 * 1024 * 1024
        ),
    )(
        jnp.transpose(fields, (1, 2, 0)),
        jnp.transpose(support_rows, (0, 2, 1)),
        jnp.transpose(support_lons, (0, 2, 1)),
        jnp.transpose(support_weights, (0, 2, 1)),
        norm_gain,
        mix_weight.reshape(bases * channels, channels),
        up_weight,
        down_weight,
    )
    return jnp.transpose(result, (2, 0, 1))


def direct_call(
    lon_count,
    lat_count,
    fields,
    support_rows,
    support_lons,
    support_weights,
    mix_weight,
    norm_gain,
    up_weight,
    down_weight,
):
    channels, rows, cols = fields.shape
    bases, hidden = mix_weight.shape[0], up_weight.shape[1]
    lon_total = lon_count * cols
    plan = plan_copies(lon_count, lat_count, rows, cols)
    count = sum(len(stage) for stage in plan[1])
    in_vmem = pl.BlockSpec(memory_space=pltpu.VMEM)
    anywhere = pl.BlockSpec(memory_space=pl.ANY)
    result = pl.pallas_call(
        functools.partial(block_kernel, lon_count, lat_count, plan),
        out_shape=jax.ShapeDtypeStruct((rows, cols, channels), jnp.bfloat16),
        in_specs=[anywhere] + [in_vmem] * 4 + [anywhere] * 3,
        out_specs=anywhere,
        scratch_shapes=[
            pltpu.VMEM((rows, cols, channels), jnp.bfloat16),
            pltpu.VMEM((rows, cols, channels), jnp.bfloat16),
            pltpu.VMEM((rows + 2, lon_total, channels), jnp.bfloat16),
            pltpu.VMEM((rows, bases * cols, 3 * lon_total), jnp.bfloat16),
            pltpu.VMEM((rows // 2 * cols, bases * channels), jnp.bfloat16),
            pltpu.VMEM((bases * channels, channels), jnp.bfloat16),
            pltpu.VMEM((channels, hidden), jnp.bfloat16),
            pltpu.VMEM((hidden, channels), jnp.bfloat16),
            pltpu.SemaphoreType.DMA((count,)),
            pltpu.SemaphoreType.DMA((count,)),
            pltpu.SemaphoreType.DMA((4,)),
            pltpu.SemaphoreType.DMA((len(plan[0]),)),
        ],
        compiler_params=pltpu.CompilerParams(
            collective_id=0, has_side_effects=True, vmem_limit_bytes=56 * 1024 * 1024
        ),
    )(
        jnp.transpose(fields, (1, 2, 0)),
        jnp.transpose(support_rows, (0, 2, 1)),
        jnp.transpose(support_lons, (0, 2, 1)),
        jnp.transpose(support_weights, (0, 2, 1)),
        norm_gain,
        mix_weight.reshape(bases * channels, channels),
        up_weight,
        down_weight,
    )
    return jnp.transpose(result, (2, 0, 1))


def on_device(lon_count, lat_count, *arrays):
    channels, rows, cols = arrays[0].shape
    if relay_fits(lon_count, lat_count, rows, cols):
        return relay_call(lon_count, lat_count, *arrays)
    return direct_call(lon_count, lat_count, *arrays)


def solution(mesh):
    in_specs = (P("member", "lat", "lon"), P(), P(), P(), P(), P(), P(), P())
    out_specs = P("member", "lat", "lon")
    return jax.shard_map(
        functools.partial(on_device, mesh.shape["lon"], mesh.shape["lat"]),
        mesh=mesh,
        in_specs=in_specs,
        out_specs=out_specs,
        check_vma=False,
    )
```

```python
import functools
import math

import jax
import jax.numpy as jnp
from jax import lax
from jax.experimental import pallas as pl
from jax.experimental.pallas import tpu as pltpu
from jax.sharding import PartitionSpec as P

norm_eps = 1e-05
MESH = pl.DeviceIdType.MESH


def plan_copies(lon_count, lat_count, rows, cols):
    lon_total, row_total = lon_count * cols, lat_count * rows

    def reach(row):
        nearest = min(row + 1, row_total - row)
        return min(lon_total // 2, 4 * row_total // nearest)

    def distance(row):
        return min(-(-reach(row) // cols), lon_count // 2)

    def in_half(span, delta):
        if delta == 0 or abs(delta) == lon_count // 2:
            return False
        return span - cols * (abs(delta) - 1) <= cols // 2

    need = [distance(max(p - 1, 0)) for p in range(rows)]
    deltas = [d for d in range(1 - lon_count // 2, lon_count // 2 + 1) if d != 0]
    counts = {delta: sum(1 for d in need if d >= abs(delta)) for delta in deltas}
    spans = [reach(max(p - 1, 0)) for p in range(rows)]
    fulls = {d: sum(1 for p in range(counts[d]) if not in_half(spans[p], d)) for d in deltas}
    edge, edge_span = 0, 0
    for boundary in range(1, lat_count):
        edge = max(edge, distance(boundary * rows - 1), distance(boundary * rows))
        edge_span = max(edge_span, reach(boundary * rows - 1), reach(boundary * rows))
    halo = [d for d in range(1 - lon_count // 2, lon_count // 2 + 1) if abs(d) <= edge]
    groups = [(rows // 2, rows), (rows // 4, rows // 2), (0, rows // 4)]
    stages = []
    upper = rows
    for low, _ in groups:
        lower = max(low - 1, 0)
        stage = []
        for delta in sorted(deltas, key=lambda d: -abs(d)):
            full, top = min(fulls[delta], upper), min(counts[delta], upper)
            if full > lower:
                stage.append(("block", delta, lower, full, False))
            if top > max(full, lower):
                stage.append(("block", delta, max(full, lower), top, True))
        stages.append(stage)
        upper = lower
    if lat_count > 1:
        stages[0] = [
            (side, d, 0, 1, in_half(edge_span, d)) for d in halo for side in ("down", "up")
        ] + stages[0]
    halves = [d for d in halo if in_half(edge_span, d)]
    return groups, stages, counts, fulls, halo, halves


def block_kernel(
    lon_count,
    lat_count,
    plan,
    x_hbm,
    rows_ref,
    lons_ref,
    weights_ref,
    gain_ref,
    mix_hbm,
    up_hbm,
    down_hbm,
    out_hbm,
    x_ref,
    out_ref,
    window,
    filters,
    product,
    mix_ref,
    up_ref,
    down_ref,
    send_sem,
    recv_sem,
    load_sem,
    out_sem,
):
    rows, cols, channels = x_ref.shape
    bases, entries = rows_ref.shape[:2]
    lon_total = lon_count * cols
    middle = lon_count // 2
    groups, stages, counts, fulls, halo, halves = plan
    me, lat = lax.axis_index("lon"), lax.axis_index("lat")
    north = 2 * lat < lat_count
    has_low, has_high = lat > 0, lat < lat_count - 1

    loads = [
        pltpu.make_async_copy(mix_hbm, mix_ref, load_sem.at[0]),
        pltpu.make_async_copy(up_hbm, up_ref, load_sem.at[1]),
        pltpu.make_async_copy(down_hbm, down_ref, load_sem.at[2]),
    ]
    fetch = pltpu.make_async_copy(x_hbm, x_ref, load_sem.at[3])
    fetch.start()

    barrier = pltpu.get_barrier_semaphore()
    halo_deltas = halo if lat_count > 1 else []
    for delta in range(1, lon_count):
        pl.semaphore_signal(
            barrier, inc=1, device_id={"lon": lax.rem(me + delta, lon_count)}, device_id_type=MESH
        )
    for present, other in ((has_low, lat - 1), (has_high, lat + 1)):

        @pl.when(present)
        def _():
            for delta in halo_deltas:
                target = lax.rem(me + lon_count - delta, lon_count)
                pl.semaphore_signal(
                    barrier, inc=1, device_id={"lon": target, "lat": other}, device_id_type=MESH
                )

    sides = jnp.where(has_low, 1, 0) + jnp.where(has_high, 1, 0)
    pl.semaphore_wait(barrier, lon_count - 1 + sides * len(halo_deltas))
    fetch.wait()

    def copy_of(index, item):
        kind, delta, first, last, halved = item
        width = cols // 2 if halved else cols
        offset = cols // 2 if halved and delta < 0 else 0
        target = lax.rem(me + lon_count - delta, lon_count)
        slot = (delta + middle) % lon_count
        here, there = pl.ds(offset, width), pl.ds(slot * cols + offset, width)
        if kind == "block":
            start = jnp.where(north, first, rows - last)
            source = x_ref.at[pl.ds(start, last - first), here]
            landing = window.at[pl.ds(start + 1, last - first), there]
            device = {"lon": target}
        elif kind == "down":
            source = x_ref.at[pl.ds(rows - 1, 1), here]
            landing = window.at[pl.ds(0, 1), there]
            device = {"lon": target, "lat": jnp.minimum(lat + 1, lat_count - 1)}
        else:
            source = x_ref.at[pl.ds(0, 1), here]
            landing = window.at[pl.ds(rows + 1, 1), there]
            device = {"lon": target, "lat": jnp.maximum(lat - 1, 0)}
        return pltpu.make_async_remote_copy(
            src_ref=source,
            dst_ref=landing,
            send_sem=send_sem.at[index],
            recv_sem=recv_sem.at[index],
            device_id=device,
            device_id_type=MESH,
        )

    copies = []
    for stage in stages:
        copies.append(list(enumerate(stage, sum(len(done) for done in copies))))

    def each(items, sending, action):
        for index, item in items:
            if item[0] == "block":
                action(copy_of(index, item))
            else:
                present = has_high if (item[0] == "down") == sending else has_low

                @pl.when(present)
                def _():
                    action(copy_of(index, item))

    for stage in copies:
        each(stage, True, lambda copy: copy.start())
    for load in loads:
        load.start()

    window[1 : rows + 1, middle * cols : (middle + 1) * cols, :] = x_ref[...]
    for delta, count in counts.items():
        slot = (delta + middle) % lon_count
        if count < rows:
            gap = (rows - count, cols, channels)
            window[pl.ds(jnp.where(north, count, 0) + 1, rows - count),
                   slot * cols : (slot + 1) * cols] = jnp.zeros(gap, jnp.bfloat16)
        partial = count - fulls[delta]
        if partial > 0:
            far = slot * cols + (0 if delta < 0 else cols // 2)
            window[pl.ds(jnp.where(north, fulls[delta], rows - count) + 1, partial),
                   far : far + cols // 2] = jnp.zeros(
                (partial, cols // 2, channels), jnp.bfloat16
            )
    for delta in halves:
        far = (delta + middle) % lon_count * cols + (0 if delta < 0 else cols // 2)
        for line in (0, rows + 1):
            window[line, far : far + cols // 2] = jnp.zeros((cols // 2, channels), jnp.bfloat16)
    for present, line in ((has_low, 0), (has_high, rows + 1)):
        for delta in range(1 - middle, middle + 1):
            slot = (delta + middle) % lon_count

            def clear():
                window[line, slot * cols : (slot + 1) * cols] = jnp.zeros(
                    (cols, channels), jnp.bfloat16
                )

            if delta in halo and lat_count > 1:
                pl.when(jnp.logical_not(present))(clear)
            else:
                clear()

    lanes = lax.broadcasted_iota(jnp.int32, (rows, lon_total), 1)
    wide = (rows, rows_ref.shape[2])
    own_rows = (
        lax.broadcasted_iota(jnp.int32, wide, 0) + lat * rows
        == lax.broadcasted_iota(jnp.int32, wide, 1)
    ).astype(jnp.float32)

    def own(ref, k):
        return lax.dot_general(
            own_rows,
            ref[k].astype(jnp.float32),
            (((1,), (1,)), ((), ())),
            precision=lax.Precision.HIGHEST,
            preferred_element_type=jnp.float32,
        )

    def build(k, carry):
        spot = own(lons_ref, k).astype(jnp.int32) + middle * cols
        spot = jnp.where(spot >= lon_total, spot - lon_total, spot)
        row_offset = own(rows_ref, k)
        weight = own(weights_ref, k)
        picked = [jnp.where(row_offset == r, weight, 0.0) for r in (-1.0, 0.0, 1.0)]
        sums = [jnp.zeros((rows, lon_total), jnp.float32) for _ in range(3)]
        for s in range(entries):
            hit = spot[:, s : s + 1] == lanes
            for r in range(3):
                sums[r] = sums[r] + jnp.where(hit, picked[r][:, s : s + 1], 0.0)
        for r in range(3):
            for i in range(rows):
                line = jnp.broadcast_to(sums[r][i : i + 1, :], (cols, lon_total))
                turned = pltpu.roll(line, 0, 1, stride=1, stride_axis=0)
                filters[i, pl.ds(pl.multiple_of(k * cols, cols), cols),
                        r * lon_total : (r + 1) * lon_total] = turned.astype(jnp.bfloat16)
        return carry

    lax.fori_loop(0, bases, build, 0)

    def group(low, high):
        start = jnp.where(north, low, rows - high)
        half = high - low
        lines = half * cols
        def filter_row(t, carry):
            i = start + t
            source = window[pl.ds(i, 3)].reshape(3 * lon_total, channels)
            filtered = jnp.dot(filters[i], source, preferred_element_type=jnp.float32)
            filtered = filtered.astype(jnp.bfloat16)
            at = pl.multiple_of(t * cols, cols)
            for k in range(bases):
                product[pl.ds(at, cols), k * channels : (k + 1) * channels] = filtered[
                    k * cols : (k + 1) * cols
                ]
            return carry

        lax.fori_loop(0, half, filter_row, 0)
        mixed = jnp.dot(product[:lines], mix_ref[...], preferred_element_type=jnp.float32)
        here = x_ref[pl.ds(start, half)].reshape(lines, channels)
        latent = here.astype(jnp.float32) + mixed
        mean = jnp.mean(latent, axis=1, keepdims=True)
        centred = latent - mean
        variance = jnp.mean(centred * centred, axis=1, keepdims=True)
        normed = (centred * lax.rsqrt(variance + norm_eps) * gain_ref[...][None, :]).astype(jnp.bfloat16)
        raised = jnp.dot(normed, up_ref[...], preferred_element_type=jnp.float32)
        hidden = 0.5 * raised * (1.0 + lax.erf(raised * math.sqrt(0.5)))
        lowered = jnp.dot(
            hidden.astype(jnp.bfloat16), down_ref[...], preferred_element_type=jnp.float32
        )
        result = (latent + lowered).astype(jnp.bfloat16)
        out_ref[pl.ds(start, half)] = result.reshape(half, cols, channels)

    puts = []
    for stage, (low, high) in zip(copies, groups):
        each(stage, False, lambda copy: copy.wait_recv())
        if stage is copies[0]:
            for load in loads:
                load.wait()
        group(low, high)
        part = pl.ds(jnp.where(north, low, rows - high), high - low)
        put = pltpu.make_async_copy(out_ref.at[part], out_hbm.at[part], out_sem.at[len(puts)])
        put.start()
        puts.append(put)
    for stage in copies:
        each(stage, True, lambda copy: copy.wait_send())
    for put in puts:
        put.wait()


def source_reach(lon_total, row_total, p):
    row = max(p - 1, 0)
    return min(lon_total // 2, 4 * row_total // min(row + 1, row_total - row))


def fold_rows(lon_count, lat_count, rows, cols):
    lon_total, row_total = lon_count * cols, lat_count * rows
    fold = 2
    while source_reach(lon_total, row_total, fold + 1) > 2 * cols:
        fold += 2
    return fold


def relay_fits(lon_count, lat_count, rows, cols):
    lon_total, row_total = lon_count * cols, lat_count * rows
    if lon_count != 8 or lat_count != 2 or rows % 4 != 0 or cols != 16:
        return False
    near = source_reach(lon_total, row_total, rows // 2 + 1) <= cols
    return near and fold_rows(lon_count, lat_count, rows, cols) <= rows // 4


def relay_kernel(
    lon_count,
    lat_count,
    x_hbm,
    rows_ref,
    lons_ref,
    weights_ref,
    gain_ref,
    mix_hbm,
    up_hbm,
    down_hbm,
    out_ref,
    window,
    fold_filters,
    wide_filters,
    near_filters,
    product,
    mixed_ref,
    fold_out,
    fold_in,
    mix_ref,
    up_ref,
    down_ref,
    send_sem,
    recv_sem,
    load_sem,
    ready,
    tables,
):
    rows, cols, channels = x_hbm.shape
    bases, entries = rows_ref.shape[:2]
    lon_total, row_total = lon_count * cols, lat_count * rows
    middle, part, half = lon_count // 2, cols // 2, rows // 2
    home = middle * cols
    fold = fold_rows(lon_count, lat_count, rows, cols)
    reaches = [source_reach(lon_total, row_total, max(p, fold + 1)) for p in range(rows)]
    wide = sum(1 for r in reaches if r > cols + part)
    near = sum(1 for r in reaches if r > cols)
    me, lat = lax.axis_index("lon"), lax.axis_index("lat")
    north = lat == 0
    turn = 1 - 2 * lax.rem(me, 2)
    place = lax.rem(me, middle)
    inward = jnp.where(place < 2, 1, -1)
    edge = jnp.where(north, rows - 1, 0)

    def device(delta):
        return lax.rem(me + delta + lon_count, lon_count)

    def at(delta):
        return pl.multiple_of(lax.rem(delta + middle + lon_count, lon_count) * cols, cols)

    def lines(first, last):
        return pl.ds(jnp.where(north, first, rows - last) + 1, last - first)

    fetch = pltpu.make_async_copy(
        x_hbm, window.at[pl.ds(1, rows), pl.ds(home, cols)], load_sem.at[3]
    )
    fetch.start()
    loads = [
        pltpu.make_async_copy(mix_hbm, mix_ref, load_sem.at[0]),
        pltpu.make_async_copy(up_hbm, up_ref, load_sem.at[1]),
        pltpu.make_async_copy(down_hbm, down_ref, load_sem.at[2]),
    ]
    barrier = pltpu.get_barrier_semaphore()
    above, below = me < lon_count - 2, me >= 2
    inner = jnp.logical_and(above, below)
    outer = jnp.logical_not(inner)

    def greet(semaphore, **other):
        pl.semaphore_signal(semaphore, inc=1, device_id=other, device_id_type=MESH)

    greet(barrier, lon=me + turn)
    greet(barrier, lat=1 - lat)

    @pl.when(above)
    def _():
        greet(barrier, lon=me + 2)

    @pl.when(below)
    def _():
        greet(barrier, lon=me - 2)

    for load in loads:
        load.start()

    def clear(where, low, high):
        size = where.size if isinstance(where, pl.Slice) else 1
        window[where, low:high] = jnp.zeros((size, high - low, channels), jnp.bfloat16)

    near_cut = half + (rows - half) // 2
    sky, halo = jnp.where(north, 0, rows + 1), jnp.where(north, rows + 1, 0)
    clear(pl.ds(sky, 1), 0, lon_total)
    clear(lines(fold + 1, wide), 0, home - 2 * cols)
    clear(lines(fold + 1, wide), home + 3 * cols, lon_total)
    clear(lines(fold - 1, fold + 1), 0, cols)

    @pl.when(place != middle - 1)
    def _():
        clear(lines(fold - 1, fold + 1), cols, 2 * cols)

    @pl.when(place != 0)
    def _():
        clear(lines(fold - 1, fold + 1), home + 3 * cols, lon_total)

    clear(lines(wide, near), 0, home - cols - part)
    clear(lines(wide, near), home + 2 * cols + part, lon_total)
    clear(lines(near, half + 1), 0, home - cols)
    clear(lines(near, half + 1), home + 2 * cols, lon_total)
    clear(lines(half + 1, near_cut), home + 2 * cols, home + 3 * cols)

    @pl.when(turn < 0)
    def _():
        clear(lines(near_cut, rows), home + 2 * cols, home + 3 * cols)

    clear(pl.ds(halo, 1), home - cols, home - part)
    clear(pl.ds(halo, 1), home + cols + part, home + 3 * cols)

    span = (rows, rows_ref.shape[2])
    order = lax.broadcasted_iota(jnp.int32, span, 0)
    local = jnp.where(north, order, rows - 2 - order + 2 * lax.rem(order, 2))
    mine = (local + lat * rows == lax.broadcasted_iota(jnp.int32, span, 1)).astype(jnp.float32)
    for which, ref in enumerate((rows_ref, lons_ref, weights_ref)):
        own = lax.dot_general(
            mine,
            ref[...].astype(jnp.float32).reshape(bases * entries, rows_ref.shape[2]),
            (((1,), (1,)), ((), ())),
            precision=lax.Precision.HIGHEST,
            preferred_element_type=jnp.float32,
        )
        for k in range(bases):
            tables[which, k] = own[:, k * entries : (k + 1) * entries]

    count = [0]

    def message(where, here, there, width, target, landing=None):
        index = count[0]
        count[0] += 1
        landing = where if landing is None else landing
        return pltpu.make_async_remote_copy(
            src_ref=window.at[where, pl.ds(here, width)],
            dst_ref=window.at[landing, pl.ds(there, width)],
            send_sem=send_sem.at[index],
            recv_sem=recv_sem.at[index],
            device_id=target,
            device_id_type=MESH,
        )

    partner, beside = {"lon": me + turn}, {"lon": device(2 * turn)}
    core, core_line = {"lat": 1 - lat}, pl.ds(edge + 1, 1)
    core_landing = pl.ds(jnp.where(north, 0, rows + 1), 1)

    def own_across(first, last):
        return message(lines(first, last), home, at(-turn), cols, partner)

    def own_along(first, last, e):
        return message(lines(first, last), home, at(-2 * e), cols, {"lon": device(2 * e)})

    def half_along(first, last, e):
        offset = part if e > 0 else 0
        return message(
            lines(first, last), home + offset, at(-2 * e) + offset, part, {"lon": device(2 * e)}
        )

    def pass_along(first, last):
        return message(lines(first, last), at(turn), at(-turn), cols, beside)

    def pass_across(first, last, e):
        return message(lines(first, last), at(2 * e), at(2 * e - turn), cols, partner)

    def to_core(col, width):
        return message(core_line, col, col, width, core, core_landing)

    after = pl.multiple_of(home + jnp.where(turn > 0, cols, -part), part)
    before = pl.multiple_of(home + jnp.where(turn > 0, -part, cols), part)
    halo_own = to_core(home, cols)
    halo_across, halo_along = to_core(after, part), to_core(before, part)
    across = [own_across(near_cut, rows), own_across(wide, near_cut)]
    along = pass_along(wide, near_cut)
    direct = own_along(near_cut, rows, -turn)
    direct_across = pass_across(near_cut, rows, turn)
    halves = [half_along(wide, near, e) for e in (1, -1)]
    fold_own = own_across(0, wide)
    along_in, along_out = own_along(0, wide, inward), own_along(fold - 1, wide, -inward)
    fold_across = pass_across(0, fold + 1, inward)
    same = turn == inward
    late_across = pass_across(fold + 1, wide, turn), pass_across(fold - 1, wide, turn)
    index = count[0]
    fold_swap = pltpu.make_async_remote_copy(
        src_ref=fold_out,
        dst_ref=fold_in,
        send_sem=send_sem.at[index],
        recv_sem=recv_sem.at[index],
        device_id={"lon": device(middle)},
        device_id_type=MESH,
    )

    def start(*copies):
        for copy in copies:
            copy.start()

    def arrived(*copies):
        for copy in copies:
            copy.wait_recv()

    lanes = lax.broadcasted_iota(jnp.int32, (half, lon_total), 1)
    second = lax.rem(lax.broadcasted_iota(jnp.int32, (half, entries), 0), 2)

    def turned(line, shift):
        spread = jnp.broadcast_to(line, (cols, lon_total))
        return pltpu.roll(spread, shift, 1, stride=1, stride_axis=0)

    def build_near(k, carry):
        offset = tables[1, k, half:].astype(jnp.int32)
        row_offset = tables[0, k, half:].astype(jnp.int32)
        weight = tables[2, k, half:]
        spot = (row_offset + 1 + second) * (4 * cols) + offset + cols
        sums = [jnp.zeros((half, lon_total), jnp.float32) for _ in range(2)]
        for s in range(entries):
            for v in range(2):
                hit = spot[:, s : s + 1] == lanes + v * lon_total
                sums[v] = sums[v] + jnp.where(hit, weight[:, s : s + 1], 0.0)
        for n in range(half):
            for v in range(2):
                spot_at = pl.multiple_of(k * 2 * cols + (n % 2) * cols, cols)
                near_filters[n // 2, pl.ds(spot_at, cols), v * lon_total : (v + 1) * lon_total] = (
                    turned(sums[v][n : n + 1, :], 0).astype(jnp.bfloat16)
                )
        return carry

    polar = lax.broadcasted_iota(jnp.int32, (half, entries), 0) < fold
    start_col = jnp.where(polar, place * cols, home)
    lower = lax.broadcasted_iota(jnp.int32, (cols, lon_total), 1) < home

    def build_polar(k, carry):
        spot = tables[1, k, :half].astype(jnp.int32) + start_col
        spot = jnp.where(spot >= lon_total, spot - lon_total, spot)
        spot = jnp.where(spot < 0, spot + lon_total, spot)
        row_offset = tables[0, k, :half]
        weight = tables[2, k, :half]
        picked = [jnp.where(row_offset == r, weight, 0.0) for r in (-1.0, 0.0, 1.0)]
        sums = [jnp.zeros((half, lon_total), jnp.float32) for _ in range(3)]
        for s in range(entries):
            hit = spot[:, s : s + 1] == lanes
            for r in range(3):
                sums[r] = sums[r] + jnp.where(hit, picked[r][:, s : s + 1], 0.0)
        none = jnp.zeros((cols, lon_total), jnp.float32)
        for n in range(fold):
            late = n % 2
            kept = [none] * 4
            moved = [none] * 4
            for r in range(3):
                kept[r + late] = turned(sums[r][n : n + 1, :], 0)
                moved[r + late] = turned(sums[r][n : n + 1, :], home)
            for v in range(2):
                here = jnp.where(lower, kept[2 * v], moved[2 * v + 1])
                there = jnp.where(lower, moved[2 * v], kept[2 * v + 1])
                for who, value in enumerate((here, there)):
                    spot_at = pl.multiple_of(k * 4 * cols + (2 * who + late) * cols, cols)
                    fold_filters[
                        n // 2, pl.ds(spot_at, cols), v * lon_total : (v + 1) * lon_total
                    ] = value.astype(jnp.bfloat16)
        for n in range(fold, half):
            late = n % 2
            spot_at = pl.ds(pl.multiple_of(k * 2 * cols + late * cols, cols), cols)
            for r in range(3):
                low = (r + late) * lon_total
                wide_filters[(n - fold) // 2, spot_at, low : low + lon_total] = turned(
                    sums[r][n : n + 1, :], 0
                ).astype(jnp.bfloat16)
            low = (3 - 3 * late) * lon_total
            wide_filters[(n - fold) // 2, spot_at, low : low + lon_total] = none.astype(jnp.bfloat16)
        return carry

    def filter_pairs(first, last):
        pairs = last - first
        base = jnp.where(north, 2 * first, rows - 2 * last)
        for t in range(pairs):
            q = jnp.where(north, first + t, last - 1 - t)
            taken = pl.ds(base + 2 * t, 4)
            if 2 * first >= half:
                low = home - cols
                source = window[taken, low : low + 4 * cols].reshape(16 * cols, channels)
                matrix = near_filters[q - half // 2]
            else:
                source = window[taken].reshape(4 * lon_total, channels)
                matrix = wide_filters[q - fold // 2]
            filtered = jnp.dot(matrix, source, preferred_element_type=jnp.float32)
            filtered = filtered.astype(jnp.bfloat16)
            for k in range(bases):
                product[2 * t * cols : 2 * (t + 1) * cols, k * channels : (k + 1) * channels] = (
                    filtered[2 * k * cols : 2 * (k + 1) * cols]
                )

    def fold_pairs():
        pairs = fold // 2
        cells = fold * cols
        base = jnp.where(north, 0, rows - fold)
        for t in range(pairs):
            q = jnp.where(north, t, pairs - 1 - t)
            source = window[pl.ds(base + 2 * t, 4), pl.ds(at(-place), 4 * cols)]
            source = source.reshape(16 * cols, channels)
            filtered = jnp.dot(fold_filters[q], source, preferred_element_type=jnp.float32)
            filtered = filtered.astype(jnp.bfloat16)
            for k in range(bases):
                for who in range(2):
                    low, from_row = who * cells + 2 * t * cols, (4 * k + 2 * who) * cols
                    product[low : low + 2 * cols, k * channels : (k + 1) * channels] = filtered[
                        from_row : from_row + 2 * cols
                    ]
        mixed = jnp.dot(product[: 2 * cells], mix_ref[...], preferred_element_type=jnp.float32)
        fold_out[...] = mixed[cells:].astype(jnp.bfloat16)
        mixed_ref[pl.ds(jnp.where(north, 0, half * cols - cells), cells)] = mixed[:cells]

    def mix_pairs(pairs):
        cells = 2 * pairs * cols
        return jnp.dot(product[:cells], mix_ref[...], preferred_element_type=jnp.float32)

    def finish(mixed, base, depth):
        cells = depth * cols
        here = window[pl.ds(base + 1, depth), home : home + cols].reshape(cells, channels)
        latent = here.astype(jnp.float32) + mixed
        mean = jnp.mean(latent, axis=1, keepdims=True)
        centred = latent - mean
        variance = jnp.mean(centred * centred, axis=1, keepdims=True)
        normed = (centred * lax.rsqrt(variance + norm_eps) * gain_ref[...][None, :]).astype(
            jnp.bfloat16
        )
        raised = jnp.dot(normed, up_ref[...], preferred_element_type=jnp.float32)
        hidden = 0.5 * raised * (1.0 + lax.erf(raised * math.sqrt(0.5)))
        lowered = jnp.dot(
            hidden.astype(jnp.bfloat16), down_ref[...], preferred_element_type=jnp.float32
        )
        result = (latent + lowered).astype(jnp.bfloat16)
        out_ref[pl.ds(base, depth)] = result.reshape(depth, cols, channels)

    fold_pair, half_pair, all_pairs = fold // 2, half // 2, rows // 2
    pl.semaphore_wait(barrier, 2 + jnp.where(above, 1, 0) + jnp.where(below, 1, 0))

    @pl.when(inner)
    def _():
        greet(ready.at[0], lon=me + 2)
        greet(ready.at[0], lon=me - 2)

    fetch.wait()
    start(halo_own, fold_own, along_in, across[1])
    goes_near = jnp.logical_or(inner, jnp.logical_not(same))

    @pl.when(goes_near)
    def _():
        start(direct)

    @pl.when(inner)
    def _():
        start(along_out)

    lax.fori_loop(0, bases // 2, build_near, 0)
    pl.semaphore_wait(ready.at[0], 1)

    @pl.when(inner)
    def _():
        greet(ready.at[1], lon=device(2 * inward))

    lax.fori_loop(bases // 2, bases, build_near, 0)
    lax.fori_loop(0, bases // 2, build_polar, 0)

    @pl.when(outer)
    def _():
        pl.semaphore_wait(ready.at[1], 1)

        @pl.when(same)
        def _():
            start(direct)

        start(along_out)

    start(*halves)
    lax.fori_loop(bases // 2, bases, build_polar, 0)
    arrived(along_in)
    start(fold_across, across[0])
    arrived(across[1])
    start(along)
    arrived(direct)
    start(direct_across)
    for load in loads:
        load.wait()
    arrived(fold_own, fold_across)
    fold_pairs()
    arrived(along_out)

    @pl.when(same)
    def _():
        start(late_across[0])

    @pl.when(jnp.logical_not(same))
    def _():
        start(late_across[1])

    start(fold_swap)
    arrived(across[0])
    start(halo_across)
    arrived(direct_across)
    start(halo_along)
    arrived(halo_own, halo_across, halo_along, along, *halves)
    filter_pairs(half_pair, all_pairs)
    finish(mix_pairs(all_pairs - half_pair), jnp.where(north, half, 0), rows - half)

    @pl.when(same)
    def _():
        arrived(late_across[1])

    @pl.when(jnp.logical_not(same))
    def _():
        arrived(late_across[0])

    filter_pairs(fold_pair, half_pair)
    cells = (half - fold) * cols
    mixed_ref[pl.ds(jnp.where(north, fold * cols, 0), cells)] = mix_pairs(half_pair - fold_pair)
    arrived(fold_swap)
    own_part = pl.ds(jnp.where(north, 0, half * cols - fold * cols), fold * cols)
    mixed_ref[own_part] = mixed_ref[own_part] + fold_in[...].astype(jnp.float32)
    finish(mixed_ref[...], jnp.where(north, 0, half), half)

    @pl.when(same)
    def _():
        late_across[0].wait_send()

    @pl.when(jnp.logical_not(same))
    def _():
        late_across[1].wait_send()

    sent = [halo_own, halo_across, halo_along, fold_own, fold_across, along_in, along_out]
    sent += [along, direct, direct_across, fold_swap]
    for copy in sent + across + halves:
        copy.wait_send()


def relay_call(
    lon_count,
    lat_count,
    fields,
    support_rows,
    support_lons,
    support_weights,
    mix_weight,
    norm_gain,
    up_weight,
    down_weight,
):
    channels, rows, cols = fields.shape
    bases, hidden = mix_weight.shape[0], up_weight.shape[1]
    lon_total = lon_count * cols
    half, copies = rows // 2, 20
    fold = fold_rows(lon_count, lat_count, rows, cols)
    in_vmem = pl.BlockSpec(memory_space=pltpu.VMEM)
    anywhere = pl.BlockSpec(memory_space=pl.ANY)
    result = pl.pallas_call(
        functools.partial(relay_kernel, lon_count, lat_count),
        out_shape=pltpu.VMEM((rows, cols, channels), jnp.bfloat16),
        in_specs=[anywhere] + [in_vmem] * 4 + [anywhere] * 3,
        out_specs=in_vmem,
        scratch_shapes=[
            pltpu.VMEM((rows + 2, lon_total, channels), jnp.bfloat16),
            pltpu.VMEM((fold // 2, 4 * bases * cols, 16 * cols), jnp.bfloat16),
            pltpu.VMEM(((half - fold) // 2, 2 * bases * cols, 4 * lon_total), jnp.bfloat16),
            pltpu.VMEM((half // 2, 2 * bases * cols, 16 * cols), jnp.bfloat16),
            pltpu.VMEM((half * cols, bases * channels), jnp.bfloat16),
            pltpu.VMEM((half * cols, channels), jnp.float32),
            pltpu.VMEM((fold * cols, channels), jnp.bfloat16),
            pltpu.VMEM((fold * cols, channels), jnp.bfloat16),
            pltpu.VMEM((bases * channels, channels), jnp.bfloat16),
            pltpu.VMEM((channels, hidden), jnp.bfloat16),
            pltpu.VMEM((hidden, channels), jnp.bfloat16),
            pltpu.SemaphoreType.DMA((copies,)),
            pltpu.SemaphoreType.DMA((copies,)),
            pltpu.SemaphoreType.DMA((4,)),
            pltpu.SemaphoreType.REGULAR((2,)),
            pltpu.VMEM((3, bases, rows, support_rows.shape[2]), jnp.float32),
        ],
        compiler_params=pltpu.CompilerParams(
            collective_id=0, has_side_effects=True, vmem_limit_bytes=56 * 1024 * 1024
        ),
    )(
        jnp.transpose(fields, (1, 2, 0)),
        jnp.transpose(support_rows, (0, 2, 1)),
        jnp.transpose(support_lons, (0, 2, 1)),
        jnp.transpose(support_weights, (0, 2, 1)),
        norm_gain,
        mix_weight.reshape(bases * channels, channels),
        up_weight,
        down_weight,
    )
    return jnp.transpose(result, (2, 0, 1))


def direct_call(
    lon_count,
    lat_count,
    fields,
    support_rows,
    support_lons,
    support_weights,
    mix_weight,
    norm_gain,
    up_weight,
    down_weight,
):
    channels, rows, cols = fields.shape
    bases, hidden = mix_weight.shape[0], up_weight.shape[1]
    lon_total = lon_count * cols
    plan = plan_copies(lon_count, lat_count, rows, cols)
    count = sum(len(stage) for stage in plan[1])
    in_vmem = pl.BlockSpec(memory_space=pltpu.VMEM)
    anywhere = pl.BlockSpec(memory_space=pl.ANY)
    result = pl.pallas_call(
        functools.partial(block_kernel, lon_count, lat_count, plan),
        out_shape=jax.ShapeDtypeStruct((rows, cols, channels), jnp.bfloat16),
        in_specs=[anywhere] + [in_vmem] * 4 + [anywhere] * 3,
        out_specs=anywhere,
        scratch_shapes=[
            pltpu.VMEM((rows, cols, channels), jnp.bfloat16),
            pltpu.VMEM((rows, cols, channels), jnp.bfloat16),
            pltpu.VMEM((rows + 2, lon_total, channels), jnp.bfloat16),
            pltpu.VMEM((rows, bases * cols, 3 * lon_total), jnp.bfloat16),
            pltpu.VMEM((rows // 2 * cols, bases * channels), jnp.bfloat16),
            pltpu.VMEM((bases * channels, channels), jnp.bfloat16),
            pltpu.VMEM((channels, hidden), jnp.bfloat16),
            pltpu.VMEM((hidden, channels), jnp.bfloat16),
            pltpu.SemaphoreType.DMA((count,)),
            pltpu.SemaphoreType.DMA((count,)),
            pltpu.SemaphoreType.DMA((4,)),
            pltpu.SemaphoreType.DMA((len(plan[0]),)),
        ],
        compiler_params=pltpu.CompilerParams(
            collective_id=0, has_side_effects=True, vmem_limit_bytes=56 * 1024 * 1024
        ),
    )(
        jnp.transpose(fields, (1, 2, 0)),
        jnp.transpose(support_rows, (0, 2, 1)),
        jnp.transpose(support_lons, (0, 2, 1)),
        jnp.transpose(support_weights, (0, 2, 1)),
        norm_gain,
        mix_weight.reshape(bases * channels, channels),
        up_weight,
        down_weight,
    )
    return jnp.transpose(result, (2, 0, 1))


def on_device(lon_count, lat_count, *arrays):
    channels, rows, cols = arrays[0].shape
    if relay_fits(lon_count, lat_count, rows, cols):
        return relay_call(lon_count, lat_count, *arrays)
    return direct_call(lon_count, lat_count, *arrays)


def solution(mesh):
    in_specs = (P("member", "lat", "lon"), P(), P(), P(), P(), P(), P(), P())
    out_specs = P("member", "lat", "lon")
    return jax.shard_map(
        functools.partial(on_device, mesh.shape["lon"], mesh.shape["lat"]),
        mesh=mesh,
        in_specs=in_specs,
        out_specs=out_specs,
        check_vma=False,
    )
```

```python
import functools
import math

import jax
import jax.numpy as jnp
from jax import lax
from jax.experimental import pallas as pl
from jax.experimental.pallas import tpu as pltpu
from jax.sharding import PartitionSpec as P

norm_eps = 1e-05
MESH = pl.DeviceIdType.MESH


def plan_copies(lon_count, lat_count, rows, cols):
    lon_total, row_total = lon_count * cols, lat_count * rows

    def reach(row):
        nearest = min(row + 1, row_total - row)
        return min(lon_total // 2, 4 * row_total // nearest)

    def distance(row):
        return min(-(-reach(row) // cols), lon_count // 2)

    def in_half(span, delta):
        if delta == 0 or abs(delta) == lon_count // 2:
            return False
        return span - cols * (abs(delta) - 1) <= cols // 2

    need = [distance(max(p - 1, 0)) for p in range(rows)]
    deltas = [d for d in range(1 - lon_count // 2, lon_count // 2 + 1) if d != 0]
    counts = {delta: sum(1 for d in need if d >= abs(delta)) for delta in deltas}
    spans = [reach(max(p - 1, 0)) for p in range(rows)]
    fulls = {d: sum(1 for p in range(counts[d]) if not in_half(spans[p], d)) for d in deltas}
    edge, edge_span = 0, 0
    for boundary in range(1, lat_count):
        edge = max(edge, distance(boundary * rows - 1), distance(boundary * rows))
        edge_span = max(edge_span, reach(boundary * rows - 1), reach(boundary * rows))
    halo = [d for d in range(1 - lon_count // 2, lon_count // 2 + 1) if abs(d) <= edge]
    groups = [(rows // 2, rows), (rows // 4, rows // 2), (0, rows // 4)]
    stages = []
    upper = rows
    for low, _ in groups:
        lower = max(low - 1, 0)
        stage = []
        for delta in sorted(deltas, key=lambda d: -abs(d)):
            full, top = min(fulls[delta], upper), min(counts[delta], upper)
            if full > lower:
                stage.append(("block", delta, lower, full, False))
            if top > max(full, lower):
                stage.append(("block", delta, max(full, lower), top, True))
        stages.append(stage)
        upper = lower
    if lat_count > 1:
        stages[0] = [
            (side, d, 0, 1, in_half(edge_span, d)) for d in halo for side in ("down", "up")
        ] + stages[0]
    halves = [d for d in halo if in_half(edge_span, d)]
    return groups, stages, counts, fulls, halo, halves


def block_kernel(
    lon_count,
    lat_count,
    plan,
    x_hbm,
    rows_ref,
    lons_ref,
    weights_ref,
    gain_ref,
    mix_hbm,
    up_hbm,
    down_hbm,
    out_hbm,
    x_ref,
    out_ref,
    window,
    filters,
    product,
    mix_ref,
    up_ref,
    down_ref,
    send_sem,
    recv_sem,
    load_sem,
    out_sem,
):
    rows, cols, channels = x_ref.shape
    bases, entries = rows_ref.shape[:2]
    lon_total = lon_count * cols
    middle = lon_count // 2
    groups, stages, counts, fulls, halo, halves = plan
    me, lat = lax.axis_index("lon"), lax.axis_index("lat")
    north = 2 * lat < lat_count
    has_low, has_high = lat > 0, lat < lat_count - 1

    loads = [
        pltpu.make_async_copy(mix_hbm, mix_ref, load_sem.at[0]),
        pltpu.make_async_copy(up_hbm, up_ref, load_sem.at[1]),
        pltpu.make_async_copy(down_hbm, down_ref, load_sem.at[2]),
    ]
    fetch = pltpu.make_async_copy(x_hbm, x_ref, load_sem.at[3])
    fetch.start()

    barrier = pltpu.get_barrier_semaphore()
    halo_deltas = halo if lat_count > 1 else []
    for delta in range(1, lon_count):
        pl.semaphore_signal(
            barrier, inc=1, device_id={"lon": lax.rem(me + delta, lon_count)}, device_id_type=MESH
        )
    for present, other in ((has_low, lat - 1), (has_high, lat + 1)):

        @pl.when(present)
        def _():
            for delta in halo_deltas:
                target = lax.rem(me + lon_count - delta, lon_count)
                pl.semaphore_signal(
                    barrier, inc=1, device_id={"lon": target, "lat": other}, device_id_type=MESH
                )

    sides = jnp.where(has_low, 1, 0) + jnp.where(has_high, 1, 0)
    pl.semaphore_wait(barrier, lon_count - 1 + sides * len(halo_deltas))
    fetch.wait()

    def copy_of(index, item):
        kind, delta, first, last, halved = item
        width = cols // 2 if halved else cols
        offset = cols // 2 if halved and delta < 0 else 0
        target = lax.rem(me + lon_count - delta, lon_count)
        slot = (delta + middle) % lon_count
        here, there = pl.ds(offset, width), pl.ds(slot * cols + offset, width)
        if kind == "block":
            start = jnp.where(north, first, rows - last)
            source = x_ref.at[pl.ds(start, last - first), here]
            landing = window.at[pl.ds(start + 1, last - first), there]
            device = {"lon": target}
        elif kind == "down":
            source = x_ref.at[pl.ds(rows - 1, 1), here]
            landing = window.at[pl.ds(0, 1), there]
            device = {"lon": target, "lat": jnp.minimum(lat + 1, lat_count - 1)}
        else:
            source = x_ref.at[pl.ds(0, 1), here]
            landing = window.at[pl.ds(rows + 1, 1), there]
            device = {"lon": target, "lat": jnp.maximum(lat - 1, 0)}
        return pltpu.make_async_remote_copy(
            src_ref=source,
            dst_ref=landing,
            send_sem=send_sem.at[index],
            recv_sem=recv_sem.at[index],
            device_id=device,
            device_id_type=MESH,
        )

    copies = []
    for stage in stages:
        copies.append(list(enumerate(stage, sum(len(done) for done in copies))))

    def each(items, sending, action):
        for index, item in items:
            if item[0] == "block":
                action(copy_of(index, item))
            else:
                present = has_high if (item[0] == "down") == sending else has_low

                @pl.when(present)
                def _():
                    action(copy_of(index, item))

    for stage in copies:
        each(stage, True, lambda copy: copy.start())
    for load in loads:
        load.start()

    window[1 : rows + 1, middle * cols : (middle + 1) * cols, :] = x_ref[...]
    for delta, count in counts.items():
        slot = (delta + middle) % lon_count
        if count < rows:
            gap = (rows - count, cols, channels)
            window[pl.ds(jnp.where(north, count, 0) + 1, rows - count),
                   slot * cols : (slot + 1) * cols] = jnp.zeros(gap, jnp.bfloat16)
        partial = count - fulls[delta]
        if partial > 0:
            far = slot * cols + (0 if delta < 0 else cols // 2)
            window[pl.ds(jnp.where(north, fulls[delta], rows - count) + 1, partial),
                   far : far + cols // 2] = jnp.zeros(
                (partial, cols // 2, channels), jnp.bfloat16
            )
    for delta in halves:
        far = (delta + middle) % lon_count * cols + (0 if delta < 0 else cols // 2)
        for line in (0, rows + 1):
            window[line, far : far + cols // 2] = jnp.zeros((cols // 2, channels), jnp.bfloat16)
    for present, line in ((has_low, 0), (has_high, rows + 1)):
        for delta in range(1 - middle, middle + 1):
            slot = (delta + middle) % lon_count

            def clear():
                window[line, slot * cols : (slot + 1) * cols] = jnp.zeros(
                    (cols, channels), jnp.bfloat16
                )

            if delta in halo and lat_count > 1:
                pl.when(jnp.logical_not(present))(clear)
            else:
                clear()

    lanes = lax.broadcasted_iota(jnp.int32, (rows, lon_total), 1)
    wide = (rows, rows_ref.shape[2])
    own_rows = (
        lax.broadcasted_iota(jnp.int32, wide, 0) + lat * rows
        == lax.broadcasted_iota(jnp.int32, wide, 1)
    ).astype(jnp.float32)

    def own(ref, k):
        return lax.dot_general(
            own_rows,
            ref[k].astype(jnp.float32),
            (((1,), (1,)), ((), ())),
            precision=lax.Precision.HIGHEST,
            preferred_element_type=jnp.float32,
        )

    def build(k, carry):
        spot = own(lons_ref, k).astype(jnp.int32) + middle * cols
        spot = jnp.where(spot >= lon_total, spot - lon_total, spot)
        row_offset = own(rows_ref, k)
        weight = own(weights_ref, k)
        picked = [jnp.where(row_offset == r, weight, 0.0) for r in (-1.0, 0.0, 1.0)]
        sums = [jnp.zeros((rows, lon_total), jnp.float32) for _ in range(3)]
        for s in range(entries):
            hit = spot[:, s : s + 1] == lanes
            for r in range(3):
                sums[r] = sums[r] + jnp.where(hit, picked[r][:, s : s + 1], 0.0)
        for r in range(3):
            for i in range(rows):
                line = jnp.broadcast_to(sums[r][i : i + 1, :], (cols, lon_total))
                turned = pltpu.roll(line, 0, 1, stride=1, stride_axis=0)
                filters[i, pl.ds(pl.multiple_of(k * cols, cols), cols),
                        r * lon_total : (r + 1) * lon_total] = turned.astype(jnp.bfloat16)
        return carry

    lax.fori_loop(0, bases, build, 0)

    def group(low, high):
        start = jnp.where(north, low, rows - high)
        half = high - low
        lines = half * cols
        def filter_row(t, carry):
            i = start + t
            source = window[pl.ds(i, 3)].reshape(3 * lon_total, channels)
            filtered = jnp.dot(filters[i], source, preferred_element_type=jnp.float32)
            filtered = filtered.astype(jnp.bfloat16)
            at = pl.multiple_of(t * cols, cols)
            for k in range(bases):
                product[pl.ds(at, cols), k * channels : (k + 1) * channels] = filtered[
                    k * cols : (k + 1) * cols
                ]
            return carry

        lax.fori_loop(0, half, filter_row, 0)
        mixed = jnp.dot(product[:lines], mix_ref[...], preferred_element_type=jnp.float32)
        here = x_ref[pl.ds(start, half)].reshape(lines, channels)
        latent = here.astype(jnp.float32) + mixed
        mean = jnp.mean(latent, axis=1, keepdims=True)
        centred = latent - mean
        variance = jnp.mean(centred * centred, axis=1, keepdims=True)
        normed = (centred * lax.rsqrt(variance + norm_eps) * gain_ref[...][None, :]).astype(jnp.bfloat16)
        raised = jnp.dot(normed, up_ref[...], preferred_element_type=jnp.float32)
        hidden = 0.5 * raised * (1.0 + lax.erf(raised * math.sqrt(0.5)))
        lowered = jnp.dot(
            hidden.astype(jnp.bfloat16), down_ref[...], preferred_element_type=jnp.float32
        )
        result = (latent + lowered).astype(jnp.bfloat16)
        out_ref[pl.ds(start, half)] = result.reshape(half, cols, channels)

    puts = []
    for stage, (low, high) in zip(copies, groups):
        each(stage, False, lambda copy: copy.wait_recv())
        if stage is copies[0]:
            for load in loads:
                load.wait()
        group(low, high)
        part = pl.ds(jnp.where(north, low, rows - high), high - low)
        put = pltpu.make_async_copy(out_ref.at[part], out_hbm.at[part], out_sem.at[len(puts)])
        put.start()
        puts.append(put)
    for stage in copies:
        each(stage, True, lambda copy: copy.wait_send())
    for put in puts:
        put.wait()


def source_reach(lon_total, row_total, p):
    row = max(p - 1, 0)
    return min(lon_total // 2, 4 * row_total // min(row + 1, row_total - row))


def fold_rows(lon_count, lat_count, rows, cols):
    lon_total, row_total = lon_count * cols, lat_count * rows
    fold = 2
    while source_reach(lon_total, row_total, fold + 1) > 2 * cols:
        fold += 2
    return fold


def relay_fits(lon_count, lat_count, rows, cols):
    lon_total, row_total = lon_count * cols, lat_count * rows
    if lon_count != 8 or lat_count != 2 or rows % 4 != 0 or cols != 16:
        return False
    near = source_reach(lon_total, row_total, rows // 2 + 1) <= cols
    return near and fold_rows(lon_count, lat_count, rows, cols) <= rows // 4


def relay_kernel(
    lon_count,
    lat_count,
    x_hbm,
    rows_hbm,
    lons_hbm,
    weights_hbm,
    gain_hbm,
    mix_hbm,
    up_hbm,
    down_hbm,
    out_ref,
    window,
    fold_filters,
    wide_filters,
    near_filters,
    product,
    mixed_ref,
    fold_out_a,
    fold_out_b,
    fold_in_a,
    fold_in_b,
    mix_ref,
    up_ref,
    down_ref,
    send_sem,
    recv_sem,
    load_sem,
    ready,
    tables,
    rows_ref,
    lons_ref,
    weights_ref,
    gain_ref,
):
    rows, cols, channels = x_hbm.shape
    bases, entries = rows_ref.shape[:2]
    lon_total, row_total = lon_count * cols, lat_count * rows
    middle, part, half = lon_count // 2, cols // 2, rows // 2
    home = middle * cols
    fold = fold_rows(lon_count, lat_count, rows, cols)
    reaches = [source_reach(lon_total, row_total, max(p, fold + 1)) for p in range(rows)]
    wide = sum(1 for r in reaches if r > cols + part)
    near = sum(1 for r in reaches if r > cols)
    me, lat = lax.axis_index("lon"), lax.axis_index("lat")
    north = lat == 0
    turn = 1 - 2 * lax.rem(me, 2)
    place = lax.rem(me, middle)
    inward = jnp.where(place < 2, 1, -1)
    edge = jnp.where(north, rows - 1, 0)

    def device(delta):
        return lax.rem(me + delta + lon_count, lon_count)

    def at(delta):
        return pl.multiple_of(lax.rem(delta + middle + lon_count, lon_count) * cols, cols)

    def lines(first, last):
        return pl.ds(jnp.where(north, first, rows - last) + 1, last - first)

    fetch = pltpu.make_async_copy(
        x_hbm, window.at[pl.ds(1, rows), pl.ds(home, cols)], load_sem.at[3]
    )
    loads = [
        pltpu.make_async_copy(mix_hbm, mix_ref, load_sem.at[0]),
        pltpu.make_async_copy(up_hbm, up_ref, load_sem.at[1]),
        pltpu.make_async_copy(down_hbm, down_ref, load_sem.at[2]),
    ]
    supports = [
        pltpu.make_async_copy(source, landing, load_sem.at[4 + n])
        for n, (source, landing) in enumerate(
            [(rows_hbm, rows_ref), (lons_hbm, lons_ref), (weights_hbm, weights_ref)]
        )
    ]
    loads.append(pltpu.make_async_copy(gain_hbm, gain_ref, load_sem.at[7]))
    barrier = pltpu.get_barrier_semaphore()
    above, below = me < lon_count - 2, me >= 2
    inner = jnp.logical_and(above, below)
    outer = jnp.logical_not(inner)

    def greet(semaphore, **other):
        pl.semaphore_signal(semaphore, inc=1, device_id=other, device_id_type=MESH)

    greet(barrier, lon=me + turn)
    greet(barrier, lat=1 - lat)

    @pl.when(above)
    def _():
        greet(barrier, lon=me + 2)

    @pl.when(below)
    def _():
        greet(barrier, lon=me - 2)

    for load in [fetch] + supports + loads:
        load.start()

    def clear(where, low, high):
        size = where.size if isinstance(where, pl.Slice) else 1
        window[where, low:high] = jnp.zeros((size, high - low, channels), jnp.bfloat16)

    near_cut, last = half + (rows - half) // 2 - 1, rows - 1
    sky, halo = jnp.where(north, 0, rows + 1), jnp.where(north, rows + 1, 0)
    clear(pl.ds(sky, 1), 0, lon_total)
    clear(lines(fold + 1, wide), 0, home - 2 * cols)
    clear(lines(fold + 1, wide), home + 3 * cols, lon_total)
    clear(lines(fold - 1, fold + 1), 0, cols)

    @pl.when(place != middle - 1)
    def _():
        clear(lines(fold - 1, fold + 1), cols, 2 * cols)

    @pl.when(place != 0)
    def _():
        clear(lines(fold - 1, fold + 1), home + 3 * cols, lon_total)

    clear(lines(wide, near), 0, home - cols - part)
    clear(lines(wide, near), home + 2 * cols + part, lon_total)
    clear(lines(near, half + 1), 0, home - cols)
    clear(lines(near, half + 1), home + 2 * cols, lon_total)
    clear(lines(half + 1, near_cut), home + 2 * cols, home + 3 * cols)
    clear(lines(last, rows), home + 2 * cols, home + 3 * cols)

    @pl.when(turn < 0)
    def _():
        clear(lines(near_cut, last), home + 2 * cols, home + 3 * cols)

    clear(pl.ds(halo, 1), home - cols, home - part)
    clear(pl.ds(halo, 1), home + cols + part, home + 3 * cols)

    for support in supports:
        support.wait()
    span = (rows, rows_ref.shape[2])
    order = lax.broadcasted_iota(jnp.int32, span, 0)
    local = jnp.where(north, order, rows - 2 - order + 2 * lax.rem(order, 2))
    mine = (local + lat * rows == lax.broadcasted_iota(jnp.int32, span, 1)).astype(jnp.float32)
    for which, ref in enumerate((rows_ref, lons_ref, weights_ref)):
        own = lax.dot_general(
            mine,
            ref[...].astype(jnp.float32).reshape(bases * entries, rows_ref.shape[2]),
            (((1,), (1,)), ((), ())),
            precision=lax.Precision.HIGHEST,
            preferred_element_type=jnp.float32,
        )
        for k in range(bases):
            tables[which, k] = own[:, k * entries : (k + 1) * entries]

    count = [0]

    def message(where, here, there, width, target, landing=None):
        index = count[0]
        count[0] += 1
        landing = where if landing is None else landing
        return pltpu.make_async_remote_copy(
            src_ref=window.at[where, pl.ds(here, width)],
            dst_ref=window.at[landing, pl.ds(there, width)],
            send_sem=send_sem.at[index],
            recv_sem=recv_sem.at[index],
            device_id=target,
            device_id_type=MESH,
        )

    partner, beside = {"lon": me + turn}, {"lon": device(2 * turn)}
    core, core_line = {"lat": 1 - lat}, pl.ds(edge + 1, 1)
    core_landing = pl.ds(jnp.where(north, 0, rows + 1), 1)

    def own_across(first, last):
        return message(lines(first, last), home, at(-turn), cols, partner)

    def own_along(first, last, e):
        return message(lines(first, last), home, at(-2 * e), cols, {"lon": device(2 * e)})

    def half_along(first, last, e):
        offset = part if e > 0 else 0
        return message(
            lines(first, last), home + offset, at(-2 * e) + offset, part, {"lon": device(2 * e)}
        )

    def pass_along(first, last):
        return message(lines(first, last), at(turn), at(-turn), cols, beside)

    def pass_across(first, last, e):
        return message(lines(first, last), at(2 * e), at(2 * e - turn), cols, partner)

    def to_core(col, width):
        return message(core_line, col, col, width, core, core_landing)

    after = pl.multiple_of(home + jnp.where(turn > 0, cols, -part), part)
    before = pl.multiple_of(home + jnp.where(turn > 0, -part, cols), part)
    halo_own = to_core(home, cols)
    halo_across, halo_along = to_core(after, part), to_core(before, part)
    across = [own_across(last, rows), own_across(wide, near_cut)]
    across_late = [own_across(fold + 1, wide), own_across(near_cut, last)]
    along = [pass_along(last, rows), pass_along(wide, near_cut)]
    direct = own_along(near_cut, last, -turn)
    direct_across = pass_across(near_cut, last, turn)
    halves = [half_along(wide, near, e) for e in (1, -1)]
    fold_own = own_across(0, fold + 1)
    along_in, along_out = own_along(0, wide, inward), own_along(fold - 1, wide, -inward)
    fold_across = pass_across(0, fold + 1, inward)
    same = turn == inward
    late_across = pass_across(fold + 1, wide, turn), pass_across(fold - 1, wide, turn)
    pieces = channels // 256 // 2 * 256
    pieces = [(0, pieces), (pieces, channels)]
    fold_swap = [
        pltpu.make_async_remote_copy(
            src_ref=(fold_out_a, fold_out_b)[n],
            dst_ref=(fold_in_a, fold_in_b)[n],
            send_sem=send_sem.at[count[0] + n],
            recv_sem=recv_sem.at[count[0] + n],
            device_id={"lon": device(middle)},
            device_id_type=MESH,
        )
        for n, (low, high) in enumerate(pieces)
    ]

    def start(*copies):
        for copy in copies:
            copy.start()

    def arrived(*copies):
        for copy in copies:
            copy.wait_recv()

    lanes = lax.broadcasted_iota(jnp.int32, (half, lon_total), 1)
    second = lax.rem(lax.broadcasted_iota(jnp.int32, (half, entries), 0), 2)

    def turned(line, shift):
        spread = jnp.broadcast_to(line, (cols, lon_total))
        return pltpu.roll(spread, shift, 1, stride=1, stride_axis=0)

    def build_near(k, carry):
        offset = tables[1, k, half:].astype(jnp.int32)
        row_offset = tables[0, k, half:].astype(jnp.int32)
        weight = tables[2, k, half:]
        spot = (row_offset + 1 + second) * (4 * cols) + offset + cols
        sums = [jnp.zeros((half, lon_total), jnp.float32) for _ in range(2)]
        for s in range(entries):
            for v in range(2):
                hit = spot[:, s : s + 1] == lanes + v * lon_total
                sums[v] = sums[v] + jnp.where(hit, weight[:, s : s + 1], 0.0)
        for n in range(half):
            for v in range(2):
                spot_at = pl.multiple_of(k * 2 * cols + (n % 2) * cols, cols)
                near_filters[n // 2, pl.ds(spot_at, cols), v * lon_total : (v + 1) * lon_total] = (
                    turned(sums[v][n : n + 1, :], 0).astype(jnp.bfloat16)
                )
        return carry

    polar = lax.broadcasted_iota(jnp.int32, (half, entries), 0) < fold
    start_col = jnp.where(polar, place * cols, home)
    lower = lax.broadcasted_iota(jnp.int32, (cols, lon_total), 1) < home

    def build_polar(k, carry):
        spot = tables[1, k, :half].astype(jnp.int32) + start_col
        spot = jnp.where(spot >= lon_total, spot - lon_total, spot)
        spot = jnp.where(spot < 0, spot + lon_total, spot)
        row_offset = tables[0, k, :half]
        weight = tables[2, k, :half]
        picked = [jnp.where(row_offset == r, weight, 0.0) for r in (-1.0, 0.0, 1.0)]
        sums = [jnp.zeros((half, lon_total), jnp.float32) for _ in range(3)]
        for s in range(entries):
            hit = spot[:, s : s + 1] == lanes
            for r in range(3):
                sums[r] = sums[r] + jnp.where(hit, picked[r][:, s : s + 1], 0.0)
        none = jnp.zeros((cols, lon_total), jnp.float32)
        for n in range(fold):
            late = n % 2
            kept = [none] * 4
            moved = [none] * 4
            for r in range(3):
                kept[r + late] = turned(sums[r][n : n + 1, :], 0)
                moved[r + late] = turned(sums[r][n : n + 1, :], home)
            for v in range(2):
                here = jnp.where(lower, kept[2 * v], moved[2 * v + 1])
                there = jnp.where(lower, moved[2 * v], kept[2 * v + 1])
                for who, value in enumerate((here, there)):
                    spot_at = pl.multiple_of(k * 4 * cols + (2 * who + late) * cols, cols)
                    fold_filters[
                        n // 2, pl.ds(spot_at, cols), v * lon_total : (v + 1) * lon_total
                    ] = value.astype(jnp.bfloat16)
        for n in range(fold, half):
            late = n % 2
            spot_at = pl.ds(pl.multiple_of(k * 2 * cols + late * cols, cols), cols)
            for r in range(3):
                low = (r + late) * lon_total
                wide_filters[(n - fold) // 2, spot_at, low : low + lon_total] = turned(
                    sums[r][n : n + 1, :], 0
                ).astype(jnp.bfloat16)
            low = (3 - 3 * late) * lon_total
            wide_filters[(n - fold) // 2, spot_at, low : low + lon_total] = none.astype(jnp.bfloat16)
        return carry

    def filter_pairs(first, last):
        pairs = last - first
        base = jnp.where(north, 2 * first, rows - 2 * last)
        for t in range(pairs):
            q = jnp.where(north, first + t, last - 1 - t)
            taken = pl.ds(base + 2 * t, 4)
            if 2 * first >= half:
                low = home - cols
                source = window[taken, low : low + 4 * cols].reshape(16 * cols, channels)
                matrix = near_filters[q - half // 2]
            else:
                source = window[taken].reshape(4 * lon_total, channels)
                matrix = wide_filters[q - fold // 2]
            filtered = jnp.dot(matrix, source, preferred_element_type=jnp.float32)
            filtered = filtered.astype(jnp.bfloat16)
            for k in range(bases):
                product[2 * t * cols : 2 * (t + 1) * cols, k * channels : (k + 1) * channels] = (
                    filtered[2 * k * cols : 2 * (k + 1) * cols]
                )

    def fold_pairs():
        pairs = fold // 2
        cells = fold * cols
        base = jnp.where(north, 0, rows - fold)
        for t in range(pairs):
            q = jnp.where(north, t, pairs - 1 - t)
            source = window[pl.ds(base + 2 * t, 4), pl.ds(at(-place), 4 * cols)]
            source = source.reshape(16 * cols, channels)
            filtered = jnp.dot(fold_filters[q], source, preferred_element_type=jnp.float32)
            filtered = filtered.astype(jnp.bfloat16)
            for k in range(bases):
                for who in range(2):
                    low, from_row = who * cells + 2 * t * cols, (4 * k + 2 * who) * cols
                    product[low : low + 2 * cols, k * channels : (k + 1) * channels] = filtered[
                        from_row : from_row + 2 * cols
                    ]

    def fold_mix(low, high):
        cells = fold * cols
        mixed = jnp.dot(
            product[: 2 * cells], mix_ref[:, low:high], preferred_element_type=jnp.float32
        )
        (fold_out_a if low == 0 else fold_out_b)[...] = mixed[cells:].astype(jnp.bfloat16)
        mixed_ref[pl.ds(jnp.where(north, 0, half * cols - cells), cells), low:high] = mixed[:cells]

    def mix_pairs(pairs):
        cells = 2 * pairs * cols
        return jnp.dot(product[:cells], mix_ref[...], preferred_element_type=jnp.float32)

    def finish(mixed, base, depth):
        cells = depth * cols
        here = window[pl.ds(base + 1, depth), home : home + cols].reshape(cells, channels)
        latent = here.astype(jnp.float32) + mixed
        mean = jnp.mean(latent, axis=1, keepdims=True)
        centred = latent - mean
        variance = jnp.mean(centred * centred, axis=1, keepdims=True)
        normed = (centred * lax.rsqrt(variance + norm_eps) * gain_ref[...][None, :]).astype(
            jnp.bfloat16
        )
        raised = jnp.dot(normed, up_ref[...], preferred_element_type=jnp.float32)
        hidden = 0.5 * raised * (1.0 + lax.erf(raised * math.sqrt(0.5)))
        lowered = jnp.dot(
            hidden.astype(jnp.bfloat16), down_ref[...], preferred_element_type=jnp.float32
        )
        result = (latent + lowered).astype(jnp.bfloat16)
        out_ref[pl.ds(base, depth)] = result.reshape(depth, cols, channels)

    fold_pair, half_pair, all_pairs = fold // 2, half // 2, rows // 2
    pl.semaphore_wait(barrier, 2 + jnp.where(above, 1, 0) + jnp.where(below, 1, 0))

    @pl.when(inner)
    def _():
        greet(ready.at[0], lon=me + 2)
        greet(ready.at[0], lon=me - 2)

    fetch.wait()
    start(halo_own, *across, fold_own, along_in)
    goes_near = jnp.logical_or(inner, jnp.logical_not(same))

    @pl.when(goes_near)
    def _():
        start(direct)

    @pl.when(inner)
    def _():
        start(along_out)

    lax.fori_loop(0, bases // 2, build_near, 0)
    pl.semaphore_wait(ready.at[0], 1)

    @pl.when(inner)
    def _():
        greet(ready.at[1], lon=device(2 * inward))

    lax.fori_loop(bases // 2, bases, build_near, 0)
    lax.fori_loop(0, bases // 2, build_polar, 0)

    @pl.when(outer)
    def _():
        pl.semaphore_wait(ready.at[1], 1)

        @pl.when(same)
        def _():
            start(direct)

        start(along_out)

    start(*halves)
    lax.fori_loop(bases // 2, bases, build_polar, 0)
    arrived(along_in)
    start(fold_across, *across_late)
    arrived(*across)
    start(*along, halo_across)
    arrived(direct)
    start(direct_across)
    for load in loads:
        load.wait()
    arrived(fold_own, fold_across)
    fold_pairs()
    for swap, (low, high) in zip(fold_swap, pieces):
        fold_mix(low, high)
        start(swap)
    arrived(along_out)

    @pl.when(same)
    def _():
        start(late_across[0])

    @pl.when(jnp.logical_not(same))
    def _():
        start(late_across[1])

    arrived(along[0])
    start(halo_along)
    arrived(across_late[1], direct_across, halo_own, halo_across, halo_along, along[1], *halves)
    filter_pairs(half_pair, all_pairs)
    finish(mix_pairs(all_pairs - half_pair), jnp.where(north, half, 0), rows - half)

    @pl.when(same)
    def _():
        arrived(late_across[1])

    @pl.when(jnp.logical_not(same))
    def _():
        arrived(late_across[0])

    arrived(across_late[0])
    filter_pairs(fold_pair, half_pair)
    cells = (half - fold) * cols
    mixed_ref[pl.ds(jnp.where(north, fold * cols, 0), cells)] = mix_pairs(half_pair - fold_pair)
    arrived(*fold_swap)
    own_part = pl.ds(jnp.where(north, 0, half * cols - fold * cols), fold * cols)
    for (low, high), piece in zip(pieces, (fold_in_a, fold_in_b)):
        mixed_ref[own_part, low:high] = mixed_ref[own_part, low:high] + piece[...].astype(jnp.float32)
    finish(mixed_ref[...], jnp.where(north, 0, half), half)

    @pl.when(same)
    def _():
        late_across[0].wait_send()

    @pl.when(jnp.logical_not(same))
    def _():
        late_across[1].wait_send()

    sent = [halo_own, halo_across, halo_along, fold_own, fold_across, along_in, along_out]
    sent += [direct, direct_across] + fold_swap
    for copy in sent + across + across_late + along + halves:
        copy.wait_send()


def relay_call(
    lon_count,
    lat_count,
    fields,
    support_rows,
    support_lons,
    support_weights,
    mix_weight,
    norm_gain,
    up_weight,
    down_weight,
):
    channels, rows, cols = fields.shape
    bases, hidden = mix_weight.shape[0], up_weight.shape[1]
    lon_total = lon_count * cols
    half, copies = rows // 2, 24
    fold = fold_rows(lon_count, lat_count, rows, cols)
    piece = channels // 256 // 2 * 256
    in_vmem = pl.BlockSpec(memory_space=pltpu.VMEM)
    anywhere = pl.BlockSpec(memory_space=pl.ANY)
    result = pl.pallas_call(
        functools.partial(relay_kernel, lon_count, lat_count),
        out_shape=pltpu.VMEM((rows, cols, channels), jnp.bfloat16),
        in_specs=[anywhere] * 8,
        out_specs=in_vmem,
        scratch_shapes=[
            pltpu.VMEM((rows + 2, lon_total, channels), jnp.bfloat16),
            pltpu.VMEM((fold // 2, 4 * bases * cols, 16 * cols), jnp.bfloat16),
            pltpu.VMEM(((half - fold) // 2, 2 * bases * cols, 4 * lon_total), jnp.bfloat16),
            pltpu.VMEM((half // 2, 2 * bases * cols, 16 * cols), jnp.bfloat16),
            pltpu.VMEM((half * cols, bases * channels), jnp.bfloat16),
            pltpu.VMEM((half * cols, channels), jnp.float32),
            pltpu.VMEM((fold * cols, piece), jnp.bfloat16),
            pltpu.VMEM((fold * cols, channels - piece), jnp.bfloat16),
            pltpu.VMEM((fold * cols, piece), jnp.bfloat16),
            pltpu.VMEM((fold * cols, channels - piece), jnp.bfloat16),
            pltpu.VMEM((bases * channels, channels), jnp.bfloat16),
            pltpu.VMEM((channels, hidden), jnp.bfloat16),
            pltpu.VMEM((hidden, channels), jnp.bfloat16),
            pltpu.SemaphoreType.DMA((copies,)),
            pltpu.SemaphoreType.DMA((copies,)),
            pltpu.SemaphoreType.DMA((8,)),
            pltpu.SemaphoreType.REGULAR((2,)),
            pltpu.VMEM((3, bases, rows, support_rows.shape[2]), jnp.float32),
            pltpu.VMEM((bases, support_rows.shape[2], support_rows.shape[1]), jnp.int32),
            pltpu.VMEM((bases, support_rows.shape[2], support_rows.shape[1]), jnp.int32),
            pltpu.VMEM((bases, support_rows.shape[2], support_rows.shape[1]), jnp.float32),
            pltpu.VMEM((channels,), jnp.float32),
        ],
        compiler_params=pltpu.CompilerParams(
            collective_id=0, has_side_effects=True, vmem_limit_bytes=56 * 1024 * 1024
        ),
    )(
        jnp.transpose(fields, (1, 2, 0)),
        jnp.transpose(support_rows, (0, 2, 1)),
        jnp.transpose(support_lons, (0, 2, 1)),
        jnp.transpose(support_weights, (0, 2, 1)),
        norm_gain,
        mix_weight.reshape(bases * channels, channels),
        up_weight,
        down_weight,
    )
    return jnp.transpose(result, (2, 0, 1))


def direct_call(
    lon_count,
    lat_count,
    fields,
    support_rows,
    support_lons,
    support_weights,
    mix_weight,
    norm_gain,
    up_weight,
    down_weight,
):
    channels, rows, cols = fields.shape
    bases, hidden = mix_weight.shape[0], up_weight.shape[1]
    lon_total = lon_count * cols
    plan = plan_copies(lon_count, lat_count, rows, cols)
    count = sum(len(stage) for stage in plan[1])
    in_vmem = pl.BlockSpec(memory_space=pltpu.VMEM)
    anywhere = pl.BlockSpec(memory_space=pl.ANY)
    result = pl.pallas_call(
        functools.partial(block_kernel, lon_count, lat_count, plan),
        out_shape=jax.ShapeDtypeStruct((rows, cols, channels), jnp.bfloat16),
        in_specs=[anywhere] + [in_vmem] * 4 + [anywhere] * 3,
        out_specs=anywhere,
        scratch_shapes=[
            pltpu.VMEM((rows, cols, channels), jnp.bfloat16),
            pltpu.VMEM((rows, cols, channels), jnp.bfloat16),
            pltpu.VMEM((rows + 2, lon_total, channels), jnp.bfloat16),
            pltpu.VMEM((rows, bases * cols, 3 * lon_total), jnp.bfloat16),
            pltpu.VMEM((rows // 2 * cols, bases * channels), jnp.bfloat16),
            pltpu.VMEM((bases * channels, channels), jnp.bfloat16),
            pltpu.VMEM((channels, hidden), jnp.bfloat16),
            pltpu.VMEM((hidden, channels), jnp.bfloat16),
            pltpu.SemaphoreType.DMA((count,)),
            pltpu.SemaphoreType.DMA((count,)),
            pltpu.SemaphoreType.DMA((4,)),
            pltpu.SemaphoreType.DMA((len(plan[0]),)),
        ],
        compiler_params=pltpu.CompilerParams(
            collective_id=0, has_side_effects=True, vmem_limit_bytes=56 * 1024 * 1024
        ),
    )(
        jnp.transpose(fields, (1, 2, 0)),
        jnp.transpose(support_rows, (0, 2, 1)),
        jnp.transpose(support_lons, (0, 2, 1)),
        jnp.transpose(support_weights, (0, 2, 1)),
        norm_gain,
        mix_weight.reshape(bases * channels, channels),
        up_weight,
        down_weight,
    )
    return jnp.transpose(result, (2, 0, 1))


def on_device(lon_count, lat_count, *arrays):
    channels, rows, cols = arrays[0].shape
    if relay_fits(lon_count, lat_count, rows, cols):
        return relay_call(lon_count, lat_count, *arrays)
    return direct_call(lon_count, lat_count, *arrays)


def solution(mesh):
    in_specs = (P("member", "lat", "lon"), P(), P(), P(), P(), P(), P(), P())
    out_specs = P("member", "lat", "lon")
    return jax.shard_map(
        functools.partial(on_device, mesh.shape["lon"], mesh.shape["lat"]),
        mesh=mesh,
        in_specs=in_specs,
        out_specs=out_specs,
        check_vma=False,
    )
```

```python
import functools
import math

import jax
import jax.numpy as jnp
from jax import lax
from jax.experimental import pallas as pl
from jax.experimental.pallas import tpu as pltpu
from jax.sharding import PartitionSpec as P

norm_eps = 1e-05
MESH = pl.DeviceIdType.MESH


def plan_copies(lon_count, lat_count, rows, cols):
    lon_total, row_total = lon_count * cols, lat_count * rows

    def reach(row):
        nearest = min(row + 1, row_total - row)
        return min(lon_total // 2, 4 * row_total // nearest)

    def distance(row):
        return min(-(-reach(row) // cols), lon_count // 2)

    def in_half(span, delta):
        if delta == 0 or abs(delta) == lon_count // 2:
            return False
        return span - cols * (abs(delta) - 1) <= cols // 2

    need = [distance(max(p - 1, 0)) for p in range(rows)]
    deltas = [d for d in range(1 - lon_count // 2, lon_count // 2 + 1) if d != 0]
    counts = {delta: sum(1 for d in need if d >= abs(delta)) for delta in deltas}
    spans = [reach(max(p - 1, 0)) for p in range(rows)]
    fulls = {d: sum(1 for p in range(counts[d]) if not in_half(spans[p], d)) for d in deltas}
    edge, edge_span = 0, 0
    for boundary in range(1, lat_count):
        edge = max(edge, distance(boundary * rows - 1), distance(boundary * rows))
        edge_span = max(edge_span, reach(boundary * rows - 1), reach(boundary * rows))
    halo = [d for d in range(1 - lon_count // 2, lon_count // 2 + 1) if abs(d) <= edge]
    groups = [(rows // 2, rows), (rows // 4, rows // 2), (0, rows // 4)]
    stages = []
    upper = rows
    for low, _ in groups:
        lower = max(low - 1, 0)
        stage = []
        for delta in sorted(deltas, key=lambda d: -abs(d)):
            full, top = min(fulls[delta], upper), min(counts[delta], upper)
            if full > lower:
                stage.append(("block", delta, lower, full, False))
            if top > max(full, lower):
                stage.append(("block", delta, max(full, lower), top, True))
        stages.append(stage)
        upper = lower
    if lat_count > 1:
        stages[0] = [
            (side, d, 0, 1, in_half(edge_span, d)) for d in halo for side in ("down", "up")
        ] + stages[0]
    halves = [d for d in halo if in_half(edge_span, d)]
    return groups, stages, counts, fulls, halo, halves


def block_kernel(
    lon_count,
    lat_count,
    plan,
    x_hbm,
    rows_ref,
    lons_ref,
    weights_ref,
    gain_ref,
    mix_hbm,
    up_hbm,
    down_hbm,
    out_hbm,
    x_ref,
    out_ref,
    window,
    filters,
    product,
    mix_ref,
    up_ref,
    down_ref,
    send_sem,
    recv_sem,
    load_sem,
    out_sem,
):
    rows, cols, channels = x_ref.shape
    bases, entries = rows_ref.shape[:2]
    lon_total = lon_count * cols
    middle = lon_count // 2
    groups, stages, counts, fulls, halo, halves = plan
    me, lat = lax.axis_index("lon"), lax.axis_index("lat")
    north = 2 * lat < lat_count
    has_low, has_high = lat > 0, lat < lat_count - 1

    loads = [
        pltpu.make_async_copy(mix_hbm, mix_ref, load_sem.at[0]),
        pltpu.make_async_copy(up_hbm, up_ref, load_sem.at[1]),
        pltpu.make_async_copy(down_hbm, down_ref, load_sem.at[2]),
    ]
    fetch = pltpu.make_async_copy(x_hbm, x_ref, load_sem.at[3])
    fetch.start()

    barrier = pltpu.get_barrier_semaphore()
    halo_deltas = halo if lat_count > 1 else []
    for delta in range(1, lon_count):
        pl.semaphore_signal(
            barrier, inc=1, device_id={"lon": lax.rem(me + delta, lon_count)}, device_id_type=MESH
        )
    for present, other in ((has_low, lat - 1), (has_high, lat + 1)):

        @pl.when(present)
        def _():
            for delta in halo_deltas:
                target = lax.rem(me + lon_count - delta, lon_count)
                pl.semaphore_signal(
                    barrier, inc=1, device_id={"lon": target, "lat": other}, device_id_type=MESH
                )

    sides = jnp.where(has_low, 1, 0) + jnp.where(has_high, 1, 0)
    pl.semaphore_wait(barrier, lon_count - 1 + sides * len(halo_deltas))
    fetch.wait()

    def copy_of(index, item):
        kind, delta, first, last, halved = item
        width = cols // 2 if halved else cols
        offset = cols // 2 if halved and delta < 0 else 0
        target = lax.rem(me + lon_count - delta, lon_count)
        slot = (delta + middle) % lon_count
        here, there = pl.ds(offset, width), pl.ds(slot * cols + offset, width)
        if kind == "block":
            start = jnp.where(north, first, rows - last)
            source = x_ref.at[pl.ds(start, last - first), here]
            landing = window.at[pl.ds(start + 1, last - first), there]
            device = {"lon": target}
        elif kind == "down":
            source = x_ref.at[pl.ds(rows - 1, 1), here]
            landing = window.at[pl.ds(0, 1), there]
            device = {"lon": target, "lat": jnp.minimum(lat + 1, lat_count - 1)}
        else:
            source = x_ref.at[pl.ds(0, 1), here]
            landing = window.at[pl.ds(rows + 1, 1), there]
            device = {"lon": target, "lat": jnp.maximum(lat - 1, 0)}
        return pltpu.make_async_remote_copy(
            src_ref=source,
            dst_ref=landing,
            send_sem=send_sem.at[index],
            recv_sem=recv_sem.at[index],
            device_id=device,
            device_id_type=MESH,
        )

    copies = []
    for stage in stages:
        copies.append(list(enumerate(stage, sum(len(done) for done in copies))))

    def each(items, sending, action):
        for index, item in items:
            if item[0] == "block":
                action(copy_of(index, item))
            else:
                present = has_high if (item[0] == "down") == sending else has_low

                @pl.when(present)
                def _():
                    action(copy_of(index, item))

    for stage in copies:
        each(stage, True, lambda copy: copy.start())
    for load in loads:
        load.start()

    window[1 : rows + 1, middle * cols : (middle + 1) * cols, :] = x_ref[...]
    for delta, count in counts.items():
        slot = (delta + middle) % lon_count
        if count < rows:
            gap = (rows - count, cols, channels)
            window[pl.ds(jnp.where(north, count, 0) + 1, rows - count),
                   slot * cols : (slot + 1) * cols] = jnp.zeros(gap, jnp.bfloat16)
        partial = count - fulls[delta]
        if partial > 0:
            far = slot * cols + (0 if delta < 0 else cols // 2)
            window[pl.ds(jnp.where(north, fulls[delta], rows - count) + 1, partial),
                   far : far + cols // 2] = jnp.zeros(
                (partial, cols // 2, channels), jnp.bfloat16
            )
    for delta in halves:
        far = (delta + middle) % lon_count * cols + (0 if delta < 0 else cols // 2)
        for line in (0, rows + 1):
            window[line, far : far + cols // 2] = jnp.zeros((cols // 2, channels), jnp.bfloat16)
    for present, line in ((has_low, 0), (has_high, rows + 1)):
        for delta in range(1 - middle, middle + 1):
            slot = (delta + middle) % lon_count

            def clear():
                window[line, slot * cols : (slot + 1) * cols] = jnp.zeros(
                    (cols, channels), jnp.bfloat16
                )

            if delta in halo and lat_count > 1:
                pl.when(jnp.logical_not(present))(clear)
            else:
                clear()

    lanes = lax.broadcasted_iota(jnp.int32, (rows, lon_total), 1)
    wide = (rows, rows_ref.shape[2])
    own_rows = (
        lax.broadcasted_iota(jnp.int32, wide, 0) + lat * rows
        == lax.broadcasted_iota(jnp.int32, wide, 1)
    ).astype(jnp.float32)

    def own(ref, k):
        return lax.dot_general(
            own_rows,
            ref[k].astype(jnp.float32),
            (((1,), (1,)), ((), ())),
            precision=lax.Precision.HIGHEST,
            preferred_element_type=jnp.float32,
        )

    def build(k, carry):
        spot = own(lons_ref, k).astype(jnp.int32) + middle * cols
        spot = jnp.where(spot >= lon_total, spot - lon_total, spot)
        row_offset = own(rows_ref, k)
        weight = own(weights_ref, k)
        picked = [jnp.where(row_offset == r, weight, 0.0) for r in (-1.0, 0.0, 1.0)]
        sums = [jnp.zeros((rows, lon_total), jnp.float32) for _ in range(3)]
        for s in range(entries):
            hit = spot[:, s : s + 1] == lanes
            for r in range(3):
                sums[r] = sums[r] + jnp.where(hit, picked[r][:, s : s + 1], 0.0)
        for r in range(3):
            for i in range(rows):
                line = jnp.broadcast_to(sums[r][i : i + 1, :], (cols, lon_total))
                turned = pltpu.roll(line, 0, 1, stride=1, stride_axis=0)
                filters[i, pl.ds(pl.multiple_of(k * cols, cols), cols),
                        r * lon_total : (r + 1) * lon_total] = turned.astype(jnp.bfloat16)
        return carry

    lax.fori_loop(0, bases, build, 0)

    def group(low, high):
        start = jnp.where(north, low, rows - high)
        half = high - low
        lines = half * cols
        def filter_row(t, carry):
            i = start + t
            source = window[pl.ds(i, 3)].reshape(3 * lon_total, channels)
            filtered = jnp.dot(filters[i], source, preferred_element_type=jnp.float32)
            filtered = filtered.astype(jnp.bfloat16)
            at = pl.multiple_of(t * cols, cols)
            for k in range(bases):
                product[pl.ds(at, cols), k * channels : (k + 1) * channels] = filtered[
                    k * cols : (k + 1) * cols
                ]
            return carry

        lax.fori_loop(0, half, filter_row, 0)
        mixed = jnp.dot(product[:lines], mix_ref[...], preferred_element_type=jnp.float32)
        here = x_ref[pl.ds(start, half)].reshape(lines, channels)
        latent = here.astype(jnp.float32) + mixed
        mean = jnp.mean(latent, axis=1, keepdims=True)
        centred = latent - mean
        variance = jnp.mean(centred * centred, axis=1, keepdims=True)
        normed = (centred * lax.rsqrt(variance + norm_eps) * gain_ref[...][None, :]).astype(jnp.bfloat16)
        raised = jnp.dot(normed, up_ref[...], preferred_element_type=jnp.float32)
        hidden = 0.5 * raised * (1.0 + lax.erf(raised * math.sqrt(0.5)))
        lowered = jnp.dot(
            hidden.astype(jnp.bfloat16), down_ref[...], preferred_element_type=jnp.float32
        )
        result = (latent + lowered).astype(jnp.bfloat16)
        out_ref[pl.ds(start, half)] = result.reshape(half, cols, channels)

    puts = []
    for stage, (low, high) in zip(copies, groups):
        each(stage, False, lambda copy: copy.wait_recv())
        if stage is copies[0]:
            for load in loads:
                load.wait()
        group(low, high)
        part = pl.ds(jnp.where(north, low, rows - high), high - low)
        put = pltpu.make_async_copy(out_ref.at[part], out_hbm.at[part], out_sem.at[len(puts)])
        put.start()
        puts.append(put)
    for stage in copies:
        each(stage, True, lambda copy: copy.wait_send())
    for put in puts:
        put.wait()


def source_reach(lon_total, row_total, p):
    row = max(p - 1, 0)
    return min(lon_total // 2, 4 * row_total // min(row + 1, row_total - row))


def fold_rows(lon_count, lat_count, rows, cols):
    lon_total, row_total = lon_count * cols, lat_count * rows
    fold = 2
    while source_reach(lon_total, row_total, fold + 1) > 2 * cols:
        fold += 2
    return fold


def relay_fits(lon_count, lat_count, rows, cols):
    lon_total, row_total = lon_count * cols, lat_count * rows
    if lon_count != 8 or lat_count != 2 or rows % 4 != 0 or cols != 16:
        return False
    near = source_reach(lon_total, row_total, rows // 2 + 1) <= cols
    return near and fold_rows(lon_count, lat_count, rows, cols) <= rows // 4


def relay_kernel(
    lon_count,
    lat_count,
    x_hbm,
    rows_hbm,
    lons_hbm,
    weights_hbm,
    gain_hbm,
    mix_hbm,
    up_hbm,
    down_hbm,
    out_ref,
    window,
    fold_filters,
    wide_filters,
    near_filters,
    product,
    mixed_ref,
    fold_out_a,
    fold_out_b,
    fold_in_a,
    fold_in_b,
    mix_ref,
    up_ref,
    down_ref,
    send_sem,
    recv_sem,
    load_sem,
    ready,
    tables,
    rows_ref,
    lons_ref,
    weights_ref,
    gain_ref,
):
    rows, cols, channels = x_hbm.shape
    bases, entries = rows_ref.shape[:2]
    lon_total, row_total = lon_count * cols, lat_count * rows
    middle, part, half = lon_count // 2, cols // 2, rows // 2
    home = middle * cols
    fold = fold_rows(lon_count, lat_count, rows, cols)
    reaches = [source_reach(lon_total, row_total, max(p, fold + 1)) for p in range(rows)]
    wide = sum(1 for r in reaches if r > cols + part)
    near = sum(1 for r in reaches if r > cols)
    me, lat = lax.axis_index("lon"), lax.axis_index("lat")
    north = lat == 0
    turn = 1 - 2 * lax.rem(me, 2)
    place = lax.rem(me, middle)
    inward = jnp.where(place < 2, 1, -1)
    edge = jnp.where(north, rows - 1, 0)

    def device(delta):
        return lax.rem(me + delta + lon_count, lon_count)

    def at(delta):
        return pl.multiple_of(lax.rem(delta + middle + lon_count, lon_count) * cols, cols)

    def lines(first, last):
        return pl.ds(jnp.where(north, first, rows - last) + 1, last - first)

    fetch = pltpu.make_async_copy(
        x_hbm, window.at[pl.ds(1, rows), pl.ds(home, cols)], load_sem.at[3]
    )
    loads = [
        pltpu.make_async_copy(mix_hbm, mix_ref, load_sem.at[0]),
        pltpu.make_async_copy(up_hbm, up_ref, load_sem.at[1]),
        pltpu.make_async_copy(down_hbm, down_ref, load_sem.at[2]),
    ]
    supports = [
        pltpu.make_async_copy(source, landing, load_sem.at[4 + n])
        for n, (source, landing) in enumerate(
            [(rows_hbm, rows_ref), (lons_hbm, lons_ref), (weights_hbm, weights_ref)]
        )
    ]
    loads.append(pltpu.make_async_copy(gain_hbm, gain_ref, load_sem.at[7]))
    barrier = pltpu.get_barrier_semaphore()
    above, below = me < lon_count - 2, me >= 2
    inner = jnp.logical_and(above, below)
    outer = jnp.logical_not(inner)

    def greet(semaphore, **other):
        pl.semaphore_signal(semaphore, inc=1, device_id=other, device_id_type=MESH)

    greet(barrier, lon=me + turn)
    greet(barrier, lat=1 - lat)

    @pl.when(above)
    def _():
        greet(barrier, lon=me + 2)

    @pl.when(below)
    def _():
        greet(barrier, lon=me - 2)

    for load in [fetch] + supports + loads:
        load.start()

    def clear(where, low, high):
        size = where.size if isinstance(where, pl.Slice) else 1
        window[where, low:high] = jnp.zeros((size, high - low, channels), jnp.bfloat16)

    near_cut, last = half + (rows - half) // 2 - 1, rows - 1
    sky, halo = jnp.where(north, 0, rows + 1), jnp.where(north, rows + 1, 0)
    def clear_window():
        clear(pl.ds(sky, 1), 0, lon_total)
        clear(lines(fold + 1, wide), 0, home - 2 * cols)
        clear(lines(fold + 1, wide), home + 3 * cols, lon_total)
        clear(lines(fold - 1, fold + 1), 0, cols)

        @pl.when(place != middle - 1)
        def _():
            clear(lines(fold - 1, fold + 1), cols, 2 * cols)

        @pl.when(place != 0)
        def _():
            clear(lines(fold - 1, fold + 1), home + 3 * cols, lon_total)

        clear(lines(wide, near), 0, home - cols - part)
        clear(lines(wide, near), home + 2 * cols + part, lon_total)
        clear(lines(near, half + 1), 0, home - cols)
        clear(lines(near, half + 1), home + 2 * cols, lon_total)
        clear(lines(half + 1, near_cut), home + 2 * cols, home + 3 * cols)
        clear(lines(last, rows), home + 2 * cols, home + 3 * cols)

        @pl.when(turn < 0)
        def _():
            clear(lines(near_cut, last), home + 2 * cols, home + 3 * cols)

        clear(pl.ds(halo, 1), home - cols, home - part)
        clear(pl.ds(halo, 1), home + cols + part, home + 3 * cols)

    def select_tables():
        for support in supports:
            support.wait()
        span = (rows, rows_ref.shape[2])
        order = lax.broadcasted_iota(jnp.int32, span, 0)
        local = jnp.where(north, order, rows - 2 - order + 2 * lax.rem(order, 2))
        mine = (local + lat * rows == lax.broadcasted_iota(jnp.int32, span, 1)).astype(jnp.float32)
        for which, ref in enumerate((rows_ref, lons_ref, weights_ref)):
            own = lax.dot_general(
                mine,
                ref[...].astype(jnp.float32).reshape(bases * entries, rows_ref.shape[2]),
                (((1,), (1,)), ((), ())),
                precision=lax.Precision.HIGHEST,
                preferred_element_type=jnp.float32,
            )
            for k in range(bases):
                tables[which, k] = own[:, k * entries : (k + 1) * entries]

    count = [0]

    def message(where, here, there, width, target, landing=None):
        index = count[0]
        count[0] += 1
        landing = where if landing is None else landing
        return pltpu.make_async_remote_copy(
            src_ref=window.at[where, pl.ds(here, width)],
            dst_ref=window.at[landing, pl.ds(there, width)],
            send_sem=send_sem.at[index],
            recv_sem=recv_sem.at[index],
            device_id=target,
            device_id_type=MESH,
        )

    partner, beside = {"lon": me + turn}, {"lon": device(2 * turn)}
    core, core_line = {"lat": 1 - lat}, pl.ds(edge + 1, 1)
    core_landing = pl.ds(jnp.where(north, 0, rows + 1), 1)

    def own_across(first, last):
        return message(lines(first, last), home, at(-turn), cols, partner)

    def own_along(first, last, e):
        return message(lines(first, last), home, at(-2 * e), cols, {"lon": device(2 * e)})

    def half_along(first, last, e):
        offset = part if e > 0 else 0
        return message(
            lines(first, last), home + offset, at(-2 * e) + offset, part, {"lon": device(2 * e)}
        )

    def pass_along(first, last):
        return message(lines(first, last), at(turn), at(-turn), cols, beside)

    def pass_across(first, last, e):
        return message(lines(first, last), at(2 * e), at(2 * e - turn), cols, partner)

    def to_core(col, width):
        return message(core_line, col, col, width, core, core_landing)

    after = pl.multiple_of(home + jnp.where(turn > 0, cols, -part), part)
    before = pl.multiple_of(home + jnp.where(turn > 0, -part, cols), part)
    halo_own = to_core(home, cols)
    halo_across, halo_along = to_core(after, part), to_core(before, part)
    across = [own_across(last, rows), own_across(wide, near_cut)]
    across_late = [own_across(fold + 1, wide), own_across(near_cut, last)]
    along = [pass_along(last, rows), pass_along(wide, near_cut)]
    direct = own_along(near_cut, last, -turn)
    direct_across = pass_across(near_cut, last, turn)
    halves = [half_along(wide, near, e) for e in (1, -1)]
    fold_own = own_across(0, fold + 1)
    along_in, along_out = own_along(0, wide, inward), own_along(fold - 1, wide, -inward)
    fold_across = pass_across(0, fold + 1, inward)
    same = turn == inward
    late_across = pass_across(fold + 1, wide, turn), pass_across(fold - 1, wide, turn)
    pieces = channels // 256 // 2 * 256
    pieces = [(0, pieces), (pieces, channels)]
    fold_swap = [
        pltpu.make_async_remote_copy(
            src_ref=(fold_out_a, fold_out_b)[n],
            dst_ref=(fold_in_a, fold_in_b)[n],
            send_sem=send_sem.at[count[0] + n],
            recv_sem=recv_sem.at[count[0] + n],
            device_id={"lon": device(middle)},
            device_id_type=MESH,
        )
        for n, (low, high) in enumerate(pieces)
    ]

    def start(*copies):
        for copy in copies:
            copy.start()

    def arrived(*copies):
        for copy in copies:
            copy.wait_recv()

    lanes = lax.broadcasted_iota(jnp.int32, (half, lon_total), 1)
    second = lax.rem(lax.broadcasted_iota(jnp.int32, (half, entries), 0), 2)

    def turned(line, shift):
        spread = jnp.broadcast_to(line, (cols, lon_total))
        return pltpu.roll(spread, shift, 1, stride=1, stride_axis=0)

    def build_near(k, carry):
        offset = tables[1, k, half:].astype(jnp.int32)
        row_offset = tables[0, k, half:].astype(jnp.int32)
        weight = tables[2, k, half:]
        spot = (row_offset + 1 + second) * (4 * cols) + offset + cols
        sums = [jnp.zeros((half, lon_total), jnp.float32) for _ in range(2)]
        for s in range(entries):
            for v in range(2):
                hit = spot[:, s : s + 1] == lanes + v * lon_total
                sums[v] = sums[v] + jnp.where(hit, weight[:, s : s + 1], 0.0)
        for n in range(half):
            for v in range(2):
                spot_at = pl.multiple_of(k * 2 * cols + (n % 2) * cols, cols)
                near_filters[n // 2, pl.ds(spot_at, cols), v * lon_total : (v + 1) * lon_total] = (
                    turned(sums[v][n : n + 1, :], 0).astype(jnp.bfloat16)
                )
        return carry

    polar = lax.broadcasted_iota(jnp.int32, (half, entries), 0) < fold
    start_col = jnp.where(polar, place * cols, home)
    lower = lax.broadcasted_iota(jnp.int32, (cols, lon_total), 1) < home

    def build_polar(k, carry):
        spot = tables[1, k, :half].astype(jnp.int32) + start_col
        spot = jnp.where(spot >= lon_total, spot - lon_total, spot)
        spot = jnp.where(spot < 0, spot + lon_total, spot)
        row_offset = tables[0, k, :half]
        weight = tables[2, k, :half]
        picked = [jnp.where(row_offset == r, weight, 0.0) for r in (-1.0, 0.0, 1.0)]
        sums = [jnp.zeros((half, lon_total), jnp.float32) for _ in range(3)]
        for s in range(entries):
            hit = spot[:, s : s + 1] == lanes
            for r in range(3):
                sums[r] = sums[r] + jnp.where(hit, picked[r][:, s : s + 1], 0.0)
        none = jnp.zeros((cols, lon_total), jnp.float32)
        for n in range(fold):
            late = n % 2
            kept = [none] * 4
            moved = [none] * 4
            for r in range(3):
                kept[r + late] = turned(sums[r][n : n + 1, :], 0)
                moved[r + late] = turned(sums[r][n : n + 1, :], home)
            for v in range(2):
                here = jnp.where(lower, kept[2 * v], moved[2 * v + 1])
                there = jnp.where(lower, moved[2 * v], kept[2 * v + 1])
                for who, value in enumerate((here, there)):
                    spot_at = pl.multiple_of(k * 4 * cols + (2 * who + late) * cols, cols)
                    fold_filters[
                        n // 2, pl.ds(spot_at, cols), v * lon_total : (v + 1) * lon_total
                    ] = value.astype(jnp.bfloat16)
        for n in range(fold, half):
            late = n % 2
            spot_at = pl.ds(pl.multiple_of(k * 2 * cols + late * cols, cols), cols)
            for r in range(3):
                low = (r + late) * lon_total
                wide_filters[(n - fold) // 2, spot_at, low : low + lon_total] = turned(
                    sums[r][n : n + 1, :], 0
                ).astype(jnp.bfloat16)
            low = (3 - 3 * late) * lon_total
            wide_filters[(n - fold) // 2, spot_at, low : low + lon_total] = none.astype(jnp.bfloat16)
        return carry

    def filter_pairs(first, last):
        pairs = last - first
        base = jnp.where(north, 2 * first, rows - 2 * last)
        for t in range(pairs):
            q = jnp.where(north, first + t, last - 1 - t)
            taken = pl.ds(base + 2 * t, 4)
            if 2 * first >= half:
                low = home - cols
                source = window[taken, low : low + 4 * cols].reshape(16 * cols, channels)
                matrix = near_filters[q - half // 2]
            else:
                source = window[taken].reshape(4 * lon_total, channels)
                matrix = wide_filters[q - fold // 2]
            filtered = jnp.dot(matrix, source, preferred_element_type=jnp.float32)
            filtered = filtered.astype(jnp.bfloat16)
            for k in range(bases):
                product[2 * t * cols : 2 * (t + 1) * cols, k * channels : (k + 1) * channels] = (
                    filtered[2 * k * cols : 2 * (k + 1) * cols]
                )

    def fold_pairs():
        pairs = fold // 2
        cells = fold * cols
        base = jnp.where(north, 0, rows - fold)
        for t in range(pairs):
            q = jnp.where(north, t, pairs - 1 - t)
            source = window[pl.ds(base + 2 * t, 4), pl.ds(at(-place), 4 * cols)]
            source = source.reshape(16 * cols, channels)
            filtered = jnp.dot(fold_filters[q], source, preferred_element_type=jnp.float32)
            filtered = filtered.astype(jnp.bfloat16)
            for k in range(bases):
                for who in range(2):
                    low, from_row = who * cells + 2 * t * cols, (4 * k + 2 * who) * cols
                    product[low : low + 2 * cols, k * channels : (k + 1) * channels] = filtered[
                        from_row : from_row + 2 * cols
                    ]

    def fold_mix(low, high):
        cells = fold * cols
        mixed = jnp.dot(
            product[: 2 * cells], mix_ref[:, low:high], preferred_element_type=jnp.float32
        )
        (fold_out_a if low == 0 else fold_out_b)[...] = mixed[cells:].astype(jnp.bfloat16)
        mixed_ref[pl.ds(jnp.where(north, 0, half * cols - cells), cells), low:high] = mixed[:cells]

    def mix_pairs(pairs):
        cells = 2 * pairs * cols
        return jnp.dot(product[:cells], mix_ref[...], preferred_element_type=jnp.float32)

    def finish(mixed, base, depth):
        cells = depth * cols
        here = window[pl.ds(base + 1, depth), home : home + cols].reshape(cells, channels)
        latent = here.astype(jnp.float32) + mixed
        mean = jnp.mean(latent, axis=1, keepdims=True)
        centred = latent - mean
        variance = jnp.mean(centred * centred, axis=1, keepdims=True)
        normed = (centred * lax.rsqrt(variance + norm_eps) * gain_ref[...][None, :]).astype(
            jnp.bfloat16
        )
        raised = jnp.dot(normed, up_ref[...], preferred_element_type=jnp.float32)
        hidden = 0.5 * raised * (1.0 + lax.erf(raised * math.sqrt(0.5)))
        lowered = jnp.dot(
            hidden.astype(jnp.bfloat16), down_ref[...], preferred_element_type=jnp.float32
        )
        result = (latent + lowered).astype(jnp.bfloat16)
        out_ref[pl.ds(base, depth)] = result.reshape(depth, cols, channels)

    fold_pair, half_pair, all_pairs = fold // 2, half // 2, rows // 2
    pl.semaphore_wait(barrier, 2 + jnp.where(above, 1, 0) + jnp.where(below, 1, 0))

    @pl.when(inner)
    def _():
        greet(ready.at[0], lon=me + 2)
        greet(ready.at[0], lon=me - 2)

    fetch.wait()
    start(halo_own, *across, fold_own, along_in)
    goes_near = jnp.logical_or(inner, jnp.logical_not(same))

    @pl.when(goes_near)
    def _():
        start(direct)

    @pl.when(inner)
    def _():
        start(along_out)

    select_tables()
    lax.fori_loop(0, bases // 2, build_near, 0)
    pl.semaphore_wait(ready.at[0], 1)

    @pl.when(inner)
    def _():
        greet(ready.at[1], lon=device(2 * inward))

    lax.fori_loop(bases // 2, bases, build_near, 0)
    lax.fori_loop(0, bases // 2, build_polar, 0)

    @pl.when(outer)
    def _():
        pl.semaphore_wait(ready.at[1], 1)

        @pl.when(same)
        def _():
            start(direct)

        start(along_out)

    start(*halves)
    arrived(along_in)
    start(fold_across, *across_late)
    arrived(*across)
    start(*along, halo_across)
    lax.fori_loop(bases // 2, bases, build_polar, 0)
    clear_window()
    arrived(direct)
    start(direct_across)
    for load in loads:
        load.wait()
    arrived(fold_own, fold_across)
    fold_pairs()
    for swap, (low, high) in zip(fold_swap, pieces):
        fold_mix(low, high)
        start(swap)
    arrived(along_out)

    @pl.when(same)
    def _():
        start(late_across[0])

    @pl.when(jnp.logical_not(same))
    def _():
        start(late_across[1])

    arrived(along[0])
    start(halo_along)
    arrived(across_late[1], direct_across, halo_own, halo_across, halo_along, along[1], *halves)
    filter_pairs(half_pair, all_pairs)
    finish(mix_pairs(all_pairs - half_pair), jnp.where(north, half, 0), rows - half)

    @pl.when(same)
    def _():
        arrived(late_across[1])

    @pl.when(jnp.logical_not(same))
    def _():
        arrived(late_across[0])

    arrived(across_late[0])
    filter_pairs(fold_pair, half_pair)
    cells = (half - fold) * cols
    mixed_ref[pl.ds(jnp.where(north, fold * cols, 0), cells)] = mix_pairs(half_pair - fold_pair)
    arrived(*fold_swap)
    own_part = pl.ds(jnp.where(north, 0, half * cols - fold * cols), fold * cols)
    for (low, high), piece in zip(pieces, (fold_in_a, fold_in_b)):
        mixed_ref[own_part, low:high] = mixed_ref[own_part, low:high] + piece[...].astype(jnp.float32)
    finish(mixed_ref[...], jnp.where(north, 0, half), half)

    @pl.when(same)
    def _():
        late_across[0].wait_send()

    @pl.when(jnp.logical_not(same))
    def _():
        late_across[1].wait_send()

    sent = [halo_own, halo_across, halo_along, fold_own, fold_across, along_in, along_out]
    sent += [direct, direct_across] + fold_swap
    for copy in sent + across + across_late + along + halves:
        copy.wait_send()


def relay_call(
    lon_count,
    lat_count,
    fields,
    support_rows,
    support_lons,
    support_weights,
    mix_weight,
    norm_gain,
    up_weight,
    down_weight,
):
    channels, rows, cols = fields.shape
    bases, hidden = mix_weight.shape[0], up_weight.shape[1]
    lon_total = lon_count * cols
    half, copies = rows // 2, 24
    fold = fold_rows(lon_count, lat_count, rows, cols)
    piece = channels // 256 // 2 * 256
    in_vmem = pl.BlockSpec(memory_space=pltpu.VMEM)
    anywhere = pl.BlockSpec(memory_space=pl.ANY)
    result = pl.pallas_call(
        functools.partial(relay_kernel, lon_count, lat_count),
        out_shape=pltpu.VMEM((rows, cols, channels), jnp.bfloat16),
        in_specs=[anywhere] * 8,
        out_specs=in_vmem,
        scratch_shapes=[
            pltpu.VMEM((rows + 2, lon_total, channels), jnp.bfloat16),
            pltpu.VMEM((fold // 2, 4 * bases * cols, 16 * cols), jnp.bfloat16),
            pltpu.VMEM(((half - fold) // 2, 2 * bases * cols, 4 * lon_total), jnp.bfloat16),
            pltpu.VMEM((half // 2, 2 * bases * cols, 16 * cols), jnp.bfloat16),
            pltpu.VMEM((half * cols, bases * channels), jnp.bfloat16),
            pltpu.VMEM((half * cols, channels), jnp.float32),
            pltpu.VMEM((fold * cols, piece), jnp.bfloat16),
            pltpu.VMEM((fold * cols, channels - piece), jnp.bfloat16),
            pltpu.VMEM((fold * cols, piece), jnp.bfloat16),
            pltpu.VMEM((fold * cols, channels - piece), jnp.bfloat16),
            pltpu.VMEM((bases * channels, channels), jnp.bfloat16),
            pltpu.VMEM((channels, hidden), jnp.bfloat16),
            pltpu.VMEM((hidden, channels), jnp.bfloat16),
            pltpu.SemaphoreType.DMA((copies,)),
            pltpu.SemaphoreType.DMA((copies,)),
            pltpu.SemaphoreType.DMA((8,)),
            pltpu.SemaphoreType.REGULAR((2,)),
            pltpu.VMEM((3, bases, rows, support_rows.shape[2]), jnp.float32),
            pltpu.VMEM((bases, support_rows.shape[2], support_rows.shape[1]), jnp.int32),
            pltpu.VMEM((bases, support_rows.shape[2], support_rows.shape[1]), jnp.int32),
            pltpu.VMEM((bases, support_rows.shape[2], support_rows.shape[1]), jnp.float32),
            pltpu.VMEM((channels,), jnp.float32),
        ],
        compiler_params=pltpu.CompilerParams(
            collective_id=0, has_side_effects=True, vmem_limit_bytes=56 * 1024 * 1024,
        ),
    )(
        jnp.transpose(fields, (1, 2, 0)),
        jnp.transpose(support_rows, (0, 2, 1)),
        jnp.transpose(support_lons, (0, 2, 1)),
        jnp.transpose(support_weights, (0, 2, 1)),
        norm_gain,
        mix_weight.reshape(bases * channels, channels),
        up_weight,
        down_weight,
    )
    return jnp.transpose(result, (2, 0, 1))


def direct_call(
    lon_count,
    lat_count,
    fields,
    support_rows,
    support_lons,
    support_weights,
    mix_weight,
    norm_gain,
    up_weight,
    down_weight,
):
    channels, rows, cols = fields.shape
    bases, hidden = mix_weight.shape[0], up_weight.shape[1]
    lon_total = lon_count * cols
    plan = plan_copies(lon_count, lat_count, rows, cols)
    count = sum(len(stage) for stage in plan[1])
    in_vmem = pl.BlockSpec(memory_space=pltpu.VMEM)
    anywhere = pl.BlockSpec(memory_space=pl.ANY)
    result = pl.pallas_call(
        functools.partial(block_kernel, lon_count, lat_count, plan),
        out_shape=jax.ShapeDtypeStruct((rows, cols, channels), jnp.bfloat16),
        in_specs=[anywhere] + [in_vmem] * 4 + [anywhere] * 3,
        out_specs=anywhere,
        scratch_shapes=[
            pltpu.VMEM((rows, cols, channels), jnp.bfloat16),
            pltpu.VMEM((rows, cols, channels), jnp.bfloat16),
            pltpu.VMEM((rows + 2, lon_total, channels), jnp.bfloat16),
            pltpu.VMEM((rows, bases * cols, 3 * lon_total), jnp.bfloat16),
            pltpu.VMEM((rows // 2 * cols, bases * channels), jnp.bfloat16),
            pltpu.VMEM((bases * channels, channels), jnp.bfloat16),
            pltpu.VMEM((channels, hidden), jnp.bfloat16),
            pltpu.VMEM((hidden, channels), jnp.bfloat16),
            pltpu.SemaphoreType.DMA((count,)),
            pltpu.SemaphoreType.DMA((count,)),
            pltpu.SemaphoreType.DMA((4,)),
            pltpu.SemaphoreType.DMA((len(plan[0]),)),
        ],
        compiler_params=pltpu.CompilerParams(
            collective_id=0, has_side_effects=True, vmem_limit_bytes=56 * 1024 * 1024
        ),
    )(
        jnp.transpose(fields, (1, 2, 0)),
        jnp.transpose(support_rows, (0, 2, 1)),
        jnp.transpose(support_lons, (0, 2, 1)),
        jnp.transpose(support_weights, (0, 2, 1)),
        norm_gain,
        mix_weight.reshape(bases * channels, channels),
        up_weight,
        down_weight,
    )
    return jnp.transpose(result, (2, 0, 1))


def on_device(lon_count, lat_count, *arrays):
    channels, rows, cols = arrays[0].shape
    if relay_fits(lon_count, lat_count, rows, cols):
        return relay_call(lon_count, lat_count, *arrays)
    return direct_call(lon_count, lat_count, *arrays)


def solution(mesh):
    in_specs = (P("member", "lat", "lon"), P(), P(), P(), P(), P(), P(), P())
    out_specs = P("member", "lat", "lon")
    return jax.shard_map(
        functools.partial(on_device, mesh.shape["lon"], mesh.shape["lat"]),
        mesh=mesh,
        in_specs=in_specs,
        out_specs=out_specs,
        check_vma=False,
    )
```

```python
import functools
import math

import jax
import jax.numpy as jnp
from jax import lax
from jax.experimental import pallas as pl
from jax.experimental.pallas import tpu as pltpu
from jax.sharding import PartitionSpec as P

norm_eps = 1e-05
MESH = pl.DeviceIdType.MESH


def plan_copies(lon_count, lat_count, rows, cols):
    lon_total, row_total = lon_count * cols, lat_count * rows

    def reach(row):
        nearest = min(row + 1, row_total - row)
        return min(lon_total // 2, 4 * row_total // nearest)

    def distance(row):
        return min(-(-reach(row) // cols), lon_count // 2)

    def in_half(span, delta):
        if delta == 0 or abs(delta) == lon_count // 2:
            return False
        return span - cols * (abs(delta) - 1) <= cols // 2

    need = [distance(max(p - 1, 0)) for p in range(rows)]
    deltas = [d for d in range(1 - lon_count // 2, lon_count // 2 + 1) if d != 0]
    counts = {delta: sum(1 for d in need if d >= abs(delta)) for delta in deltas}
    spans = [reach(max(p - 1, 0)) for p in range(rows)]
    fulls = {d: sum(1 for p in range(counts[d]) if not in_half(spans[p], d)) for d in deltas}
    edge, edge_span = 0, 0
    for boundary in range(1, lat_count):
        edge = max(edge, distance(boundary * rows - 1), distance(boundary * rows))
        edge_span = max(edge_span, reach(boundary * rows - 1), reach(boundary * rows))
    halo = [d for d in range(1 - lon_count // 2, lon_count // 2 + 1) if abs(d) <= edge]
    groups = [(rows // 2, rows), (rows // 4, rows // 2), (0, rows // 4)]
    stages = []
    upper = rows
    for low, _ in groups:
        lower = max(low - 1, 0)
        stage = []
        for delta in sorted(deltas, key=lambda d: -abs(d)):
            full, top = min(fulls[delta], upper), min(counts[delta], upper)
            if full > lower:
                stage.append(("block", delta, lower, full, False))
            if top > max(full, lower):
                stage.append(("block", delta, max(full, lower), top, True))
        stages.append(stage)
        upper = lower
    if lat_count > 1:
        stages[0] = [
            (side, d, 0, 1, in_half(edge_span, d)) for d in halo for side in ("down", "up")
        ] + stages[0]
    halves = [d for d in halo if in_half(edge_span, d)]
    return groups, stages, counts, fulls, halo, halves


def block_kernel(
    lon_count,
    lat_count,
    plan,
    x_hbm,
    rows_ref,
    lons_ref,
    weights_ref,
    gain_ref,
    mix_hbm,
    up_hbm,
    down_hbm,
    out_hbm,
    x_ref,
    out_ref,
    window,
    filters,
    product,
    mix_ref,
    up_ref,
    down_ref,
    send_sem,
    recv_sem,
    load_sem,
    out_sem,
):
    rows, cols, channels = x_ref.shape
    bases, entries = rows_ref.shape[:2]
    lon_total = lon_count * cols
    middle = lon_count // 2
    groups, stages, counts, fulls, halo, halves = plan
    me, lat = lax.axis_index("lon"), lax.axis_index("lat")
    north = 2 * lat < lat_count
    has_low, has_high = lat > 0, lat < lat_count - 1

    loads = [
        pltpu.make_async_copy(mix_hbm, mix_ref, load_sem.at[0]),
        pltpu.make_async_copy(up_hbm, up_ref, load_sem.at[1]),
        pltpu.make_async_copy(down_hbm, down_ref, load_sem.at[2]),
    ]
    fetch = pltpu.make_async_copy(x_hbm, x_ref, load_sem.at[3])
    fetch.start()

    barrier = pltpu.get_barrier_semaphore()
    halo_deltas = halo if lat_count > 1 else []
    for delta in range(1, lon_count):
        pl.semaphore_signal(
            barrier, inc=1, device_id={"lon": lax.rem(me + delta, lon_count)}, device_id_type=MESH
        )
    for present, other in ((has_low, lat - 1), (has_high, lat + 1)):

        @pl.when(present)
        def _():
            for delta in halo_deltas:
                target = lax.rem(me + lon_count - delta, lon_count)
                pl.semaphore_signal(
                    barrier, inc=1, device_id={"lon": target, "lat": other}, device_id_type=MESH
                )

    sides = jnp.where(has_low, 1, 0) + jnp.where(has_high, 1, 0)
    pl.semaphore_wait(barrier, lon_count - 1 + sides * len(halo_deltas))
    fetch.wait()

    def copy_of(index, item):
        kind, delta, first, last, halved = item
        width = cols // 2 if halved else cols
        offset = cols // 2 if halved and delta < 0 else 0
        target = lax.rem(me + lon_count - delta, lon_count)
        slot = (delta + middle) % lon_count
        here, there = pl.ds(offset, width), pl.ds(slot * cols + offset, width)
        if kind == "block":
            start = jnp.where(north, first, rows - last)
            source = x_ref.at[pl.ds(start, last - first), here]
            landing = window.at[pl.ds(start + 1, last - first), there]
            device = {"lon": target}
        elif kind == "down":
            source = x_ref.at[pl.ds(rows - 1, 1), here]
            landing = window.at[pl.ds(0, 1), there]
            device = {"lon": target, "lat": jnp.minimum(lat + 1, lat_count - 1)}
        else:
            source = x_ref.at[pl.ds(0, 1), here]
            landing = window.at[pl.ds(rows + 1, 1), there]
            device = {"lon": target, "lat": jnp.maximum(lat - 1, 0)}
        return pltpu.make_async_remote_copy(
            src_ref=source,
            dst_ref=landing,
            send_sem=send_sem.at[index],
            recv_sem=recv_sem.at[index],
            device_id=device,
            device_id_type=MESH,
        )

    copies = []
    for stage in stages:
        copies.append(list(enumerate(stage, sum(len(done) for done in copies))))

    def each(items, sending, action):
        for index, item in items:
            if item[0] == "block":
                action(copy_of(index, item))
            else:
                present = has_high if (item[0] == "down") == sending else has_low

                @pl.when(present)
                def _():
                    action(copy_of(index, item))

    for stage in copies:
        each(stage, True, lambda copy: copy.start())
    for load in loads:
        load.start()

    window[1 : rows + 1, middle * cols : (middle + 1) * cols, :] = x_ref[...]
    for delta, count in counts.items():
        slot = (delta + middle) % lon_count
        if count < rows:
            gap = (rows - count, cols, channels)
            window[pl.ds(jnp.where(north, count, 0) + 1, rows - count),
                   slot * cols : (slot + 1) * cols] = jnp.zeros(gap, jnp.bfloat16)
        partial = count - fulls[delta]
        if partial > 0:
            far = slot * cols + (0 if delta < 0 else cols // 2)
            window[pl.ds(jnp.where(north, fulls[delta], rows - count) + 1, partial),
                   far : far + cols // 2] = jnp.zeros(
                (partial, cols // 2, channels), jnp.bfloat16
            )
    for delta in halves:
        far = (delta + middle) % lon_count * cols + (0 if delta < 0 else cols // 2)
        for line in (0, rows + 1):
            window[line, far : far + cols // 2] = jnp.zeros((cols // 2, channels), jnp.bfloat16)
    for present, line in ((has_low, 0), (has_high, rows + 1)):
        for delta in range(1 - middle, middle + 1):
            slot = (delta + middle) % lon_count

            def clear():
                window[line, slot * cols : (slot + 1) * cols] = jnp.zeros(
                    (cols, channels), jnp.bfloat16
                )

            if delta in halo and lat_count > 1:
                pl.when(jnp.logical_not(present))(clear)
            else:
                clear()

    lanes = lax.broadcasted_iota(jnp.int32, (rows, lon_total), 1)
    wide = (rows, rows_ref.shape[2])
    own_rows = (
        lax.broadcasted_iota(jnp.int32, wide, 0) + lat * rows
        == lax.broadcasted_iota(jnp.int32, wide, 1)
    ).astype(jnp.float32)

    def own(ref, k):
        return lax.dot_general(
            own_rows,
            ref[k].astype(jnp.float32),
            (((1,), (1,)), ((), ())),
            precision=lax.Precision.HIGHEST,
            preferred_element_type=jnp.float32,
        )

    def build(k, carry):
        spot = own(lons_ref, k).astype(jnp.int32) + middle * cols
        spot = jnp.where(spot >= lon_total, spot - lon_total, spot)
        row_offset = own(rows_ref, k)
        weight = own(weights_ref, k)
        picked = [jnp.where(row_offset == r, weight, 0.0) for r in (-1.0, 0.0, 1.0)]
        sums = [jnp.zeros((rows, lon_total), jnp.float32) for _ in range(3)]
        for s in range(entries):
            hit = spot[:, s : s + 1] == lanes
            for r in range(3):
                sums[r] = sums[r] + jnp.where(hit, picked[r][:, s : s + 1], 0.0)
        for r in range(3):
            for i in range(rows):
                line = jnp.broadcast_to(sums[r][i : i + 1, :], (cols, lon_total))
                turned = pltpu.roll(line, 0, 1, stride=1, stride_axis=0)
                filters[i, pl.ds(pl.multiple_of(k * cols, cols), cols),
                        r * lon_total : (r + 1) * lon_total] = turned.astype(jnp.bfloat16)
        return carry

    lax.fori_loop(0, bases, build, 0)

    def group(low, high):
        start = jnp.where(north, low, rows - high)
        half = high - low
        lines = half * cols
        def filter_row(t, carry):
            i = start + t
            source = window[pl.ds(i, 3)].reshape(3 * lon_total, channels)
            filtered = jnp.dot(filters[i], source, preferred_element_type=jnp.float32)
            filtered = filtered.astype(jnp.bfloat16)
            at = pl.multiple_of(t * cols, cols)
            for k in range(bases):
                product[pl.ds(at, cols), k * channels : (k + 1) * channels] = filtered[
                    k * cols : (k + 1) * cols
                ]
            return carry

        lax.fori_loop(0, half, filter_row, 0)
        mixed = jnp.dot(product[:lines], mix_ref[...], preferred_element_type=jnp.float32)
        here = x_ref[pl.ds(start, half)].reshape(lines, channels)
        latent = here.astype(jnp.float32) + mixed
        mean = jnp.mean(latent, axis=1, keepdims=True)
        centred = latent - mean
        variance = jnp.mean(centred * centred, axis=1, keepdims=True)
        normed = (centred * lax.rsqrt(variance + norm_eps) * gain_ref[...][None, :]).astype(jnp.bfloat16)
        raised = jnp.dot(normed, up_ref[...], preferred_element_type=jnp.float32)
        hidden = 0.5 * raised * (1.0 + lax.erf(raised * math.sqrt(0.5)))
        lowered = jnp.dot(
            hidden.astype(jnp.bfloat16), down_ref[...], preferred_element_type=jnp.float32
        )
        result = (latent + lowered).astype(jnp.bfloat16)
        out_ref[pl.ds(start, half)] = result.reshape(half, cols, channels)

    puts = []
    for stage, (low, high) in zip(copies, groups):
        each(stage, False, lambda copy: copy.wait_recv())
        if stage is copies[0]:
            for load in loads:
                load.wait()
        group(low, high)
        part = pl.ds(jnp.where(north, low, rows - high), high - low)
        put = pltpu.make_async_copy(out_ref.at[part], out_hbm.at[part], out_sem.at[len(puts)])
        put.start()
        puts.append(put)
    for stage in copies:
        each(stage, True, lambda copy: copy.wait_send())
    for put in puts:
        put.wait()


def source_reach(lon_total, row_total, p):
    row = max(p - 1, 0)
    return min(lon_total // 2, 4 * row_total // min(row + 1, row_total - row))


def fold_rows(lon_count, lat_count, rows, cols):
    lon_total, row_total = lon_count * cols, lat_count * rows
    fold = 2
    while source_reach(lon_total, row_total, fold + 1) > 2 * cols:
        fold += 2
    return fold


def relay_fits(lon_count, lat_count, rows, cols):
    lon_total, row_total = lon_count * cols, lat_count * rows
    if lon_count != 8 or lat_count != 2 or rows % 4 != 0 or cols != 16:
        return False
    near = source_reach(lon_total, row_total, rows // 2 + 1) <= cols
    return near and fold_rows(lon_count, lat_count, rows, cols) <= rows // 4


def relay_kernel(
    lon_count,
    lat_count,
    x_hbm,
    rows_hbm,
    lons_hbm,
    weights_hbm,
    gain_hbm,
    mix_hbm,
    up_hbm,
    down_hbm,
    out_ref,
    window,
    fold_filters,
    wide_filters,
    near_filters,
    product,
    mixed_ref,
    fold_out_a,
    fold_out_b,
    fold_in_a,
    fold_in_b,
    mix_ref,
    up_ref,
    down_ref,
    send_sem,
    recv_sem,
    load_sem,
    ready,
    tables,
    rows_ref,
    lons_ref,
    weights_ref,
    gain_ref,
):
    rows, cols, channels = x_hbm.shape
    bases, entries = rows_ref.shape[:2]
    lon_total, row_total = lon_count * cols, lat_count * rows
    middle, part, half = lon_count // 2, cols // 2, rows // 2
    home = middle * cols
    fold = fold_rows(lon_count, lat_count, rows, cols)
    reaches = [source_reach(lon_total, row_total, max(p, fold + 1)) for p in range(rows)]
    wide = sum(1 for r in reaches if r > cols + part)
    near = sum(1 for r in reaches if r > cols)
    me, lat = lax.axis_index("lon"), lax.axis_index("lat")
    north = lat == 0
    turn = 1 - 2 * lax.rem(me, 2)
    place = lax.rem(me, middle)
    inward = jnp.where(place < 2, 1, -1)
    edge = jnp.where(north, rows - 1, 0)

    def device(delta):
        return lax.rem(me + delta + lon_count, lon_count)

    def at(delta):
        return pl.multiple_of(lax.rem(delta + middle + lon_count, lon_count) * cols, cols)

    def lines(first, last):
        return pl.ds(jnp.where(north, first, rows - last) + 1, last - first)

    fetch = pltpu.make_async_copy(
        x_hbm, window.at[pl.ds(1, rows), pl.ds(home, cols)], load_sem.at[3]
    )
    loads = [
        pltpu.make_async_copy(mix_hbm, mix_ref, load_sem.at[0]),
        pltpu.make_async_copy(up_hbm, up_ref, load_sem.at[1]),
        pltpu.make_async_copy(down_hbm, down_ref, load_sem.at[2]),
    ]
    supports = [
        pltpu.make_async_copy(source, landing, load_sem.at[4 + n])
        for n, (source, landing) in enumerate(
            [(rows_hbm, rows_ref), (lons_hbm, lons_ref), (weights_hbm, weights_ref)]
        )
    ]
    loads.append(pltpu.make_async_copy(gain_hbm, gain_ref, load_sem.at[7]))
    barrier = pltpu.get_barrier_semaphore()
    above, below = me < lon_count - 2, me >= 2
    inner = jnp.logical_and(above, below)
    outer = jnp.logical_not(inner)

    def greet(semaphore, **other):
        pl.semaphore_signal(semaphore, inc=1, device_id=other, device_id_type=MESH)

    greet(barrier, lon=me + turn)
    greet(barrier, lat=1 - lat)

    @pl.when(above)
    def _():
        greet(barrier, lon=me + 2)

    @pl.when(below)
    def _():
        greet(barrier, lon=me - 2)

    for load in [fetch] + supports + loads:
        load.start()

    def clear(where, low, high):
        size = where.size if isinstance(where, pl.Slice) else 1
        window[where, low:high] = jnp.zeros((size, high - low, channels), jnp.bfloat16)

    near_cut, last = half + (rows - half) // 2 - 1, rows - 1
    sky, halo = jnp.where(north, 0, rows + 1), jnp.where(north, rows + 1, 0)
    def clear_window():
        clear(pl.ds(sky, 1), 0, lon_total)
        clear(lines(fold + 1, wide), 0, home - 2 * cols)
        clear(lines(fold + 1, wide), home + 3 * cols, lon_total)
        clear(lines(fold - 1, fold + 1), 0, cols)

        @pl.when(place != middle - 1)
        def _():
            clear(lines(fold - 1, fold + 1), cols, 2 * cols)

        @pl.when(place != 0)
        def _():
            clear(lines(fold - 1, fold + 1), home + 3 * cols, lon_total)

        clear(lines(wide, near), 0, home - cols - part)
        clear(lines(wide, near), home + 2 * cols + part, lon_total)
        clear(lines(near, half + 1), 0, home - cols)
        clear(lines(near, half + 1), home + 2 * cols, lon_total)
        clear(lines(half + 1, near_cut), home + 2 * cols, home + 3 * cols)
        clear(lines(last, rows), home + 2 * cols, home + 3 * cols)

        @pl.when(turn < 0)
        def _():
            clear(lines(near_cut, last), home + 2 * cols, home + 3 * cols)

        clear(pl.ds(halo, 1), home - cols, home - part)
        clear(pl.ds(halo, 1), home + cols + part, home + 3 * cols)

    def select_tables():
        for support in supports:
            support.wait()
        span = (rows, rows_ref.shape[2])
        order = lax.broadcasted_iota(jnp.int32, span, 0)
        local = jnp.where(north, order, rows - 2 - order + 2 * lax.rem(order, 2))
        mine = (local + lat * rows == lax.broadcasted_iota(jnp.int32, span, 1)).astype(jnp.float32)
        for which, ref in enumerate((rows_ref, lons_ref, weights_ref)):
            own = lax.dot_general(
                mine,
                ref[...].astype(jnp.float32).reshape(bases * entries, rows_ref.shape[2]),
                (((1,), (1,)), ((), ())),
                precision=lax.Precision.HIGHEST,
                preferred_element_type=jnp.float32,
            )
            for k in range(bases):
                tables[which, k] = own[:, k * entries : (k + 1) * entries]

    count = [0]

    def message(where, here, there, width, target, landing=None):
        index = count[0]
        count[0] += 1
        landing = where if landing is None else landing
        return pltpu.make_async_remote_copy(
            src_ref=window.at[where, pl.ds(here, width)],
            dst_ref=window.at[landing, pl.ds(there, width)],
            send_sem=send_sem.at[index],
            recv_sem=recv_sem.at[index],
            device_id=target,
            device_id_type=MESH,
        )

    partner, beside = {"lon": me + turn}, {"lon": device(2 * turn)}
    core, core_line = {"lat": 1 - lat}, pl.ds(edge + 1, 1)
    core_landing = pl.ds(jnp.where(north, 0, rows + 1), 1)

    def own_across(first, last):
        return message(lines(first, last), home, at(-turn), cols, partner)

    def own_along(first, last, e):
        return message(lines(first, last), home, at(-2 * e), cols, {"lon": device(2 * e)})

    def half_along(first, last, e):
        offset = part if e > 0 else 0
        return message(
            lines(first, last), home + offset, at(-2 * e) + offset, part, {"lon": device(2 * e)}
        )

    def pass_along(first, last):
        return message(lines(first, last), at(turn), at(-turn), cols, beside)

    def pass_across(first, last, e):
        return message(lines(first, last), at(2 * e), at(2 * e - turn), cols, partner)

    def to_core(col, width):
        return message(core_line, col, col, width, core, core_landing)

    after = pl.multiple_of(home + jnp.where(turn > 0, cols, -part), part)
    before = pl.multiple_of(home + jnp.where(turn > 0, -part, cols), part)
    halo_own = to_core(home, cols)
    halo_across, halo_along = to_core(after, part), to_core(before, part)
    across = [own_across(last, rows), own_across(wide, near_cut)]
    across_late = [own_across(fold + 1, wide), own_across(near_cut, last)]
    along = [pass_along(last, rows), pass_along(wide, near_cut)]
    direct = own_along(near_cut, last, -turn)
    direct_across = pass_across(near_cut, last, turn)
    halves = [half_along(wide, near, e) for e in (1, -1)]
    fold_own = own_across(0, fold + 1)
    along_in, along_out = own_along(0, wide, inward), own_along(fold - 1, wide, -inward)
    fold_across = pass_across(0, fold + 1, inward)
    same = turn == inward
    late_across = pass_across(fold + 1, wide, turn), pass_across(fold - 1, wide, turn)
    pieces = channels // 256 // 2 * 256
    pieces = [(0, pieces), (pieces, channels)]
    fold_swap = [
        pltpu.make_async_remote_copy(
            src_ref=(fold_out_a, fold_out_b)[n],
            dst_ref=(fold_in_a, fold_in_b)[n],
            send_sem=send_sem.at[count[0] + n],
            recv_sem=recv_sem.at[count[0] + n],
            device_id={"lon": device(middle)},
            device_id_type=MESH,
        )
        for n, (low, high) in enumerate(pieces)
    ]

    def start(*copies):
        for copy in copies:
            copy.start()

    def arrived(*copies):
        for copy in copies:
            copy.wait_recv()

    lanes = lax.broadcasted_iota(jnp.int32, (half, lon_total), 1)
    second = lax.rem(lax.broadcasted_iota(jnp.int32, (half, entries), 0), 2)

    def turned(line, shift):
        spread = jnp.broadcast_to(line, (cols, lon_total))
        return pltpu.roll(spread, shift, 1, stride=1, stride_axis=0)

    def build_near(k, carry):
        offset = tables[1, k, half:].astype(jnp.int32)
        row_offset = tables[0, k, half:].astype(jnp.int32)
        weight = tables[2, k, half:]
        spot = (row_offset + 1 + second) * (4 * cols) + offset + cols
        sums = [jnp.zeros((half, lon_total), jnp.float32) for _ in range(2)]
        for s in range(entries):
            for v in range(2):
                hit = spot[:, s : s + 1] == lanes + v * lon_total
                sums[v] = sums[v] + jnp.where(hit, weight[:, s : s + 1], 0.0)
        for n in range(half):
            for v in range(2):
                spot_at = pl.multiple_of(k * 2 * cols + (n % 2) * cols, cols)
                near_filters[n // 2, pl.ds(spot_at, cols), v * lon_total : (v + 1) * lon_total] = (
                    turned(sums[v][n : n + 1, :], 0).astype(jnp.bfloat16)
                )
        return carry

    polar = lax.broadcasted_iota(jnp.int32, (half, entries), 0) < fold
    start_col = jnp.where(polar, place * cols, home)
    lower = lax.broadcasted_iota(jnp.int32, (cols, lon_total), 1) < home

    def build_polar(k, carry):
        spot = tables[1, k, :half].astype(jnp.int32) + start_col
        spot = jnp.where(spot >= lon_total, spot - lon_total, spot)
        spot = jnp.where(spot < 0, spot + lon_total, spot)
        row_offset = tables[0, k, :half]
        weight = tables[2, k, :half]
        picked = [jnp.where(row_offset == r, weight, 0.0) for r in (-1.0, 0.0, 1.0)]
        sums = [jnp.zeros((half, lon_total), jnp.float32) for _ in range(3)]
        for s in range(entries):
            hit = spot[:, s : s + 1] == lanes
            for r in range(3):
                sums[r] = sums[r] + jnp.where(hit, picked[r][:, s : s + 1], 0.0)
        none = jnp.zeros((cols, lon_total), jnp.float32)
        for n in range(fold):
            late = n % 2
            kept = [none] * 4
            moved = [none] * 4
            for r in range(3):
                kept[r + late] = turned(sums[r][n : n + 1, :], 0)
                moved[r + late] = turned(sums[r][n : n + 1, :], home)
            for v in range(2):
                here = jnp.where(lower, kept[2 * v], moved[2 * v + 1])
                there = jnp.where(lower, moved[2 * v], kept[2 * v + 1])
                for who, value in enumerate((here, there)):
                    spot_at = pl.multiple_of(k * 4 * cols + (2 * who + late) * cols, cols)
                    fold_filters[
                        n // 2, pl.ds(spot_at, cols), v * lon_total : (v + 1) * lon_total
                    ] = value.astype(jnp.bfloat16)
        for n in range(fold, half):
            late = n % 2
            spot_at = pl.ds(pl.multiple_of(k * 2 * cols + late * cols, cols), cols)
            for r in range(3):
                low = (r + late) * lon_total
                wide_filters[(n - fold) // 2, spot_at, low : low + lon_total] = turned(
                    sums[r][n : n + 1, :], 0
                ).astype(jnp.bfloat16)
            low = (3 - 3 * late) * lon_total
            wide_filters[(n - fold) // 2, spot_at, low : low + lon_total] = none.astype(jnp.bfloat16)
        return carry

    def filter_pairs(first, last):
        pairs = last - first
        base = jnp.where(north, 2 * first, rows - 2 * last)
        for t in range(pairs):
            q = jnp.where(north, first + t, last - 1 - t)
            taken = pl.ds(base + 2 * t, 4)
            if 2 * first >= half:
                low = home - cols
                source = window[taken, low : low + 4 * cols].reshape(16 * cols, channels)
                matrix = near_filters[q - half // 2]
            else:
                source = window[taken].reshape(4 * lon_total, channels)
                matrix = wide_filters[q - fold // 2]
            filtered = jnp.dot(matrix, source, preferred_element_type=jnp.float32)
            filtered = filtered.astype(jnp.bfloat16)
            for k in range(bases):
                product[2 * t * cols : 2 * (t + 1) * cols, k * channels : (k + 1) * channels] = (
                    filtered[2 * k * cols : 2 * (k + 1) * cols]
                )

    def fold_pairs():
        pairs = fold // 2
        cells = fold * cols
        base = jnp.where(north, 0, rows - fold)
        for t in range(pairs):
            q = jnp.where(north, t, pairs - 1 - t)
            source = window[pl.ds(base + 2 * t, 4), pl.ds(at(-place), 4 * cols)]
            source = source.reshape(16 * cols, channels)
            filtered = jnp.dot(fold_filters[q], source, preferred_element_type=jnp.float32)
            filtered = filtered.astype(jnp.bfloat16)
            for k in range(bases):
                for who in range(2):
                    low, from_row = who * cells + 2 * t * cols, (4 * k + 2 * who) * cols
                    product[low : low + 2 * cols, k * channels : (k + 1) * channels] = filtered[
                        from_row : from_row + 2 * cols
                    ]

    def fold_mix(low, high):
        cells = fold * cols
        mixed = jnp.dot(
            product[: 2 * cells], mix_ref[:, low:high], preferred_element_type=jnp.float32
        )
        (fold_out_a if low == 0 else fold_out_b)[...] = mixed[cells:].astype(jnp.bfloat16)
        mixed_ref[pl.ds(jnp.where(north, 0, half * cols - cells), cells), low:high] = mixed[:cells]

    def mix_pairs(pairs):
        cells = 2 * pairs * cols
        return jnp.dot(product[:cells], mix_ref[...], preferred_element_type=jnp.float32)

    def finish(mixed, base, depth):
        cells = depth * cols
        here = window[pl.ds(base + 1, depth), home : home + cols].reshape(cells, channels)
        latent = here.astype(jnp.float32) + mixed
        mean = jnp.mean(latent, axis=1, keepdims=True)
        centred = latent - mean
        variance = jnp.mean(centred * centred, axis=1, keepdims=True)
        normed = (centred * lax.rsqrt(variance + norm_eps) * gain_ref[...][None, :]).astype(
            jnp.bfloat16
        )
        raised = jnp.dot(normed, up_ref[...], preferred_element_type=jnp.float32)
        hidden = 0.5 * raised * (1.0 + lax.erf(raised * math.sqrt(0.5)))
        lowered = jnp.dot(
            hidden.astype(jnp.bfloat16), down_ref[...], preferred_element_type=jnp.float32
        )
        result = (latent + lowered).astype(jnp.bfloat16)
        out_ref[pl.ds(base, depth)] = result.reshape(depth, cols, channels)

    fold_pair, half_pair, all_pairs = fold // 2, half // 2, rows // 2
    pl.semaphore_wait(barrier, 2 + jnp.where(above, 1, 0) + jnp.where(below, 1, 0))

    @pl.when(inner)
    def _():
        greet(ready.at[0], lon=me + 2)
        greet(ready.at[0], lon=me - 2)

    fetch.wait()
    start(halo_own, *across, fold_own, along_in)
    goes_near = jnp.logical_or(inner, jnp.logical_not(same))

    @pl.when(goes_near)
    def _():
        start(direct)

    @pl.when(inner)
    def _():
        start(along_out)

    select_tables()
    lax.fori_loop(0, bases // 2, build_near, 0)
    pl.semaphore_wait(ready.at[0], 1)

    @pl.when(inner)
    def _():
        greet(ready.at[1], lon=device(2 * inward))

    lax.fori_loop(bases // 2, bases, build_near, 0)
    lax.fori_loop(0, bases // 2, build_polar, 0)

    @pl.when(outer)
    def _():
        pl.semaphore_wait(ready.at[1], 1)

        @pl.when(same)
        def _():
            start(direct)

        start(along_out)

    start(*halves)
    arrived(along_in)
    start(fold_across, *across_late)
    arrived(*across)
    start(*along, halo_across)
    lax.fori_loop(bases // 2, bases, build_polar, 0)
    clear_window()
    arrived(direct)
    start(direct_across)
    arrived(along_out)

    @pl.when(same)
    def _():
        start(late_across[0])

    @pl.when(jnp.logical_not(same))
    def _():
        start(late_across[1])

    for load in loads:
        load.wait()
    arrived(fold_own, fold_across)
    fold_pairs()
    for swap, (low, high) in zip(fold_swap, pieces):
        fold_mix(low, high)
        start(swap)
    arrived(along[0])
    start(halo_along)
    arrived(across_late[1], direct_across, halo_own, halo_across, halo_along, along[1], *halves)
    filter_pairs(half_pair, all_pairs)
    finish(mix_pairs(all_pairs - half_pair), jnp.where(north, half, 0), rows - half)

    @pl.when(same)
    def _():
        arrived(late_across[1])

    @pl.when(jnp.logical_not(same))
    def _():
        arrived(late_across[0])

    arrived(across_late[0])
    filter_pairs(fold_pair, half_pair)
    cells = (half - fold) * cols
    mixed_ref[pl.ds(jnp.where(north, fold * cols, 0), cells)] = mix_pairs(half_pair - fold_pair)
    arrived(*fold_swap)
    own_part = pl.ds(jnp.where(north, 0, half * cols - fold * cols), fold * cols)
    for (low, high), piece in zip(pieces, (fold_in_a, fold_in_b)):
        mixed_ref[own_part, low:high] = mixed_ref[own_part, low:high] + piece[...].astype(jnp.float32)
    finish(mixed_ref[...], jnp.where(north, 0, half), half)

    @pl.when(same)
    def _():
        late_across[0].wait_send()

    @pl.when(jnp.logical_not(same))
    def _():
        late_across[1].wait_send()

    sent = [halo_own, halo_across, halo_along, fold_own, fold_across, along_in, along_out]
    sent += [direct, direct_across] + fold_swap
    for copy in sent + across + across_late + along + halves:
        copy.wait_send()


def relay_call(
    lon_count,
    lat_count,
    fields,
    support_rows,
    support_lons,
    support_weights,
    mix_weight,
    norm_gain,
    up_weight,
    down_weight,
):
    channels, rows, cols = fields.shape
    bases, hidden = mix_weight.shape[0], up_weight.shape[1]
    lon_total = lon_count * cols
    half, copies = rows // 2, 24
    fold = fold_rows(lon_count, lat_count, rows, cols)
    piece = channels // 256 // 2 * 256
    in_vmem = pl.BlockSpec(memory_space=pltpu.VMEM)
    anywhere = pl.BlockSpec(memory_space=pl.ANY)
    result = pl.pallas_call(
        functools.partial(relay_kernel, lon_count, lat_count),
        out_shape=pltpu.VMEM((rows, cols, channels), jnp.bfloat16),
        in_specs=[anywhere] * 8,
        out_specs=in_vmem,
        scratch_shapes=[
            pltpu.VMEM((rows + 2, lon_total, channels), jnp.bfloat16),
            pltpu.VMEM((fold // 2, 4 * bases * cols, 16 * cols), jnp.bfloat16),
            pltpu.VMEM(((half - fold) // 2, 2 * bases * cols, 4 * lon_total), jnp.bfloat16),
            pltpu.VMEM((half // 2, 2 * bases * cols, 16 * cols), jnp.bfloat16),
            pltpu.VMEM((half * cols, bases * channels), jnp.bfloat16),
            pltpu.VMEM((half * cols, channels), jnp.float32),
            pltpu.VMEM((fold * cols, piece), jnp.bfloat16),
            pltpu.VMEM((fold * cols, channels - piece), jnp.bfloat16),
            pltpu.VMEM((fold * cols, piece), jnp.bfloat16),
            pltpu.VMEM((fold * cols, channels - piece), jnp.bfloat16),
            pltpu.VMEM((bases * channels, channels), jnp.bfloat16),
            pltpu.VMEM((channels, hidden), jnp.bfloat16),
            pltpu.VMEM((hidden, channels), jnp.bfloat16),
            pltpu.SemaphoreType.DMA((copies,)),
            pltpu.SemaphoreType.DMA((copies,)),
            pltpu.SemaphoreType.DMA((8,)),
            pltpu.SemaphoreType.REGULAR((2,)),
            pltpu.VMEM((3, bases, rows, support_rows.shape[2]), jnp.float32),
            pltpu.VMEM((bases, support_rows.shape[2], support_rows.shape[1]), jnp.int32),
            pltpu.VMEM((bases, support_rows.shape[2], support_rows.shape[1]), jnp.int32),
            pltpu.VMEM((bases, support_rows.shape[2], support_rows.shape[1]), jnp.float32),
            pltpu.VMEM((channels,), jnp.float32),
        ],
        compiler_params=pltpu.CompilerParams(
            collective_id=0, has_side_effects=True, vmem_limit_bytes=56 * 1024 * 1024,
        ),
    )(
        jnp.transpose(fields, (1, 2, 0)),
        jnp.transpose(support_rows, (0, 2, 1)),
        jnp.transpose(support_lons, (0, 2, 1)),
        jnp.transpose(support_weights, (0, 2, 1)),
        norm_gain,
        mix_weight.reshape(bases * channels, channels),
        up_weight,
        down_weight,
    )
    return jnp.transpose(result, (2, 0, 1))


def direct_call(
    lon_count,
    lat_count,
    fields,
    support_rows,
    support_lons,
    support_weights,
    mix_weight,
    norm_gain,
    up_weight,
    down_weight,
):
    channels, rows, cols = fields.shape
    bases, hidden = mix_weight.shape[0], up_weight.shape[1]
    lon_total = lon_count * cols
    plan = plan_copies(lon_count, lat_count, rows, cols)
    count = sum(len(stage) for stage in plan[1])
    in_vmem = pl.BlockSpec(memory_space=pltpu.VMEM)
    anywhere = pl.BlockSpec(memory_space=pl.ANY)
    result = pl.pallas_call(
        functools.partial(block_kernel, lon_count, lat_count, plan),
        out_shape=jax.ShapeDtypeStruct((rows, cols, channels), jnp.bfloat16),
        in_specs=[anywhere] + [in_vmem] * 4 + [anywhere] * 3,
        out_specs=anywhere,
        scratch_shapes=[
            pltpu.VMEM((rows, cols, channels), jnp.bfloat16),
            pltpu.VMEM((rows, cols, channels), jnp.bfloat16),
            pltpu.VMEM((rows + 2, lon_total, channels), jnp.bfloat16),
            pltpu.VMEM((rows, bases * cols, 3 * lon_total), jnp.bfloat16),
            pltpu.VMEM((rows // 2 * cols, bases * channels), jnp.bfloat16),
            pltpu.VMEM((bases * channels, channels), jnp.bfloat16),
            pltpu.VMEM((channels, hidden), jnp.bfloat16),
            pltpu.VMEM((hidden, channels), jnp.bfloat16),
            pltpu.SemaphoreType.DMA((count,)),
            pltpu.SemaphoreType.DMA((count,)),
            pltpu.SemaphoreType.DMA((4,)),
            pltpu.SemaphoreType.DMA((len(plan[0]),)),
        ],
        compiler_params=pltpu.CompilerParams(
            collective_id=0, has_side_effects=True, vmem_limit_bytes=56 * 1024 * 1024
        ),
    )(
        jnp.transpose(fields, (1, 2, 0)),
        jnp.transpose(support_rows, (0, 2, 1)),
        jnp.transpose(support_lons, (0, 2, 1)),
        jnp.transpose(support_weights, (0, 2, 1)),
        norm_gain,
        mix_weight.reshape(bases * channels, channels),
        up_weight,
        down_weight,
    )
    return jnp.transpose(result, (2, 0, 1))


def on_device(lon_count, lat_count, *arrays):
    channels, rows, cols = arrays[0].shape
    if relay_fits(lon_count, lat_count, rows, cols):
        return relay_call(lon_count, lat_count, *arrays)
    return direct_call(lon_count, lat_count, *arrays)


def solution(mesh):
    in_specs = (P("member", "lat", "lon"), P(), P(), P(), P(), P(), P(), P())
    out_specs = P("member", "lat", "lon")
    return jax.shard_map(
        functools.partial(on_device, mesh.shape["lon"], mesh.shape["lat"]),
        mesh=mesh,
        in_specs=in_specs,
        out_specs=out_specs,
        check_vma=False,
    )
```
